256 devices in a mesh: patch: 32 (over y, z), req: 4 (over x), owner: 2 (over core).
Axes of the slice: x: 4, y: 4, z: 8, core: 2. Of those that a mesh axis runs over, the one named last changes fastest.
Arguments:
- latents: bfloat16 [8, 256, 256, 320], P('req', 'patch', 'owner'), may hold values from -24 to 24
- timestep_embedding: bfloat16 [8, 1280], P('req'), may hold values from -6 to 6
- embedding_weight: bfloat16 [1280, 320], replicated, may hold values from -0.15625 to 0.15625
- group_norm_gain: float32 [2, 320], replicated, may hold values from 0.25 to 1.75
- group_norm_shift: float32 [2, 320], replicated, may hold values from -3 to 3
- kernel_weight: bfloat16 [2, 9, 320, 320], replicated, may hold values from -0.109375 to 0.109375
- plugin_reduce_library: bfloat16 [8, 2, 184320], P(('req', 'owner'), None, 'patch'), may hold values from -0.109375 to 0.109375
- plugin_expand_library: bfloat16 [8, 2, 20480], P(('req', 'owner'), None, 'patch'), may hold values from -0.75 to 0.75
- image_adapter: int32 [8, 1], P('req'), may hold values from 0 to 7
- adapter_bank_row: int32 [8], replicated, may hold values from 0 to 7, each once
Outputs:
- result: bfloat16 [8, 256, 256, 320], P('req', 'patch', 'owner')
The draws below stay inside these ranges and needn't reach their ends.
Inputs may be any that keep to these rules, and one draw needn't show every extreme that they name: `image_adapter`: each image names one adapter; every adapter is named by some image. A permutation: adapter a is stored in bank row adapter_bank_row[a].
All inputs are finite; a program needn't handle non-finite values.
Results may differ from the reference program's by a relative error of at most 0.0055.
Values may be sent and summed in bfloat16 or wider, within the bound.
A program may use at most 128 MiB of HBM per device.

```python
import math
import jax
import jax.numpy as jnp
from jax import lax

NUM_FEATURES = 320
GROUPS = 32
EMBED = 1280
INNER_DIMENSION = 64
LATENT_TALL = 256
LATENT_BROAD = 256
NUM_PICTURES = 8
NUM_PLUGINS = 8


def draw_latents(key, part):
    key_base, key_chan = jax.random.split(key, 2)
    rows = jnp.arange(LATENT_TALL, dtype=jnp.float32) / max(LATENT_TALL - 1, 1)
    columns = jnp.arange(LATENT_BROAD, dtype=jnp.float32) / max(LATENT_BROAD - 1, 1)
    channel = jnp.exp(jax.random.uniform(key_chan, (NUM_FEATURES,), jnp.float32, math.log(0.3), math.log(3.0)))
    scale = (3.0 ** rows)[:, None, None] * (2.0 ** columns)[None, :, None] * channel[None, None, :] / 3.0
    shape = (NUM_PICTURES, LATENT_TALL, LATENT_BROAD, NUM_FEATURES)
    base = jnp.clip(jax.random.normal(key_base, shape, jnp.float32), -4.0, 4.0)
    values = base * scale[None]
    return values.astype(jnp.bfloat16)


def steps_of(key, extent, cuts, smallest, largest):
    loudness = 1.0
    for dim, parts in cuts:
        heights = jax.random.uniform(jax.random.fold_in(jax.random.fold_in(key, 6), dim), (parts,), jnp.float32, smallest / len(cuts), largest / len(cuts))
        loudness = loudness * jnp.repeat(jnp.exp(heights), extent[dim] // parts).reshape((-1,) + (1,) * (len(extent) - 1 - dim))
    return loudness


def different_ones(own_key, rows, number_of, top, lift):
    ranking = jax.random.permutation(jax.random.fold_in(own_key, 1), number_of)
    boost = ranking
    for power in range(3):
        boost = boost * boost // number_of
    boost = boost * lift // number_of
    lots = jax.random.randint(jax.random.fold_in(own_key, 2), (rows, number_of), 0, 4096) + boost
    sure = jax.random.permutation(jax.random.fold_in(own_key, 3), rows)[jnp.arange(number_of) % rows]
    lots = jnp.where(jnp.arange(rows)[:, None] == sure[None, :], 1 << 14, lots)
    merit = lots * number_of + jnp.arange(number_of)
    return lax.top_k(merit.astype(jnp.int32), top)[1].astype(jnp.int32)


def noise(key, extent, deviation, reach, shards=(), kind=jnp.bfloat16):
    entries = deviation * jax.random.normal(key, extent, jnp.float32)
    if shards:
        entries = entries * steps_of(key, extent, shards, -0.22, 0.18)
    return jnp.clip(entries, -reach, reach).astype(kind)


def setup_inputs(seed: int = 0) -> dict:
    arg_keys = jax.random.split(jax.random.key(seed), 11)
    return {
        "latents": draw_latents(jax.random.fold_in(arg_keys[10], 71), 0),
        "timestep_embedding": noise(arg_keys[1], (NUM_PICTURES, EMBED), 1.0, 6.0, ((0, 4),)),
        "embedding_weight": noise(arg_keys[2], (EMBED, NUM_FEATURES), EMBED ** -0.5, 0.15625),
        "group_norm_gain": jnp.clip(1.0 + 0.15 * jax.random.normal(arg_keys[3], (2, NUM_FEATURES), jnp.float32), 0.25, 1.75),
        "group_norm_shift": noise(arg_keys[4], (2, NUM_FEATURES), 0.5, 3.0, (), jnp.float32),
        "kernel_weight": noise(arg_keys[5], (2, 9, NUM_FEATURES, NUM_FEATURES), (9 * NUM_FEATURES) ** -0.5, 0.109375),
        "plugin_reduce_library": noise(arg_keys[6], (NUM_PLUGINS, 2, 9 * NUM_FEATURES * INNER_DIMENSION), (9 * NUM_FEATURES) ** -0.5, 0.109375, ((0, 8), (2, 32))),
        "plugin_expand_library": noise(arg_keys[7], (NUM_PLUGINS, 2, INNER_DIMENSION * NUM_FEATURES), INNER_DIMENSION ** -0.5, 0.75, ((0, 8), (2, 32))),
        "image_adapter": different_ones(arg_keys[8], NUM_PICTURES, NUM_PLUGINS, 1, 2048),
        "adapter_bank_row": jax.random.permutation(arg_keys[9], NUM_PLUGINS).astype(jnp.int32),
    }


def group_act(values, gain, shift):
    grouped = values.reshape(LATENT_TALL, LATENT_BROAD, GROUPS, NUM_FEATURES // GROUPS)
    mean = lax.optimization_barrier(jnp.mean(grouped, axis=(0, 1, 3), keepdims=True))
    var = lax.optimization_barrier(jnp.mean(jnp.square(grouped - mean), axis=(0, 1, 3), keepdims=True))
    normed = ((grouped - mean) / jnp.sqrt(var + 1e-05)).reshape(LATENT_TALL, LATENT_BROAD, NUM_FEATURES)
    return jax.nn.silu(normed * gain + shift).astype(jnp.bfloat16)

def convolve(act, kernel):
    cin = kernel.shape[1]
    cout = kernel.shape[2]
    return lax.conv_general_dilated(act.astype(jnp.float32)[None], kernel.astype(jnp.float32).reshape(3, 3, cin, cout), (1, 1), 'SAME', dimension_numbers=('NHWC', 'HWIO', 'NHWC'))[0]

def one_image(inputs, group_norm_gain, group_norm_shift, kernel_weight):
    image, proj, reducing_filter, expanding_linear_map = inputs
    act1 = group_act(image.astype(jnp.float32), group_norm_gain[0], group_norm_shift[0])
    narrow_first = convolve(act1, reducing_filter[0]).astype(jnp.bfloat16)
    correction_first = jnp.dot(narrow_first.reshape(-1, INNER_DIMENSION), expanding_linear_map[0], preferred_element_type=jnp.float32).reshape(LATENT_TALL, LATENT_BROAD, NUM_FEATURES)
    hidden1 = (convolve(act1, kernel_weight[0]) + correction_first + proj[None, None, :]).astype(jnp.bfloat16)
    act2 = group_act(hidden1.astype(jnp.float32), group_norm_gain[1], group_norm_shift[1])
    narrow_second = convolve(act2, reducing_filter[1]).astype(jnp.bfloat16)
    correction_second = jnp.dot(narrow_second.reshape(-1, INNER_DIMENSION), expanding_linear_map[1], preferred_element_type=jnp.float32).reshape(LATENT_TALL, LATENT_BROAD, NUM_FEATURES)
    return (image.astype(jnp.float32) + convolve(act2, kernel_weight[1]) + correction_second).astype(jnp.bfloat16)

def reference(latents, timestep_embedding, embedding_weight, group_norm_gain, group_norm_shift, kernel_weight, plugin_reduce_library, plugin_expand_library, image_adapter, adapter_bank_row):
    library_entry = adapter_bank_row[image_adapter[:, 0]]
    reducing_filter = plugin_reduce_library[library_entry].reshape(NUM_PICTURES, 2, 9, NUM_FEATURES, INNER_DIMENSION)
    expanding_linear_map = plugin_expand_library[library_entry].reshape(NUM_PICTURES, 2, INNER_DIMENSION, NUM_FEATURES)
    temb = jax.nn.silu(timestep_embedding.astype(jnp.float32)).astype(jnp.bfloat16)
    proj = jnp.dot(temb, embedding_weight, preferred_element_type=jnp.float32)
    return lax.map(lambda inputs: one_image(inputs, group_norm_gain, group_norm_shift, kernel_weight), (latents, proj, reducing_filter, expanding_linear_map))
```

```python
import functools

import jax
import jax.numpy as jnp
from jax import lax
from jax.experimental import pallas as pl
from jax.experimental.pallas import tpu as pltpu
from jax.sharding import PartitionSpec as P

MESH = pl.DeviceIdType.MESH
F32, BF16 = jnp.float32, jnp.bfloat16
Y, Z = 4, 8
RANK = 64
EDGE = 16
GROUP = 10


def remote(src, dst, send, recv, device):
    return pltpu.make_async_remote_copy(
        src_ref=src, dst_ref=dst, send_sem=send, recv_sem=recv, device_id=device, device_id_type=MESH
    )


def place():
    patch, req, owner = lax.axis_index("patch"), lax.axis_index("req"), lax.axis_index("owner")
    return patch, req, owner, patch // Z, patch % Z


def greet(bank):
    patch, req, owner, y, z = place()
    sem = pltpu.get_barrier_semaphore()
    count = 0

    def signal(device):
        pl.semaphore_signal(sem, inc=1, device_id=device, device_id_type=MESH)

    for k in range(1, 2 * Y):
        g = (y * 2 + owner + k) % (2 * Y)
        signal(((g // 2) * Z + z, req, g % 2))
        count += 1
    for k in range(1, Z):
        signal((y * Z + (z + k) % Z, req, owner))
        count += 1
    for step in (1, Y * Z - 1):
        for other in (owner, 1 - owner):
            signal(((patch + step) % (Y * Z), req, other))
            count += 1
    if bank:
        for k in range(1, 8):
            g = (req * 2 + owner + k) % 8
            signal((patch, g // 2, g % 2))
            count += 1
    pl.semaphore_wait(sem, count)


def start_borders(src, top, bot, col, send, recv):
    patch, req, owner, y, z = place()
    rows = src.shape[1]
    last = Y * Z - 1
    edge = pl.multiple_of((1 - owner) * (src.shape[2] - EDGE), EDGE)
    cols = pl.ds(edge, EDGE)
    down = (patch + 1, req, owner)
    up = (patch - 1, req, owner)
    copies = [
        (patch < last, patch > 0, remote(src.at[:, rows - 1], top, send.at[0], recv.at[0], down)),
        (patch > 0, patch < last, remote(src.at[:, 0], bot, send.at[1], recv.at[1], up)),
        (
            patch < last,
            patch > 0,
            remote(src.at[:, rows - 1, cols], col.at[:, 0], send.at[2], recv.at[2], (patch + 1, req, 1 - owner)),
        ),
        (
            patch > 0,
            patch < last,
            remote(src.at[:, 0, cols], col.at[:, rows + 1], send.at[3], recv.at[3], (patch - 1, req, 1 - owner)),
        ),
        (
            None,
            None,
            remote(src.at[:, :, cols], col.at[:, pl.ds(1, rows)], send.at[4], recv.at[4], (patch, req, 1 - owner)),
        ),
    ]
    for sends, _, copy in copies:
        if sends is None:
            copy.start()
        else:
            pl.when(sends)(copy.start)

    @pl.when(patch == 0)
    def _():
        top[...] = jnp.zeros_like(top)
        col[:, 0] = jnp.zeros_like(col[:, 0])

    @pl.when(patch == last)
    def _():
        bot[...] = jnp.zeros_like(bot)
        col[:, rows + 1] = jnp.zeros_like(col[:, rows + 1])

    return copies


def wait_borders(copies):
    for sends, receives, copy in copies:
        if sends is None:
            copy.wait_send()
            copy.wait_recv()
        else:
            pl.when(sends)(copy.wait_send)
            pl.when(receives)(copy.wait_recv)


def local_stats(rows_of, rows):
    def add(f):
        def step(r, total):
            x = f(rows_of(r).astype(F32))
            return total + jnp.sum(x.reshape(x.shape[0] // 8, 8, x.shape[1]), axis=0)

        return step

    chans = rows_of(0).shape[1]
    count = rows * rows_of(0).shape[0]
    zero = jnp.zeros((8, chans), F32)
    total = lax.fori_loop(0, rows, add(lambda x: x), zero)
    mean = jnp.sum(total, axis=0, keepdims=True) * (1.0 / count)
    spread = lax.fori_loop(0, rows, add(lambda x: (x - mean) * (x - mean)), zero)
    return mean, jnp.sum(spread, axis=0, keepdims=True)


def start_exchange(slots, send, recv, peers):
    copies = [
        remote(slots.at[0], slots.at[k], send.at[k], recv.at[k], peer) for k, peer in enumerate(peers, 1)
    ]
    for copy in copies:
        copy.start()
    return copies


def combine(slots, count):
    values = slots[...]
    total = jnp.sum(values, axis=0)
    mean = total * (1.0 / values.shape[0])
    off = values - mean[None]
    between = jnp.sum(off * off, axis=0)
    return mean[0:2], total[2:4] + count * between[0:2]


def first_peers():
    patch, req, owner, y, z = place()
    peers = []
    for k in range(1, 2 * Y):
        g = (y * 2 + owner + k) % (2 * Y)
        peers.append(((g // 2) * Z + z, req, g % 2))
    return peers


def second_peers():
    patch, req, owner, y, z = place()
    return [(y * Z + (z + k) % Z, req, owner) for k in range(1, Z)]


def group_mean(values, groups):
    high = values.astype(BF16)
    rest = values - high.astype(F32)
    middle = rest.astype(BF16)
    low = (rest - middle.astype(F32)).astype(BF16)
    total = (
        jnp.dot(high, groups, preferred_element_type=F32)
        + jnp.dot(middle, groups, preferred_element_type=F32)
        + jnp.dot(low, groups, preferred_element_type=F32)
    )
    return total * (1.0 / GROUP)


def finish_norm(mean, spread, count, gain, shift):
    chans = mean.shape[1]
    row = lax.broadcasted_iota(jnp.int32, (chans, chans), 0)
    column = lax.broadcasted_iota(jnp.int32, (chans, chans), 1)
    groups = jnp.where((row * 6554) >> 16 == (column * 6554) >> 16, 1.0, 0.0).astype(BF16)
    both = jnp.concatenate([mean, mean, mean, mean], axis=0)
    center = group_mean(both, groups)[0:2]
    off = mean - center
    local = spread * (1.0 / count) + off * off
    var = group_mean(jnp.concatenate([local, local, local, local], axis=0), groups)[0:2]
    scale = gain / jnp.sqrt(var + 1e-05)
    return center, 0.5 * scale, 0.5 * shift


def gather_bank(piece, image_adapter, bank_row, held, lora, send, recv):
    patch, req, owner, y, z = place()
    me = req * 2 + owner
    held[me] = piece[...]
    copies = []
    for k in range(1, 8):
        g = (me + k) % 8
        copy = remote(held.at[me], held.at[me], send.at[k], recv.at[k], (patch, g // 2, g % 2))
        copy.start()
        copies.append(copy)
    for copy in copies:
        copy.wait()
    slot = bank_row[image_adapter[owner, 0]]
    lora[owner, z, y] = held[slot]
    copies = []
    for k in range(1, Y):
        block = lora.at[owner, z, y]
        copy = remote(block, block, send.at[7 + k], recv.at[7 + k], (((y + k) % Y) * Z + z, req, owner))
        copy.start()
        copies.append(copy)
    for copy in copies:
        copy.wait()
    right = (y * Z + (z + 1) % Z, req, owner)
    left = (y * Z + (z + Z - 1) % Z, req, owner)
    sibling = (patch, req, 1 - owner)
    relays = []

    def relay(block, at):
        copy = remote(lora.at[owner, block], lora.at[owner, block], send.at[at], recv.at[at], sibling)
        copy.start()
        relays.append(copy)

    relay(z, 20)
    half = Y // 2
    for step in range(Z // 2):
        forward = (z + Z - step) % Z
        backward = (z + step) % Z
        a, b = lora.at[owner, forward], lora.at[owner, backward]
        if step == Z // 2 - 1:
            a, b = lora.at[owner, forward, pl.ds(0, half)], lora.at[owner, backward, pl.ds(half, half)]
        at = 11 + 2 * step
        first = remote(a, a, send.at[at], recv.at[at], right)
        second = remote(b, b, send.at[at + 1], recv.at[at + 1], left)
        first.start()
        second.start()
        first.wait()
        second.wait()
        if step < Z // 2 - 1:
            relay((z + Z - step - 1) % Z, 21 + 2 * step)
            relay((z + step + 1) % Z, 22 + 2 * step)
        else:
            relay((z + Z // 2) % Z, 21 + 2 * step)
    for copy in relays:
        copy.wait()


def first_kernel(
    source, piece, image_adapter, bank_row, embedding, weight, gain, shift,
    top, bot, col, norm, lora,
    own, held, one, two, local_sem, edge_send, edge_recv, one_send, one_recv, two_send, two_recv, bank_send, bank_recv,
):
    fetch = pltpu.make_async_copy(source, own, local_sem)
    fetch.start()
    greet(True)
    borders = start_borders(source, top, bot, col, edge_send, edge_recv)
    fetch.wait()
    rows = own.shape[1]
    count = rows * own.shape[2]
    for image in range(2):
        mean, spread = local_stats(lambda r: own[image, r], rows)
        one[0, pl.ds(image, 1)] = mean
        one[0, pl.ds(2 + image, 1)] = spread
    one[0, pl.ds(4, 4)] = jnp.zeros((4, own.shape[3]), F32)
    copies = start_exchange(one, one_send, one_recv, first_peers())
    u = embedding[...].astype(F32)
    temb = (u / (1.0 + jnp.exp(-u))).astype(BF16)
    norm[pl.ds(5, 2)] = jnp.dot(temb, weight[...], preferred_element_type=F32)
    norm[pl.ds(7, 1)] = jnp.zeros((1, own.shape[3]), F32)
    for copy in copies:
        copy.wait()
    mean, spread = combine(one, float(count))
    two[0, pl.ds(0, 2)] = mean
    two[0, pl.ds(2, 2)] = spread
    two[0, pl.ds(4, 4)] = jnp.zeros((4, own.shape[3]), F32)
    copies = start_exchange(two, two_send, two_recv, second_peers())
    for copy in copies:
        copy.wait()
    mean, spread = combine(two, float(count * 2 * Y))
    center, scale, offset = finish_norm(
        mean, spread, float(count * 2 * Y * Z), gain[pl.ds(0, 1)], shift[pl.ds(0, 1)]
    )
    norm[pl.ds(0, 2)] = center
    norm[pl.ds(2, 2)] = scale
    norm[pl.ds(4, 1)] = offset
    gather_bank(piece, image_adapter, bank_row, held, lora, bank_send, bank_recv)
    wait_borders(borders)


def second_kernel(
    source, stats, gain, shift,
    top, bot, col, norm,
    one, two, edge_send, edge_recv, one_send, one_recv, two_send, two_recv,
):
    greet(False)
    borders = start_borders(source, top, bot, col, edge_send, edge_recv)
    count = source.shape[1] * source.shape[2]
    one[0] = stats[...]
    copies = start_exchange(one, one_send, one_recv, first_peers())
    norm[pl.ds(5, 3)] = jnp.zeros((3, stats.shape[1]), F32)
    for copy in copies:
        copy.wait()
    mean, spread = combine(one, float(count))
    two[0, pl.ds(0, 2)] = mean
    two[0, pl.ds(2, 2)] = spread
    two[0, pl.ds(4, 4)] = jnp.zeros((4, stats.shape[1]), F32)
    copies = start_exchange(two, two_send, two_recv, second_peers())
    for copy in copies:
        copy.wait()
    mean, spread = combine(two, float(count * 2 * Y))
    center, scale, offset = finish_norm(
        mean, spread, float(count * 2 * Y * Z), gain[pl.ds(1, 1)], shift[pl.ds(1, 1)]
    )
    norm[pl.ds(0, 2)] = center
    norm[pl.ds(2, 2)] = scale
    norm[pl.ds(4, 1)] = offset
    wait_borders(borders)


def conv_kernel(which, source, top, bot, col, norm, kernel, lora, *rest):
    if which == 0:
        out, stats, wide, tail, flat, expand, total, rem = rest
    else:
        latents, out, wide, tail, flat, expand, total, rem = rest
    patch, req, owner, y, z = place()
    rows, columns, chans = source.shape[1:]
    pieces = Y * Z
    piece_rows = 9 * chans // pieces
    up_at = -(-piece_rows // 16) * 16
    main = 256
    lane = lax.broadcasted_iota(jnp.int32, (3 * chans, 128), 1)
    index = lax.broadcasted_iota(jnp.int32, (columns, 1), 0)
    across = lax.broadcasted_iota(jnp.int32, (rows + 2, 1), 0)
    beyond = ((patch > 0) | (across > 0)) & ((patch < pieces - 1) | (across < rows + 1))

    def per_image(image, carry):
        for p in range(pieces):
            flat[pl.ds(p * piece_rows, piece_rows)] = lora[image, p % Z, p // Z, pl.ds(0, piece_rows)].astype(F32)
        for row_off in range(3):
            down = flat[pl.ds(row_off * 3 * chans, 3 * chans)]
            if which == 1:
                down = pltpu.roll(down, 64, 1)
            base = kernel[row_off, :, pl.ds(main, chans - main)].astype(F32)
            base = jnp.concatenate([base, jnp.zeros_like(base)], axis=1)
            tail[row_off] = jnp.where(lane >= 64, down, base).astype(BF16)
        ups = jnp.concatenate(
            [lora[image, p % Z, p // Z, pl.ds(up_at, 16)] for p in range(pieces)], axis=0
        )
        q = lax.broadcasted_iota(jnp.int32, (128, pieces * 16), 0) - 64
        s = lax.broadcasted_iota(jnp.int32, (128, pieces * 16), 1)
        for b in range(3):
            hit = (q >= 0) & (s == (q >> 1) * 16 + 4 * b + 2 * which + (q & 1))
            pick = jnp.where(hit, 1.0, 0.0).astype(BF16)
            expand[:, pl.ds(b * 128, 128)] = jnp.dot(pick, ups, preferred_element_type=F32).astype(BF16)

        center = norm[pl.ds(image, 1)]
        scale = norm[pl.ds(2 + image, 1)]
        offset = norm[pl.ds(4, 1)]

        def activate(x):
            h = (x.astype(F32) - center) * scale + offset
            return h + h * jnp.tanh(h)

        border = jnp.where(owner == 0, col[image, :, 0, :].astype(F32), col[image, :, EDGE - 1, :].astype(F32))
        rem[pl.ds(0, rows + 2)] = jnp.where(beyond, activate(border), 0.0)

        def widen(r, act):
            edge = rem[pl.ds(r, 1)]
            left = jnp.where(index == 0, jnp.where(owner == 1, edge, 0.0), pltpu.roll(act, 1, 0))
            right = jnp.where(
                index == columns - 1, jnp.where(owner == 0, edge, 0.0), pltpu.roll(act, columns - 1, 0)
            )
            wide[r] = jnp.concatenate([left, act, right], axis=1).astype(BF16)

        widen(0, jnp.where(patch > 0, activate(top[image]), 0.0))
        widen(rows + 1, jnp.where(patch < pieces - 1, activate(bot[image]), 0.0))

        def row(r, carry):
            widen(r + 1, activate(source[image, r]))
            return carry

        lax.fori_loop(0, rows, row, 0)

        part = rows // 2
        size = part * columns

        def chunk(c, carry):
            at = c * part
            window = [wide[pl.ds(at + d, part)].reshape(size, 3 * chans) for d in range(3)]
            last = sum(jnp.dot(window[d], tail[d], preferred_element_type=F32) for d in range(3))
            low = jnp.dot(last.astype(BF16), expand[...], preferred_element_type=F32)
            body = sum(
                jnp.dot(window[d], kernel[d, :, pl.ds(0, main)], preferred_element_type=F32) for d in range(3)
            )
            total[:, pl.ds(0, main)] = body + low[:, 0:main]
            total[:, pl.ds(main, 128)] = last + low[:, main:]
            for r in range(part):
                value = total[pl.ds(r * columns, columns), pl.ds(0, chans)]
                if which == 0:
                    value = value + norm[pl.ds(5 + image, 1)]
                else:
                    value = value + latents[image, at + r].astype(F32)
                out[image, at + r] = value.astype(BF16)
            return carry

        lax.fori_loop(0, 2, chunk, 0)
        if which == 0:
            mean, spread = local_stats(lambda r: out[image, r], rows)
            stats[pl.ds(image, 1)] = mean
            stats[pl.ds(2 + image, 1)] = spread
        return carry

    lax.fori_loop(0, 2, per_image, 0)
    if which == 0:
        stats[pl.ds(4, 4)] = jnp.zeros((4, chans), F32)


VM = pl.BlockSpec(memory_space=pltpu.VMEM)
HB = pl.BlockSpec(memory_space=pl.ANY)
SM = pl.BlockSpec(memory_space=pltpu.SMEM)
DMA = pltpu.SemaphoreType.DMA


def border_shapes(images, rows, columns, chans):
    line = jax.ShapeDtypeStruct((images, columns, chans), BF16)
    return [
        line,
        line,
        jax.ShapeDtypeStruct((images, rows + 2, EDGE, chans), BF16),
        jax.ShapeDtypeStruct((8, chans), F32),
    ]


def local(
    latents, timestep_embedding, embedding_weight, gain, shift, kernel_weight, reduce_library, expand_library,
    image_adapter, adapter_bank_row,
):
    images, rows, columns, chans = latents.shape
    pieces = Y * Z
    piece_rows = 9 * chans // pieces
    up_at = -(-piece_rows // 16) * 16
    down = reduce_library[0].reshape(2, piece_rows, RANK)
    down = jnp.concatenate([down[1], down[0]], axis=1)
    up = jnp.pad(expand_library[0].reshape(4, chans), ((0, 0), (0, 64))).reshape(4, 3, 128)
    up = jnp.swapaxes(up, 0, 1).reshape(12, 128)
    piece = jnp.concatenate(
        [jnp.pad(down, ((0, up_at - piece_rows), (0, 0))), jnp.pad(up, ((0, 4), (0, 0)))], axis=0
    )
    deep = up_at + 16
    exchange = [
        pltpu.VMEM((2 * Y, 8, chans), F32),
        pltpu.VMEM((Z, 8, chans), F32),
    ]
    exchange_sems = [DMA((5,)), DMA((5,)), DMA((2 * Y,)), DMA((2 * Y,)), DMA((Z,)), DMA((Z,))]
    top, bot, col, norm, lora = pl.pallas_call(
        first_kernel,
        out_shape=border_shapes(images, rows, columns, chans)
        + [jax.ShapeDtypeStruct((2, Z, Y, deep, 128), BF16)],
        in_specs=[HB, VM, SM, SM, VM, VM, VM, VM],
        out_specs=[VM] * 5,
        scratch_shapes=[
            pltpu.VMEM((images, rows, columns, chans), BF16),
            pltpu.VMEM((8, deep, 128), BF16),
            *exchange,
            DMA,
            *exchange_sems,
            DMA((32,)),
            DMA((32,)),
        ],
        compiler_params=pltpu.CompilerParams(
            collective_id=0, has_side_effects=True, vmem_limit_bytes=24 * 2**20
        ),
        name="exchange_latents",
    )(latents, piece, image_adapter, adapter_bank_row, timestep_embedding, embedding_weight, gain, shift)

    weights = kernel_weight.reshape(2, 3, 3 * chans, chans)

    def conv(which, source, top, bot, col, norm, extra):
        out_shape = [jax.ShapeDtypeStruct((images, rows, columns, chans), BF16)]
        if which == 0:
            out_shape.append(jax.ShapeDtypeStruct((8, chans), F32))
        return pl.pallas_call(
            functools.partial(conv_kernel, which),
            out_shape=out_shape,
            grid=(1,),
            in_specs=[VM] * 5
            + [pl.BlockSpec((None, 3, 3 * chans, chans), lambda i: (which, 0, 0, 0))]
            + [VM] * (1 + len(extra)),
            out_specs=[VM] * len(out_shape),
            scratch_shapes=[
                pltpu.VMEM((rows + 2, columns, 3 * chans), BF16),
                pltpu.VMEM((3, 3 * chans, 128), BF16),
                pltpu.VMEM((9 * chans, 128), F32),
                pltpu.VMEM((128, 384), BF16),
                pltpu.VMEM((rows // 2 * columns, 384), F32),
                pltpu.VMEM((16, chans), F32),
            ],
            compiler_params=pltpu.CompilerParams(vmem_limit_bytes=50 * 2**20),
            name="conv",
        )(source, top, bot, col, norm, weights, lora, *extra)

    hidden, stats = conv(0, latents, top, bot, col, norm, ())
    top, bot, col, norm = pl.pallas_call(
        second_kernel,
        out_shape=border_shapes(images, rows, columns, chans),
        in_specs=[HB, VM, VM, VM],
        out_specs=[VM] * 4,
        scratch_shapes=[*exchange, *exchange_sems],
        compiler_params=pltpu.CompilerParams(
            collective_id=1, has_side_effects=True, vmem_limit_bytes=24 * 2**20
        ),
        name="exchange_hidden",
    )(hidden, stats, gain, shift)
    (result,) = conv(1, hidden, top, bot, col, norm, (latents,))
    return result


def solution(mesh):
    in_specs = (
        P("req", "patch", "owner", None),
        P("req", None),
        P(),
        P(),
        P(),
        P(),
        P(("req", "owner"), None, "patch"),
        P(("req", "owner"), None, "patch"),
        P("req", None),
        P(),
    )
    return jax.shard_map(
        local, mesh=mesh, in_specs=in_specs, out_specs=P("req", "patch", "owner", None), check_vma=False
    )
```

```python
import jax
import jax.numpy as jnp
from jax import lax
from jax.experimental import pallas as pl
from jax.experimental.pallas import tpu as pltpu
from jax.sharding import PartitionSpec as P

MESH = pl.DeviceIdType.MESH
F32, BF16 = jnp.float32, jnp.bfloat16
Y, Z = 4, 8
RANK = 64
EDGE = 16
GROUP = 10


def remote(src, dst, send, recv, device):
    return pltpu.make_async_remote_copy(
        src_ref=src, dst_ref=dst, send_sem=send, recv_sem=recv, device_id=device, device_id_type=MESH
    )


def place():
    patch, req, owner = lax.axis_index("patch"), lax.axis_index("req"), lax.axis_index("owner")
    return patch, req, owner, patch // Z, patch % Z


def greet():
    patch, req, owner, y, z = place()
    sem = pltpu.get_barrier_semaphore()
    count = 0

    def signal(device):
        pl.semaphore_signal(sem, inc=1, device_id=device, device_id_type=MESH)

    for k in range(1, Y * Z):
        signal(((patch + k) % (Y * Z), req, owner))
        count += 1
    for k in range(1, 2 * Y, 2):
        g = (y * 2 + owner + k) % (2 * Y)
        signal(((g // 2) * Z + z, req, g % 2))
        count += 1
    for step in (1, Y * Z - 1):
        signal(((patch + step) % (Y * Z), req, 1 - owner))
        count += 1
    for k in range(1, 8):
        g = (req * 2 + owner + k) % 8
        signal((patch, g // 2, g % 2))
        count += 1
    return lambda: pl.semaphore_wait(sem, count)


def start_borders(src, top, bot, col, image, send, recv):
    patch, req, owner, y, z = place()
    rows = src.shape[1]
    last = Y * Z - 1
    edge = pl.multiple_of((1 - owner) * (src.shape[2] - EDGE), EDGE)
    cols = pl.ds(edge, EDGE)

    def copy(at, block, target, device):
        return remote(block, target, send.at[image, at], recv.at[image, at], device)

    down, up = patch < last, patch > 0
    copies = [
        (down, up, copy(0, src.at[image, rows - 1], top.at[image], (patch + 1, req, owner))),
        (up, down, copy(1, src.at[image, 0], bot.at[image], (patch - 1, req, owner))),
        (down, up, copy(2, src.at[image, rows - 1, cols], col.at[image, 0], (patch + 1, req, 1 - owner))),
        (up, down, copy(3, src.at[image, 0, cols], col.at[image, rows + 1], (patch - 1, req, 1 - owner))),
        (None, None, copy(4, src.at[image, :, cols], col.at[image, pl.ds(1, rows)], (patch, req, 1 - owner))),
    ]
    for sends, _, item in copies:
        if sends is None:
            item.start()
        else:
            pl.when(sends)(item.start)
    return copies


def clear_borders(top, bot, col):
    patch = lax.axis_index("patch")
    end = col.shape[1] - 1

    @pl.when(patch == 0)
    def _():
        top[...] = jnp.zeros_like(top)
        col[:, 0] = jnp.zeros_like(col[:, 0])

    @pl.when(patch == Y * Z - 1)
    def _():
        bot[...] = jnp.zeros_like(bot)
        col[:, end] = jnp.zeros_like(col[:, end])


def wait_borders(copies):
    for sends, receives, copy in copies:
        if sends is None:
            copy.wait_send()
            copy.wait_recv()
        else:
            pl.when(sends)(copy.wait_send)
            pl.when(receives)(copy.wait_recv)


def local_stats(rows_of, rows):
    def add(f):
        def step(r, total):
            x = f(rows_of(r).astype(F32))
            return total + jnp.sum(x.reshape(x.shape[0] // 8, 8, x.shape[1]), axis=0)

        return step

    chans = rows_of(0).shape[1]
    count = rows * rows_of(0).shape[0]
    zero = jnp.zeros((8, chans), F32)
    total = lax.fori_loop(0, rows, add(lambda x: x), zero)
    mean = jnp.sum(total, axis=0, keepdims=True) * (1.0 / count)
    spread = lax.fori_loop(0, rows, add(lambda x: (x - mean) * (x - mean)), zero)
    return mean, jnp.sum(spread, axis=0, keepdims=True)


def start_exchange(slots, send, recv, peers):
    copies = [
        remote(slots.at[0], slots.at[k], send.at[k], recv.at[k], peer) for k, peer in enumerate(peers, 1)
    ]
    for copy in copies:
        copy.start()
    return copies


def combine(slots, count):
    values = slots[...]
    total = jnp.sum(values, axis=0)
    mean = total * (1.0 / values.shape[0])
    off = values - mean[None]
    between = jnp.sum(off * off, axis=0)
    return mean[0:2], total[2:4] + count * between[0:2]


def first_peers():
    patch, req, owner, y, z = place()
    peers = []
    for k in range(1, 2 * Y):
        g = (y * 2 + owner + k) % (2 * Y)
        peers.append(((g // 2) * Z + z, req, g % 2))
    return peers


def second_peers():
    patch, req, owner, y, z = place()
    return [(y * Z + (z + k) % Z, req, owner) for k in range(1, Z)]


def group_mean(values, groups):
    high = values.astype(BF16)
    rest = values - high.astype(F32)
    middle = rest.astype(BF16)
    low = (rest - middle.astype(F32)).astype(BF16)
    total = (
        jnp.dot(high, groups, preferred_element_type=F32)
        + jnp.dot(middle, groups, preferred_element_type=F32)
        + jnp.dot(low, groups, preferred_element_type=F32)
    )
    return total * (1.0 / GROUP)


def finish_norm(mean, spread, count, gain, shift):
    chans = mean.shape[1]
    row = lax.broadcasted_iota(jnp.int32, (chans, chans), 0)
    column = lax.broadcasted_iota(jnp.int32, (chans, chans), 1)
    groups = jnp.where((row * 6554) >> 16 == (column * 6554) >> 16, 1.0, 0.0).astype(BF16)
    both = jnp.concatenate([mean, mean, mean, mean], axis=0)
    center = group_mean(both, groups)[0:2]
    off = mean - center
    local = spread * (1.0 / count) + off * off
    var = group_mean(jnp.concatenate([local, local, local, local], axis=0), groups)[0:2]
    scale = gain / jnp.sqrt(var + 1e-05)
    return center, 0.5 * scale, 0.5 * shift


def lay_piece(reduce_row, expand_row, piece):
    down = reduce_row[0].astype(F32)
    up = expand_row[0].astype(F32)
    piece[...] = jnp.zeros_like(piece)
    for i in range(down.shape[1] // 128):
        piece[:, i, :] = down[:, i * 128 : i * 128 + 128]
    for i in range(up.shape[1] // 128):
        piece[:, UP_AT + i, :] = up[:, i * 128 : i * 128 + 128]
    return piece[...].astype(BF16)


def send_pieces(lora, send, recv):
    patch, req, owner, y, z = place()
    copies = []
    for k in range(1, Y * Z):
        block = lora.at[owner, patch]
        copy = remote(block, block, send.at[k], recv.at[k], ((patch + k) % (Y * Z), req, owner))
        copy.start()
        copies.append(copy)
    return copies


def lay_adapter(lora, image, base, tail, expand, flat, ups, wide_up):
    pieces = Y * Z
    depth = tail.shape[1] * 3 // pieces
    half = depth // 2

    def lay(p, carry):
        value = lora[image, p].astype(F32)
        down = value[0:half]
        flat[pl.ds(p * depth, half, 2)] = pltpu.roll(down, 64, 1)
        flat[pl.ds(p * depth + 1, half, 2)] = down
        ups[pl.ds(pl.multiple_of(p * 8, 8), 8)] = value[UP_AT : UP_AT + 8]
        return carry

    lax.fori_loop(0, pieces, lay, 0)
    lane = lax.broadcasted_iota(jnp.int32, base.shape[1:], 1)
    for d in range(3):
        down = flat[pl.ds(d * base.shape[1], base.shape[1])]
        tail[d] = jnp.where(lane >= 64, down, base[d].astype(F32)).astype(BF16)
    line = [ups[pl.ds(k, pieces, 8)] for k in range(5)]
    turned = [pltpu.roll(v, 64, 1) for v in line]
    low = lax.broadcasted_iota(jnp.int32, line[0].shape, 1) < 64
    even = line[0:3]
    odd = [jnp.where(low, turned[2], turned[3]), jnp.where(low, turned[3], turned[4]), turned[4]]
    for b in range(3):
        wide_up[pl.ds(0, 64)] = jnp.zeros((64, 128), F32)
        wide_up[pl.ds(64, pieces, 2)] = even[b]
        wide_up[pl.ds(65, pieces, 2)] = odd[b]
        expand[:, pl.ds(b * 128, 128)] = wide_up[...].astype(BF16)


def widen_image(source, top, bot, col, norm, image, wide, rem):
    patch, req, owner, y, z = place()
    rows, columns = source.shape[1:3]
    last = Y * Z - 1
    index = lax.broadcasted_iota(jnp.int32, (columns, 1), 0)
    across = lax.broadcasted_iota(jnp.int32, (rows + 2, 1), 0)
    beyond = ((patch > 0) | (across > 0)) & ((patch < last) | (across < rows + 1))
    center = norm[pl.ds(image, 1)]
    scale = norm[pl.ds(2 + image, 1)]
    offset = norm[pl.ds(4, 1)]

    def activate(x):
        h = (x.astype(F32) - center) * scale + offset
        return h + h * jnp.tanh(h)

    border = jnp.where(owner == 0, col[image, :, 0, :].astype(F32), col[image, :, EDGE - 1, :].astype(F32))
    rem[pl.ds(0, rows + 2)] = jnp.where(beyond, activate(border), 0.0)

    def lay(r, act):
        edge = rem[pl.ds(r, 1)]
        left = jnp.where(index == 0, jnp.where(owner == 1, edge, 0.0), pltpu.roll(act, 1, 0))
        right = jnp.where(
            index == columns - 1, jnp.where(owner == 0, edge, 0.0), pltpu.roll(act, columns - 1, 0)
        )
        wide[image, r] = jnp.concatenate([left, act, right], axis=1).astype(BF16)

    lay(0, jnp.where(patch > 0, activate(top[image]), 0.0))
    lay(rows + 1, jnp.where(patch < last, activate(bot[image]), 0.0))

    def row(r, carry):
        lay(r + 1, activate(source[image, r]))
        return carry

    lax.fori_loop(0, rows, row, 0)


def windows(wide, image, at, part):
    columns, depth = wide.shape[2:]
    return [wide[image, pl.ds(at + d, part)].reshape(part * columns, depth) for d in range(3)]


def dots(window, matrix, lanes):
    return sum(jnp.dot(window[d], matrix[d, :, lanes], preferred_element_type=F32) for d in range(3))


MAIN, REST = pl.ds(0, 256), pl.ds(256, 128)
UP_AT = 48


def block_kernel(
    raw, reduce_row, expand_row, image_adapter, bank_row, embedding, weight, gain, shift, kernels_hbm,
    out,
    raw_own, own, hidden, kernels, wide, total, base, tail, expand, flat, ups, wide_up, rem,
    piece, held, lora, top, bot, col, top2, bot2, col2, norm, one, two, one2, two2,
    local_sem, bank_send, bank_recv, lora_send, lora_recv, relay_send, relay_recv,
    edge_send, edge_recv, edge2_send, edge2_recv, x_send, x_recv,
):
    patch, req, owner, y, z = place()
    images, rows, columns, chans = own.shape
    count = rows * columns
    fetch = pltpu.make_async_copy(raw, raw_own, local_sem.at[0])
    fetch.start()
    fetch_kernels = pltpu.make_async_copy(kernels_hbm, kernels, local_sem.at[1])
    fetch_kernels.start()
    arrived = greet()
    me = req * 2 + owner
    held[me] = lay_piece(reduce_row, expand_row, piece)
    clear_borders(top, bot, col)
    clear_borders(top2, bot2, col2)
    for block in (one, two, one2, two2):
        block[0, pl.ds(4, 4)] = jnp.zeros((4, chans), F32)
    fetch.wait()

    def turn(t, carry):
        image, r = t // rows, t % rows
        own[image, r] = jnp.transpose(raw_own[image, r].astype(F32)).astype(BF16)
        return carry

    lax.fori_loop(0, images * rows, turn, 0)

    def stats(source, image, target):
        mean, spread = local_stats(lambda r: source[image, r], rows)
        target[0, pl.ds(image, 1)] = mean
        target[0, pl.ds(2 + image, 1)] = spread

    for image in range(images):
        stats(own, image, one)
    arrived()

    first = start_exchange(one, x_send.at[0], x_recv.at[0], first_peers())
    bank = []
    for k in range(1, 8):
        g = (me + k) % 8
        copy = remote(held.at[me], held.at[me], bank_send.at[k], bank_recv.at[k], (patch, g // 2, g % 2))
        copy.start()
        bank.append(copy)
    borders = [start_borders(own, top, bot, col, i, edge_send, edge_recv) for i in range(images)]

    u = embedding[...].astype(F32)
    temb = (u / (1.0 + jnp.exp(-u))).astype(BF16)
    proj = lax.dot_general(temb, weight[...], (((1,), (1,)), ((), ())), preferred_element_type=F32)
    norm[0, pl.ds(5, 2)] = proj
    fetch_kernels.wait()

    def middle(first, one, two, send, recv):
        for copy in first:
            copy.wait()
        mean, spread = combine(one, float(count))
        two[0, pl.ds(0, 2)] = mean
        two[0, pl.ds(2, 2)] = spread
        return start_exchange(two, send, recv, second_peers())

    def finish(second, two, which):
        for copy in second:
            copy.wait()
        mean, spread = combine(two, float(count * 2 * Y))
        center, scale, offset = finish_norm(
            mean, spread, float(count * 2 * Y * Z), gain[pl.ds(which, 1)], shift[pl.ds(which, 1)]
        )
        norm[which, pl.ds(0, 2)] = center
        norm[which, pl.ds(2, 2)] = scale
        norm[which, pl.ds(4, 1)] = offset

    second = middle(first, one, two, x_send.at[1], x_recv.at[1])
    for copy in bank:
        copy.wait()
    chosen = held[bank_row[image_adapter[0, owner]]]
    lora[0, owner, patch] = chosen[0]
    lora[1, owner, patch] = chosen[1]
    pieces = [send_pieces(lora.at[0], lora_send.at[0], lora_recv.at[0])]
    for which in range(2):
        for d in range(3):
            last = kernels[which, d, :, pl.ds(256, chans - 256)].astype(F32)
            base[which, d] = jnp.concatenate([last, jnp.zeros_like(last)], axis=1).astype(BF16)
    finish(second, two, 0)
    for copies in borders:
        wait_borders(copies)

    part = rows // 2
    size = part * columns
    order = (owner, 1 - owner)

    def main_dots(image):
        def chunk(c, carry):
            window = windows(wide, image, c * part, part)
            total[image, pl.ds(pl.multiple_of(c * size, size), size), MAIN] = dots(window, kernels.at[0], MAIN)
            return carry

        lax.fori_loop(0, 2, chunk, 0)

    for step, image in enumerate(order):
        widen_image(own, top, bot, col, norm.at[0], image, wide, rem)
        main_dots(image)
        if step == 0:
            pieces.append(send_pieces(lora.at[1], lora_send.at[1], lora_recv.at[1]))

    def adapter(which, step, relay):
        if step == 0:
            for copy in pieces[which]:
                copy.wait()
            block = lora.at[which, owner]
            relay = remote(block, block, relay_send.at[which], relay_recv.at[which], (patch, req, 1 - owner))
            relay.start()
        else:
            relay.wait()
        image = order[step]
        lay_adapter(
            lora.at[which], image, base.at[which], tail.at[image], expand.at[image], flat, ups, wide_up
        )
        return relay

    borders, relay = [], None
    for step, image in enumerate(order):
        relay = adapter(0, step, relay)

        def chunk(c, carry, image=image):
            at = c * part
            window = windows(wide, image, at, part)
            span = pl.ds(pl.multiple_of(c * size, size), size)
            last = dots(window, tail.at[image], pl.ds(0, 128))
            small = last.astype(BF16)
            total[image, span, REST] = last + jnp.dot(small, expand[image, :, REST], preferred_element_type=F32)
            total[image, span, MAIN] += jnp.dot(small, expand[image, :, MAIN], preferred_element_type=F32)
            bias = norm[0, pl.ds(5 + image, 1)]
            for r in range(part):
                value = total[image, pl.ds(pl.multiple_of((at + r) * columns, columns), columns), pl.ds(0, chans)]
                hidden[image, at + r] = (value + bias).astype(BF16)
            return carry

        lax.fori_loop(0, 2, chunk, 0)
        borders.append(start_borders(hidden, top2, bot2, col2, image, edge2_send, edge2_recv))
        stats(hidden, image, one2)

    first = start_exchange(one2, x_send.at[2], x_recv.at[2], first_peers())
    relay = adapter(1, 0, None)
    second = middle(first, one2, two2, x_send.at[3], x_recv.at[3])
    adapter(1, 1, relay)
    finish(second, two2, 1)
    for copies in borders:
        wait_borders(copies)

    for image in order:
        widen_image(hidden, top2, bot2, col2, norm.at[1], image, wide, rem)

        def chunk(c, carry, image=image):
            at = c * part
            window = windows(wide, image, at, part)
            last = dots(window, tail.at[image], pl.ds(0, 128))
            small = last.astype(BF16)
            body = dots(window, kernels.at[1], MAIN)
            span = pl.ds(pl.multiple_of(c * size, size), size)
            total[image, span, MAIN] = body + jnp.dot(small, expand[image, :, MAIN], preferred_element_type=F32)
            total[image, span, REST] = last + jnp.dot(small, expand[image, :, REST], preferred_element_type=F32)
            for r in range(part):
                value = total[image, pl.ds(pl.multiple_of((at + r) * columns, columns), columns), pl.ds(0, chans)]
                out[image, at + r] = (value + own[image, at + r].astype(F32)).astype(BF16)
            return carry

        lax.fori_loop(0, 2, chunk, 0)


VM = pl.BlockSpec(memory_space=pltpu.VMEM)
HB = pl.BlockSpec(memory_space=pl.ANY)
SM = pl.BlockSpec(memory_space=pltpu.SMEM)
DMA = pltpu.SemaphoreType.DMA


def local(
    latents, timestep_embedding, embedding_weight, gain, shift, kernel_weight, reduce_library, expand_library,
    image_adapter, adapter_bank_row,
):
    images, rows, columns, chans = latents.shape
    pieces = Y * Z
    deep = UP_AT + 8
    map_of = (images, rows, columns, chans)
    line = pltpu.VMEM((images, columns, chans), BF16)
    edge = pltpu.VMEM((images, rows + 2, EDGE, chans), BF16)
    return pl.pallas_call(
        block_kernel,
        out_shape=jax.ShapeDtypeStruct(map_of, BF16),
        in_specs=[HB, VM, VM, SM, SM, VM, VM, VM, VM, HB],
        out_specs=VM,
        scratch_shapes=[
            pltpu.VMEM((images, rows, chans, columns), BF16),
            pltpu.VMEM(map_of, BF16),
            pltpu.VMEM(map_of, BF16),
            pltpu.VMEM((2, 3, 3 * chans, chans), BF16),
            pltpu.VMEM((images, rows + 2, columns, 3 * chans), BF16),
            pltpu.VMEM((images, rows * columns, 384), F32),
            pltpu.VMEM((2, 3, 3 * chans, 128), BF16),
            pltpu.VMEM((images, 3, 3 * chans, 128), BF16),
            pltpu.VMEM((images, 128, 384), BF16),
            pltpu.VMEM((9 * chans, 128), F32),
            pltpu.VMEM((pieces * 8, 128), F32),
            pltpu.VMEM((128, 128), F32),
            pltpu.VMEM((16, chans), F32),
            pltpu.VMEM((2, deep, 128), F32),
            pltpu.VMEM((8, 2, deep, 128), BF16),
            pltpu.VMEM((2, images, pieces, deep, 128), BF16),
            *([line, line, edge] * 2),
            pltpu.VMEM((2, 8, chans), F32),
            *([pltpu.VMEM((2 * Y, 8, chans), F32), pltpu.VMEM((Z, 8, chans), F32)] * 2),
            DMA((2,)),
            DMA((8,)),
            DMA((8,)),
            DMA((2, pieces)),
            DMA((2, pieces)),
            DMA((2,)),
            DMA((2,)),
            *([DMA((images, 5))] * 4),
            DMA((4, 8)),
            DMA((4, 8)),
        ],
        compiler_params=pltpu.CompilerParams(
            collective_id=0, has_side_effects=True, vmem_limit_bytes=56 * 2**20
        ),
        name="resnet_block",
    )(
        jnp.swapaxes(latents, 2, 3),
        reduce_library,
        expand_library,
        image_adapter.T,
        adapter_bank_row,
        timestep_embedding,
        embedding_weight.T,
        gain,
        shift,
        kernel_weight.reshape(2, 3, 3 * chans, chans),
    )


def solution(mesh):
    in_specs = (
        P("req", "patch", "owner", None),
        P("req", None),
        P(),
        P(),
        P(),
        P(),
        P(("req", "owner"), None, "patch"),
        P(("req", "owner"), None, "patch"),
        P("req", None),
        P(),
    )
    return jax.shard_map(
        local, mesh=mesh, in_specs=in_specs, out_specs=P("req", "patch", "owner", None), check_vma=False
    )
```

```python
import jax
import jax.numpy as jnp
from jax import lax
from jax.experimental import pallas as pl
from jax.experimental.pallas import tpu as pltpu
from jax.sharding import PartitionSpec as P

MESH = pl.DeviceIdType.MESH
F32, BF16 = jnp.float32, jnp.bfloat16
Y, Z = 4, 8
RANK = 64
EDGE = 16
GROUP = 10


def remote(src, dst, send, recv, device):
    return pltpu.make_async_remote_copy(
        src_ref=src, dst_ref=dst, send_sem=send, recv_sem=recv, device_id=device, device_id_type=MESH
    )


def place():
    patch, req, owner = lax.axis_index("patch"), lax.axis_index("req"), lax.axis_index("owner")
    return patch, req, owner, patch // Z, patch % Z


def near():
    patch, req, owner, y, z = place()
    return [
        (dz, dy, ((y + dy) % Y * Z + (z + dz) % Z, req, owner))
        for dz in (2, -2, 1, -1, 0)
        for dy in range(Y)
        if dz or dy
    ]


def greet():
    patch, req, owner, y, z = place()
    sem = pltpu.get_barrier_semaphore()
    count = 0

    def signal(device):
        pl.semaphore_signal(sem, inc=1, device_id=device, device_id_type=MESH)

    for _, _, device in near():
        signal(device)
        count += 1
    for dz in range(3, Z - 2):
        signal((y * Z + (z + dz) % Z, req, owner))
        count += 1
    for k in range(1, 2 * Y, 2):
        g = (y * 2 + owner + k) % (2 * Y)
        signal(((g // 2) * Z + z, req, g % 2))
        count += 1
    for step in (1, Y * Z - 1):
        signal(((patch + step) % (Y * Z), req, 1 - owner))
        count += 1
    for k in range(1, 8):
        g = (req * 2 + owner + k) % 8
        signal((patch, g // 2, g % 2))
        count += 1
    return lambda: pl.semaphore_wait(sem, count)


def start_borders(src, top, bot, col, image, send, recv):
    patch, req, owner, y, z = place()
    rows = src.shape[1]
    last = Y * Z - 1
    edge = pl.multiple_of((1 - owner) * (src.shape[2] - EDGE), EDGE)
    cols = pl.ds(edge, EDGE)

    def copy(at, block, target, device):
        return remote(block, target, send.at[image, at], recv.at[image, at], device)

    down, up = patch < last, patch > 0
    copies = [
        (down, up, copy(0, src.at[image, rows - 1], top.at[image], (patch + 1, req, owner))),
        (up, down, copy(1, src.at[image, 0], bot.at[image], (patch - 1, req, owner))),
        (down, up, copy(2, src.at[image, rows - 1, cols], col.at[image, 0], (patch + 1, req, 1 - owner))),
        (up, down, copy(3, src.at[image, 0, cols], col.at[image, rows + 1], (patch - 1, req, 1 - owner))),
        (None, None, copy(4, src.at[image, :, cols], col.at[image, pl.ds(1, rows)], (patch, req, 1 - owner))),
    ]
    for sends, _, item in copies:
        if sends is None:
            item.start()
        else:
            pl.when(sends)(item.start)
    return copies


def clear_borders(top, bot, col):
    patch = lax.axis_index("patch")
    end = col.shape[1] - 1

    @pl.when(patch == 0)
    def _():
        top[...] = jnp.zeros_like(top)
        col[:, 0] = jnp.zeros_like(col[:, 0])

    @pl.when(patch == Y * Z - 1)
    def _():
        bot[...] = jnp.zeros_like(bot)
        col[:, end] = jnp.zeros_like(col[:, end])


def wait_borders(copies):
    for sends, receives, copy in copies:
        if sends is None:
            copy.wait_send()
            copy.wait_recv()
        else:
            pl.when(sends)(copy.wait_send)
            pl.when(receives)(copy.wait_recv)


def local_stats(rows_of, rows):
    def add(f):
        def step(r, total):
            x = f(rows_of(r).astype(F32))
            return total + jnp.sum(x.reshape(x.shape[0] // 8, 8, x.shape[1]), axis=0)

        return step

    chans = rows_of(0).shape[1]
    count = rows * rows_of(0).shape[0]
    zero = jnp.zeros((8, chans), F32)
    total = lax.fori_loop(0, rows, add(lambda x: x), zero)
    mean = jnp.sum(total, axis=0, keepdims=True) * (1.0 / count)
    spread = lax.fori_loop(0, rows, add(lambda x: (x - mean) * (x - mean)), zero)
    return mean, jnp.sum(spread, axis=0, keepdims=True)


def start_exchange(slots, send, recv, peers):
    copies = [
        remote(slots.at[0], slots.at[k], send.at[k], recv.at[k], peer) for k, peer in enumerate(peers, 1)
    ]
    for copy in copies:
        copy.start()
    return copies


def combine(slots, count):
    values = slots[...]
    half = values.shape[1] // 2
    total = jnp.sum(values, axis=0)
    mean = total * (1.0 / values.shape[0])
    off = values - mean[None]
    between = jnp.sum(off * off, axis=0)
    return mean[0:half], total[half:] + count * between[0:half]


def first_peers():
    patch, req, owner, y, z = place()
    peers = []
    for k in range(1, 2 * Y):
        g = (y * 2 + owner + k) % (2 * Y)
        peers.append(((g // 2) * Z + z, req, g % 2))
    return peers


def second_peers():
    patch, req, owner, y, z = place()
    return [(y * Z + (z + k) % Z, req, owner) for k in range(1, Z)]


def group_matrix(chans):
    row = lax.broadcasted_iota(jnp.int32, (chans, chans), 0)
    column = lax.broadcasted_iota(jnp.int32, (chans, chans), 1)
    return jnp.where((row * 6554) >> 16 == (column * 6554) >> 16, 1.0, 0.0).astype(BF16)


def group_mean(values, groups):
    count = values.shape[0]
    values = jnp.concatenate([values] * (8 // count), axis=0)
    high = values.astype(BF16).astype(F32)
    rest = values - high
    middle = rest.astype(BF16).astype(F32)
    parts = jnp.concatenate([high, middle, rest - middle], axis=0).astype(BF16)
    total = jnp.dot(parts, groups, preferred_element_type=F32)
    return (total[0:count] + total[8 : 8 + count] + total[16 : 16 + count]) * (1.0 / GROUP)


def finish_norm(mean, spread, count, gain, shift, groups):
    center = group_mean(mean, groups)
    off = mean - center
    var = group_mean(spread * (1.0 / count) + off * off, groups)
    scale = gain / jnp.sqrt(var + 1e-05)
    return center, 0.5 * scale, 0.5 * shift


def lay_piece(reduce_row, expand_row, piece):
    down = reduce_row[0].astype(F32)
    up = expand_row[0].astype(F32)
    piece[...] = jnp.zeros_like(piece)
    for i in range(down.shape[1] // 128):
        piece[:, i, :] = down[:, i * 128 : i * 128 + 128]
    for i in range(up.shape[1] // 128):
        piece[:, UP_AT + i, :] = up[:, i * 128 : i * 128 + 128]
    return piece[...].astype(BF16)


def send_near(lora, send, recv):
    patch, req, owner, y, z = place()
    block = lora.at[owner, z, y]
    copies = {}
    for k, (dz, dy, device) in enumerate(near()):
        copies[dz, dy] = remote(block, block, send.at[k], recv.at[k], device)
        copies[dz, dy].start()
    return copies


def send_far(copies, lora, send, recv):
    patch, req, owner, y, z = place()
    half = Y // 2

    def forward(at, column, ys, dz):
        block = lora.at[owner, column, ys]
        copy = remote(block, block, send.at[at], recv.at[at], (y * Z + (z + dz) % Z, req, owner))
        copy.start()
        copies[at] = copy

    for dz in (2, -2):
        for dy in range(Y):
            copies.pop((dz, dy)).wait()
    below, above = (z + Z - 2) % Z, (z + 2) % Z
    forward(20, below, pl.ds(0, Y), 1)
    forward(21, above, pl.ds(0, Y), Z - 1)
    forward(22, below, pl.ds(0, half), 2)
    forward(23, above, pl.ds(half, half), Z - 2)


def lay_adapter(lora, image, base, tail, expand, flat, ups, wide_up):
    pieces = Y * Z
    depth = tail.shape[1] * 3 // pieces
    half = depth // 2

    def lay(p, carry):
        value = lora[image, p % Z, p // Z].astype(F32)
        down = value[0:half]
        flat[pl.ds(p * depth, half, 2)] = pltpu.roll(down, 64, 1)
        flat[pl.ds(p * depth + 1, half, 2)] = down
        ups[pl.ds(pl.multiple_of(p * 8, 8), 8)] = value[UP_AT : UP_AT + 8]
        return carry

    lax.fori_loop(0, pieces, lay, 0)
    lane = lax.broadcasted_iota(jnp.int32, base.shape[1:], 1)
    for d in range(3):
        down = flat[pl.ds(d * base.shape[1], base.shape[1])]
        tail[d] = jnp.where(lane >= 64, down, base[d].astype(F32)).astype(BF16)
    line = [ups[pl.ds(k, pieces, 8)] for k in range(5)]
    turned = [pltpu.roll(v, 64, 1) for v in line]
    low = lax.broadcasted_iota(jnp.int32, line[0].shape, 1) < 64
    even = line[0:3]
    odd = [jnp.where(low, turned[2], turned[3]), jnp.where(low, turned[3], turned[4]), turned[4]]
    for b in range(3):
        wide_up[pl.ds(0, 64)] = jnp.zeros((64, 128), F32)
        wide_up[pl.ds(64, pieces, 2)] = even[b]
        wide_up[pl.ds(65, pieces, 2)] = odd[b]
        expand[:, pl.ds(b * 128, 128)] = wide_up[...].astype(BF16)


def widen_image(source, top, bot, col, norm, image, wide, rem):
    patch, req, owner, y, z = place()
    rows, columns = source.shape[1:3]
    last = Y * Z - 1
    index = lax.broadcasted_iota(jnp.int32, (columns, 1), 0)
    across = lax.broadcasted_iota(jnp.int32, (rows + 2, 1), 0)
    beyond = ((patch > 0) | (across > 0)) & ((patch < last) | (across < rows + 1))
    center = norm[pl.ds(image, 1)]
    scale = norm[pl.ds(2 + image, 1)]
    offset = norm[pl.ds(4, 1)]

    def activate(x):
        h = (x.astype(F32) - center) * scale + offset
        return h + h * jnp.tanh(h)

    border = jnp.where(owner == 0, col[image, :, 0, :].astype(F32), col[image, :, EDGE - 1, :].astype(F32))
    rem[pl.ds(0, rows + 2)] = jnp.where(beyond, activate(border), 0.0)

    def lay(r, act):
        edge = rem[pl.ds(r, 1)]
        left = jnp.where(index == 0, jnp.where(owner == 1, edge, 0.0), pltpu.roll(act, 1, 0))
        right = jnp.where(
            index == columns - 1, jnp.where(owner == 0, edge, 0.0), pltpu.roll(act, columns - 1, 0)
        )
        wide[image, r] = jnp.concatenate([left, act, right], axis=1).astype(BF16)

    lay(0, jnp.where(patch > 0, activate(top[image]), 0.0))
    lay(rows + 1, jnp.where(patch < last, activate(bot[image]), 0.0))

    def row(r, carry):
        lay(r + 1, activate(source[image, r]))
        return carry

    lax.fori_loop(0, rows, row, 0)


def windows(wide, image, at, part):
    columns, depth = wide.shape[2:]
    return [wide[image, pl.ds(at + d, part)].reshape(part * columns, depth) for d in range(3)]


def dots(window, matrix, lanes):
    return sum(jnp.dot(window[d], matrix[d, :, lanes], preferred_element_type=F32) for d in range(3))


MAIN, REST = pl.ds(0, 256), pl.ds(256, 128)
UP_AT = 48


def block_kernel(
    raw, reduce_row, expand_row, image_adapter, bank_row, embedding, weight_hbm, gain, shift, kernels_hbm,
    out,
    raw_own, weight, groups, own, hidden, kernels, wide, total, base, tail, expand, flat, ups, wide_up, rem,
    piece, held, lora, top, bot, col, top2, bot2, col2, norm, one, two, one2, two2,
    local_sem, bank_send, bank_recv, lora_send, lora_recv, relay_send, relay_recv,
    edge_send, edge_recv, edge2_send, edge2_recv, x_send, x_recv,
):
    patch, req, owner, y, z = place()
    images, rows, columns, chans = own.shape
    count = rows * columns
    fetch = pltpu.make_async_copy(raw, raw_own, local_sem.at[0])
    fetch.start()
    fetch_kernels = pltpu.make_async_copy(kernels_hbm, kernels, local_sem.at[1])
    fetch_kernels.start()
    fetch_weight = pltpu.make_async_copy(weight_hbm, weight, local_sem.at[2])
    fetch_weight.start()
    arrived = greet()
    me = req * 2 + owner
    held[me] = lay_piece(reduce_row, expand_row, piece)
    clear_borders(top, bot, col)
    clear_borders(top2, bot2, col2)
    groups[...] = group_matrix(chans)
    fetch.wait()

    def turn(t, carry):
        image, r = t // rows, t % rows
        own[image, r] = jnp.transpose(raw_own[image, r].astype(F32)).astype(BF16)
        return carry

    lax.fori_loop(0, images * rows, turn, 0)

    for image in range(images):
        mean, spread = local_stats(lambda r, image=image: own[image, r], rows)
        one[0, pl.ds(image, 1)] = mean
        one[0, pl.ds(2 + image, 1)] = spread
    arrived()

    first = start_exchange(one, x_send.at[0], x_recv.at[0], first_peers())
    bank = []
    for k in range(1, 8):
        g = (me + k) % 8
        copy = remote(held.at[me], held.at[me], bank_send.at[k], bank_recv.at[k], (patch, g // 2, g % 2))
        copy.start()
        bank.append(copy)

    fetch_weight.wait()
    u = embedding[...].astype(F32)
    temb = (u / (1.0 + jnp.exp(-u))).astype(BF16)
    proj = lax.dot_general(temb, weight[...], (((1,), (1,)), ((), ())), preferred_element_type=F32)
    norm[0, pl.ds(5, 2)] = proj
    fetch_kernels.wait()

    def middle(first, one, two, at):
        for copy in first:
            copy.wait()
        mean, spread = combine(one, float(count))
        half = mean.shape[0]
        two[0, pl.ds(0, half)] = mean
        two[0, pl.ds(half, half)] = spread
        return start_exchange(two, x_send.at[at], x_recv.at[at], second_peers())

    def finish(second, two, which, image):
        for copy in second:
            copy.wait()
        mean, spread = combine(two, float(count * 2 * Y))
        half = mean.shape[0]
        center, scale, offset = finish_norm(
            mean, spread, float(count * 2 * Y * Z), gain[pl.ds(which, 1)], shift[pl.ds(which, 1)], groups[...]
        )
        norm[which, pl.ds(image, half)] = center
        norm[which, pl.ds(2 + image, half)] = scale
        norm[which, pl.ds(4, 1)] = offset

    second = middle(first, one, two, 1)
    borders = [start_borders(own, top, bot, col, i, edge_send, edge_recv) for i in range(images)]
    for copy in bank:
        copy.wait()
    chosen = held[bank_row[image_adapter[0, owner]]]
    lora[0, owner, z, y] = chosen[0]
    lora[1, owner, z, y] = chosen[1]
    pieces = [send_near(lora.at[0], lora_send.at[0], lora_recv.at[0])]
    for which in range(2):
        for d in range(3):
            last = kernels[which, d, :, pl.ds(256, chans - 256)].astype(F32)
            base[which, d] = jnp.concatenate([last, jnp.zeros_like(last)], axis=1).astype(BF16)
    finish(second, two, 0, 0)
    send_far(pieces[0], lora.at[0], lora_send.at[0], lora_recv.at[0])
    pieces.append(send_near(lora.at[1], lora_send.at[1], lora_recv.at[1]))
    for copies in borders:
        wait_borders(copies)

    part = rows // 2
    size = part * columns

    def main_chunk(image, c):
        window = windows(wide, image, c * part, part)
        total[image, pl.ds(c * size, size), MAIN] = dots(window, kernels.at[0], MAIN)

    def relay(which):
        for copy in pieces[which].values():
            copy.wait()
        block = lora.at[which, owner]
        copy = remote(block, block, relay_send.at[which], relay_recv.at[which], (patch, req, 1 - owner))
        copy.start()
        return copy

    def adapter(which, image, copy):
        pl.when(owner != image)(copy.wait)
        lay_adapter(
            lora.at[which], image, base.at[which], tail.at[image], expand.at[image], flat, ups, wide_up
        )

    def tail_chunk(image, c):
        window = windows(wide, image, c * part, part)
        span = pl.ds(c * size, size)
        last = dots(window, tail.at[image], pl.ds(0, 128))
        small = last.astype(BF16)
        total[image, span, REST] = last + jnp.dot(small, expand[image, :, REST], preferred_element_type=F32)
        total[image, span, MAIN] += jnp.dot(small, expand[image, :, MAIN], preferred_element_type=F32)
        bias = norm[0, pl.ds(5 + image, 1)]
        for r in range(c * part, c * part + part):
            value = total[image, pl.ds(r * columns, columns), pl.ds(0, chans)]
            hidden[image, r] = (value + bias).astype(BF16)

    def hidden_done(image):
        mean, spread = local_stats(lambda r: hidden[image, r], rows)
        one2[image, 0, pl.ds(0, 1)] = mean
        one2[image, 0, pl.ds(1, 1)] = spread
        first = start_exchange(one2.at[image], x_send.at[2 + image], x_recv.at[2 + image], first_peers())
        borders = start_borders(hidden, top2, bot2, col2, image, edge2_send, edge2_recv)
        return first, borders

    widen_image(own, top, bot, col, norm.at[0], 0, wide, rem)
    main_chunk(0, 0)
    main_chunk(0, 1)
    send_far(pieces[1], lora.at[1], lora_send.at[1], lora_recv.at[1])
    widen_image(own, top, bot, col, norm.at[0], 1, wide, rem)
    main_chunk(1, 0)
    relay0 = relay(0)
    main_chunk(1, 1)

    adapter(0, 0, relay0)
    tail_chunk(0, 0)
    tail_chunk(0, 1)
    first0, borders0 = hidden_done(0)
    adapter(0, 1, relay0)
    tail_chunk(1, 0)
    second0 = middle(first0, one2.at[0], two2.at[0], 4)
    tail_chunk(1, 1)
    first1, borders1 = hidden_done(1)
    relay1 = relay(1)
    adapter(1, 0, relay1)
    finish(second0, two2.at[0], 1, 0)
    wait_borders(borders0)
    second1 = middle(first1, one2.at[1], two2.at[1], 5)

    def final_chunk(image, c):
        window = windows(wide, image, c * part, part)
        last = dots(window, tail.at[image], pl.ds(0, 128))
        small = last.astype(BF16)
        body = dots(window, kernels.at[1], MAIN)
        span = pl.ds(c * size, size)
        total[image, span, MAIN] = body + jnp.dot(small, expand[image, :, MAIN], preferred_element_type=F32)
        total[image, span, REST] = last + jnp.dot(small, expand[image, :, REST], preferred_element_type=F32)
        for r in range(c * part, c * part + part):
            value = total[image, pl.ds(r * columns, columns), pl.ds(0, chans)]
            out[image, r] = (value + own[image, r].astype(F32)).astype(BF16)

    for image in range(images):
        if image == 1:
            adapter(1, 1, relay1)
            finish(second1, two2.at[1], 1, 1)
            wait_borders(borders1)
        widen_image(hidden, top2, bot2, col2, norm.at[1], image, wide, rem)
        final_chunk(image, 0)
        final_chunk(image, 1)


VM = pl.BlockSpec(memory_space=pltpu.VMEM)
HB = pl.BlockSpec(memory_space=pl.ANY)
SM = pl.BlockSpec(memory_space=pltpu.SMEM)
DMA = pltpu.SemaphoreType.DMA


def local(
    latents, timestep_embedding, embedding_weight, gain, shift, kernel_weight, reduce_library, expand_library,
    image_adapter, adapter_bank_row,
):
    images, rows, columns, chans = latents.shape
    pieces = Y * Z
    deep = UP_AT + 8
    map_of = (images, rows, columns, chans)
    line = pltpu.VMEM((images, columns, chans), BF16)
    edge = pltpu.VMEM((images, rows + 2, EDGE, chans), BF16)
    return pl.pallas_call(
        block_kernel,
        out_shape=jax.ShapeDtypeStruct(map_of, BF16),
        in_specs=[HB, VM, VM, SM, SM, VM, HB, VM, VM, HB],
        out_specs=VM,
        scratch_shapes=[
            pltpu.VMEM((images, rows, chans, columns), BF16),
            pltpu.VMEM((chans, embedding_weight.shape[0]), BF16),
            pltpu.VMEM((chans, chans), BF16),
            pltpu.VMEM(map_of, BF16),
            pltpu.VMEM(map_of, BF16),
            pltpu.VMEM((2, 3, 3 * chans, chans), BF16),
            pltpu.VMEM((images, rows + 2, columns, 3 * chans), BF16),
            pltpu.VMEM((images, rows * columns, 384), F32),
            pltpu.VMEM((2, 3, 3 * chans, 128), BF16),
            pltpu.VMEM((images, 3, 3 * chans, 128), BF16),
            pltpu.VMEM((images, 128, 384), BF16),
            pltpu.VMEM((9 * chans, 128), F32),
            pltpu.VMEM((pieces * 8, 128), F32),
            pltpu.VMEM((128, 128), F32),
            pltpu.VMEM((16, chans), F32),
            pltpu.VMEM((2, deep, 128), F32),
            pltpu.VMEM((8, 2, deep, 128), BF16),
            pltpu.VMEM((2, images, Z, Y, deep, 128), BF16),
            *([line, line, edge] * 2),
            pltpu.VMEM((2, 8, chans), F32),
            pltpu.VMEM((2 * Y, 4, chans), F32),
            pltpu.VMEM((Z, 4, chans), F32),
            pltpu.VMEM((images, 2 * Y, 2, chans), F32),
            pltpu.VMEM((images, Z, 2, chans), F32),
            DMA((3,)),
            DMA((8,)),
            DMA((8,)),
            DMA((2, 24)),
            DMA((2, 24)),
            DMA((2,)),
            DMA((2,)),
            *([DMA((images, 5))] * 4),
            DMA((6, 8)),
            DMA((6, 8)),
        ],
        compiler_params=pltpu.CompilerParams(
            collective_id=0, has_side_effects=True, vmem_limit_bytes=56 * 2**20
        ),
        name="resnet_block",
    )(
        jnp.swapaxes(latents, 2, 3),
        reduce_library,
        expand_library,
        image_adapter.T,
        adapter_bank_row,
        timestep_embedding,
        embedding_weight.T,
        gain,
        shift,
        kernel_weight.reshape(2, 3, 3 * chans, chans),
    )


def solution(mesh):
    in_specs = (
        P("req", "patch", "owner", None),
        P("req", None),
        P(),
        P(),
        P(),
        P(),
        P(("req", "owner"), None, "patch"),
        P(("req", "owner"), None, "patch"),
        P("req", None),
        P(),
    )
    return jax.shard_map(
        local, mesh=mesh, in_specs=in_specs, out_specs=P("req", "patch", "owner", None), check_vma=False
    )
```

```python
import jax
import jax.numpy as jnp
from jax import lax
from jax.experimental import pallas as pl
from jax.experimental.pallas import tpu as pltpu
from jax.sharding import PartitionSpec as P

MESH = pl.DeviceIdType.MESH
F32, BF16 = jnp.float32, jnp.bfloat16
Y, Z = 4, 8
RANK = 64
EDGE = 16
GROUP = 10


def remote(src, dst, send, recv, device):
    return pltpu.make_async_remote_copy(
        src_ref=src, dst_ref=dst, send_sem=send, recv_sem=recv, device_id=device, device_id_type=MESH
    )


def place():
    patch, req, owner = lax.axis_index("patch"), lax.axis_index("req"), lax.axis_index("owner")
    return patch, req, owner, patch // Z, patch % Z


def greet():
    patch, req, owner, y, z = place()
    sem = pltpu.get_barrier_semaphore()
    count = 0

    def signal(device):
        pl.semaphore_signal(sem, inc=1, device_id=device, device_id_type=MESH)

    for dz in range(1, Z):
        signal((y * Z + (z + dz) % Z, req, owner))
        count += 1
    for dy in range(1, Y):
        signal(((y + dy) % Y * Z + z, req, owner))
        count += 1
    for k in range(1, 2 * Y, 2):
        g = (y * 2 + owner + k) % (2 * Y)
        signal(((g // 2) * Z + z, req, g % 2))
        count += 1
    for step in (1, Y * Z - 1):
        for other in (owner, 1 - owner):
            signal(((patch + step) % (Y * Z), req, other))
            count += 1
    for k in range(1, 8):
        g = (req * 2 + owner + k) % 8
        signal((patch, g // 2, g % 2))
        count += 1
    return lambda: pl.semaphore_wait(sem, count)


def start_borders(src, top, bot, col, image, send, recv):
    patch, req, owner, y, z = place()
    rows = src.shape[1]
    last = Y * Z - 1
    edge = pl.multiple_of((1 - owner) * (src.shape[2] - EDGE), EDGE)
    cols = pl.ds(edge, EDGE)

    def copy(at, block, target, device):
        return remote(block, target, send.at[image, at], recv.at[image, at], device)

    down, up = patch < last, patch > 0
    copies = [
        (down, up, copy(0, src.at[image, rows - 1], top.at[image], (patch + 1, req, owner))),
        (up, down, copy(1, src.at[image, 0], bot.at[image], (patch - 1, req, owner))),
        (down, up, copy(2, src.at[image, rows - 1, cols], col.at[image, 0], (patch + 1, req, 1 - owner))),
        (up, down, copy(3, src.at[image, 0, cols], col.at[image, rows + 1], (patch - 1, req, 1 - owner))),
        (None, None, copy(4, src.at[image, :, cols], col.at[image, pl.ds(1, rows)], (patch, req, 1 - owner))),
    ]
    for sends, _, item in copies:
        if sends is None:
            item.start()
        else:
            pl.when(sends)(item.start)
    return copies


def clear_borders(top, bot, col):
    patch = lax.axis_index("patch")
    end = col.shape[1] - 1

    @pl.when(patch == 0)
    def _():
        top[...] = jnp.zeros_like(top)
        col[:, 0] = jnp.zeros_like(col[:, 0])

    @pl.when(patch == Y * Z - 1)
    def _():
        bot[...] = jnp.zeros_like(bot)
        col[:, end] = jnp.zeros_like(col[:, end])


def wait_borders(copies):
    for sends, receives, copy in copies:
        if sends is None:
            copy.wait()
        else:
            pl.when(sends)(copy.wait_send)
            pl.when(receives)(copy.wait_recv)


def local_stats(rows_of, rows):
    def add(f):
        def step(r, total):
            x = f(rows_of(r).astype(F32))
            return total + jnp.sum(x.reshape(x.shape[0] // 8, 8, x.shape[1]), axis=0)

        return step

    chans = rows_of(0).shape[1]
    count = rows * rows_of(0).shape[0]
    zero = jnp.zeros((8, chans), F32)
    total = lax.fori_loop(0, rows, add(lambda x: x), zero)
    mean = jnp.sum(total, axis=0, keepdims=True) * (1.0 / count)
    spread = lax.fori_loop(0, rows, add(lambda x: (x - mean) * (x - mean)), zero)
    return mean, jnp.sum(spread, axis=0, keepdims=True)


def start_exchange(slots, send, recv, peers):
    copies = [
        remote(slots.at[0], slots.at[k], send.at[k], recv.at[k], peer) for k, peer in enumerate(peers, 1)
    ]
    for copy in copies:
        copy.start()
    return copies


def combine(slots, count):
    values = slots[...]
    half = values.shape[1] // 2
    total = jnp.sum(values, axis=0)
    mean = total * (1.0 / values.shape[0])
    off = values - mean[None]
    between = jnp.sum(off * off, axis=0)
    return mean[0:half], total[half:] + count * between[0:half]


def first_peers():
    patch, req, owner, y, z = place()
    peers = []
    for k in range(1, 2 * Y):
        g = (y * 2 + owner + k) % (2 * Y)
        peers.append(((g // 2) * Z + z, req, g % 2))
    return peers


def second_peers():
    patch, req, owner, y, z = place()
    return [(y * Z + (z + k) % Z, req, owner) for k in range(1, Z)]


def group_matrix(chans):
    row = lax.broadcasted_iota(jnp.int32, (chans, chans), 0)
    column = lax.broadcasted_iota(jnp.int32, (chans, chans), 1)
    return jnp.where((row * 6554) >> 16 == (column * 6554) >> 16, 1.0, 0.0).astype(BF16)


def group_mean(values, groups):
    count = values.shape[0]
    values = jnp.concatenate([values] * (8 // count), axis=0)
    high = values.astype(BF16).astype(F32)
    rest = values - high
    middle = rest.astype(BF16).astype(F32)
    parts = jnp.concatenate([high, middle, rest - middle], axis=0).astype(BF16)
    total = jnp.dot(parts, groups, preferred_element_type=F32)
    return (total[0:count] + total[8 : 8 + count] + total[16 : 16 + count]) * (1.0 / GROUP)


def finish_norm(mean, spread, count, gain, shift, groups):
    center = group_mean(mean, groups)
    off = mean - center
    var = group_mean(spread * (1.0 / count) + off * off, groups)
    scale = gain / jnp.sqrt(var + 1e-05)
    return center, 0.5 * scale, 0.5 * shift


def lay_piece(reduce_row, expand_row, piece):
    down = reduce_row[0].astype(F32)
    up = expand_row[0].astype(F32)
    piece[...] = jnp.zeros_like(piece)
    for i in range(down.shape[1] // 128):
        piece[:, i, :] = down[:, i * 128 : i * 128 + 128]
    for i in range(up.shape[1] // 128):
        piece[:, UP_AT + i, :] = up[:, i * 128 : i * 128 + 128]
    return piece[...].astype(BF16)


def send_along_z(lora, send, recv):
    patch, req, owner, y, z = place()
    block = lora.at[owner, y, z]
    copies = [
        remote(block, block, send.at[k], recv.at[k], (y * Z + (z + k) % Z, req, owner)) for k in range(1, Z)
    ]
    for copy in copies:
        copy.start()
    return copies


def send_along_y(copies, lora, send, recv):
    patch, req, owner, y, z = place()
    for copy in copies:
        copy.wait()
    block = lora.at[owner, y]
    copies = [
        remote(block, block, send.at[Z + k], recv.at[Z + k], ((y + k) % Y * Z + z, req, owner))
        for k in (2, 1, 3)
    ]
    for copy in copies:
        copy.start()
    return copies


def lay_adapter(lora, image, base, tail, expand, flat, ups, wide_up):
    pieces = Y * Z
    depth = tail.shape[1] * 3 // pieces
    half = depth // 2

    def lay(p, carry):
        value = lora[image, p // Z, p % Z].astype(F32)
        down = value[0:half]
        flat[pl.ds(p * depth, half, 2)] = pltpu.roll(down, 64, 1)
        flat[pl.ds(p * depth + 1, half, 2)] = down
        ups[pl.ds(pl.multiple_of(p * 8, 8), 8)] = value[UP_AT : UP_AT + 8]
        return carry

    lax.fori_loop(0, pieces, lay, 0)
    lane = lax.broadcasted_iota(jnp.int32, base.shape[1:], 1)
    for d in range(3):
        down = flat[pl.ds(d * base.shape[1], base.shape[1])]
        tail[d] = jnp.where(lane >= 64, down, base[d].astype(F32)).astype(BF16)
    line = [ups[pl.ds(k, pieces, 8)] for k in range(5)]
    turned = [pltpu.roll(v, 64, 1) for v in line]
    low = lax.broadcasted_iota(jnp.int32, line[0].shape, 1) < 64
    even = line[0:3]
    odd = [jnp.where(low, turned[2], turned[3]), jnp.where(low, turned[3], turned[4]), turned[4]]
    for b in range(3):
        wide_up[pl.ds(0, 64)] = jnp.zeros((64, 128), F32)
        wide_up[pl.ds(64, pieces, 2)] = even[b]
        wide_up[pl.ds(65, pieces, 2)] = odd[b]
        expand[:, pl.ds(b * 128, 128)] = wide_up[...].astype(BF16)


def widen_image(source, top, bot, col, norm, image, wide, rem, inner):
    patch, req, owner, y, z = place()
    rows, columns = source.shape[1:3]
    last = Y * Z - 1
    index = lax.broadcasted_iota(jnp.int32, (columns, 1), 0)
    center = norm[pl.ds(image, 1)]
    scale = norm[pl.ds(2 + image, 1)]
    offset = norm[pl.ds(4, 1)]

    def activate(x):
        h = (x.astype(F32) - center) * scale + offset
        return h + h * jnp.tanh(h)

    def border(at):
        return activate(
            jnp.where(owner == 0, col[image, at, 0, :].astype(F32), col[image, at, EDGE - 1, :].astype(F32))
        )

    def lay(r, act, edge):
        left = jnp.where(index == 0, jnp.where(owner == 1, edge, 0.0), pltpu.roll(act, 1, 0))
        right = jnp.where(
            index == columns - 1, jnp.where(owner == 0, edge, 0.0), pltpu.roll(act, columns - 1, 0)
        )
        wide[image, r] = jnp.concatenate([left, act, right], axis=1).astype(BF16)

    if inner:
        rem[pl.ds(0, rows)] = border(slice(1, rows + 1))

        def row(r, carry):
            lay(r + 1, activate(source[image, r]), rem[pl.ds(r, 1)])
            return carry

        lax.fori_loop(0, rows, row, 0)
    else:
        for r, block, inside in ((0, top, patch > 0), (rows + 1, bot, patch < last)):
            edge = jnp.where(inside, border(slice(r, r + 1)), 0.0)
            lay(r, jnp.where(inside, activate(block[image]), 0.0), edge)


def windows(wide, image, at, part):
    columns, depth = wide.shape[2:]
    return [wide[image, pl.ds(at + d, part)].reshape(part * columns, depth) for d in range(3)]


def edge_windows(wide, image):
    last = wide.shape[1] - 3
    return [jnp.concatenate([wide[image, d], wide[image, last + d]], axis=0) for d in range(3)]


def dots(window, matrix, lanes):
    return sum(jnp.dot(window[d], matrix[d, :, lanes], preferred_element_type=F32) for d in range(3))


MAIN, REST = pl.ds(0, 256), pl.ds(256, 128)
UP_AT = 48


def block_kernel(
    raw, reduce_row, expand_row, image_adapter, bank_row, embedding, weight_hbm, gain, shift, kernels_hbm,
    out,
    raw_own, weight, groups, own, hidden, kernels, wide, total, base, tail, expand, flat, ups, wide_up, rem,
    piece, held, lora, top, bot, col, top2, bot2, col2, norm, one, two, one2, two2,
    local_sem, bank_send, bank_recv, lora_send, lora_recv, relay_send, relay_recv,
    edge_send, edge_recv, edge2_send, edge2_recv, x_send, x_recv,
):
    patch, req, owner, y, z = place()
    images, rows, columns, chans = own.shape
    count = rows * columns
    fetch = pltpu.make_async_copy(raw, raw_own, local_sem.at[0])
    fetch.start()
    fetch_kernels = pltpu.make_async_copy(kernels_hbm, kernels, local_sem.at[1])
    fetch_kernels.start()
    fetch_weight = pltpu.make_async_copy(weight_hbm, weight, local_sem.at[2])
    fetch_weight.start()
    arrived = greet()
    me = req * 2 + owner
    held[me] = lay_piece(reduce_row, expand_row, piece)
    clear_borders(top, bot, col)
    clear_borders(top2, bot2, col2)
    groups[...] = group_matrix(chans)
    fetch.wait()

    def turn(t, carry):
        image, r = t // rows, t % rows
        own[image, r] = jnp.transpose(raw_own[image, r].astype(F32)).astype(BF16)
        return carry

    lax.fori_loop(0, images * rows, turn, 0)

    for image in range(images):
        mean, spread = local_stats(lambda r, image=image: own[image, r], rows)
        one[0, pl.ds(image, 1)] = mean
        one[0, pl.ds(2 + image, 1)] = spread
    arrived()

    first = start_exchange(one, x_send.at[0], x_recv.at[0], first_peers())
    bank = []
    for k in range(1, 8):
        g = (me + k) % 8
        copy = remote(held.at[me], held.at[me], bank_send.at[k], bank_recv.at[k], (patch, g // 2, g % 2))
        copy.start()
        bank.append(copy)

    fetch_weight.wait()
    u = embedding[...].astype(F32)
    temb = (u / (1.0 + jnp.exp(-u))).astype(BF16)
    proj = lax.dot_general(temb, weight[...], (((1,), (1,)), ((), ())), preferred_element_type=F32)
    norm[0, pl.ds(5, 2)] = proj
    fetch_kernels.wait()

    def middle(first, one, two, at):
        for copy in first:
            copy.wait()
        mean, spread = combine(one, float(count))
        half = mean.shape[0]
        two[0, pl.ds(0, half)] = mean
        two[0, pl.ds(half, half)] = spread
        return start_exchange(two, x_send.at[at], x_recv.at[at], second_peers())

    def finish(second, two, which, image):
        for copy in second:
            copy.wait()
        mean, spread = combine(two, float(count * 2 * Y))
        half = mean.shape[0]
        center, scale, offset = finish_norm(
            mean, spread, float(count * 2 * Y * Z), gain[pl.ds(which, 1)], shift[pl.ds(which, 1)], groups[...]
        )
        norm[which, pl.ds(image, half)] = center
        norm[which, pl.ds(2 + image, half)] = scale
        norm[which, pl.ds(4, 1)] = offset

    second = middle(first, one, two, 1)
    for copy in bank:
        copy.wait()
    chosen = held[bank_row[image_adapter[0, owner]]]
    lora[0, owner, y, z] = chosen[0]
    lora[1, owner, y, z] = chosen[1]
    pieces = [send_along_z(lora.at[0], lora_send.at[0], lora_recv.at[0])]
    borders = [start_borders(own, top, bot, col, i, edge_send, edge_recv) for i in range(images)]
    for which in range(2):
        for d in range(3):
            last = kernels[which, d, :, pl.ds(256, chans - 256)].astype(F32)
            base[which, d] = jnp.concatenate([last, jnp.zeros_like(last)], axis=1).astype(BF16)
    finish(second, two, 0, 0)
    pieces[0] = send_along_y(pieces[0], lora.at[0], lora_send.at[0], lora_recv.at[0])

    order = (owner, 1 - owner)
    inner = (rows - 2) // 2
    ends = (0, rows - 1)

    def pixels(r, count=1):
        return pl.ds(pl.multiple_of(r * columns, columns), count * columns)

    def main_inner(image):
        def chunk(c, carry):
            at = 1 + c * inner
            total[image, pixels(at, inner), MAIN] = dots(windows(wide, image, at, inner), kernels.at[0], MAIN)
            return carry

        lax.fori_loop(0, 2, chunk, 0)

    def main_edges(image):
        value = dots(edge_windows(wide, image), kernels.at[0], MAIN)
        for i, r in enumerate(ends):
            total[image, pixels(r), MAIN] = value[i * columns : (i + 1) * columns]

    def relay(which):
        for copy in pieces[which]:
            copy.wait()
        block = lora.at[which, owner]
        copy = remote(block, block, relay_send.at[which], relay_recv.at[which], (patch, req, 1 - owner))
        copy.start()
        return copy

    def adapter(which, image):
        lay_adapter(
            lora.at[which], image, base.at[which], tail.at[image], expand.at[image], flat, ups, wide_up
        )

    def tail_dots(image):
        part = rows // 2

        def chunk(c, carry):
            at = c * part
            last = dots(windows(wide, image, at, part), tail.at[image], pl.ds(0, 128))
            small = last.astype(BF16)
            span = pixels(at, part)
            total[image, span, REST] = last + jnp.dot(small, expand[image, :, REST], preferred_element_type=F32)
            total[image, span, MAIN] += jnp.dot(small, expand[image, :, MAIN], preferred_element_type=F32)
            bias = norm[0, pl.ds(5 + image, 1)]
            for r in range(part):
                hidden[image, at + r] = (total[image, pixels(at + r), pl.ds(0, chans)] + bias).astype(BF16)
            return carry

        lax.fori_loop(0, 2, chunk, 0)

    for copies in borders:
        wait_borders(copies[4:])
    for step, image in enumerate(order):
        widen_image(own, top, bot, col, norm.at[0], image, wide, rem, True)
        main_inner(image)
        if step == 0:
            pieces.append(send_along_z(lora.at[1], lora_send.at[1], lora_recv.at[1]))
    for copies in borders:
        wait_borders(copies[:4])
    for image in order:
        widen_image(own, top, bot, col, norm.at[0], image, wide, rem, False)
        main_edges(image)
    pieces[1] = send_along_y(pieces[1], lora.at[1], lora_send.at[1], lora_recv.at[1])

    copy = relay(0)
    borders = []
    for step, image in enumerate(order):
        if step == 1:
            copy.wait()
        adapter(0, image)
        tail_dots(image)
        borders.append(start_borders(hidden, top2, bot2, col2, image, edge2_send, edge2_recv))
        mean, spread = local_stats(lambda r, image=image: hidden[image, r], rows)
        one2[0, pl.ds(image, 1)] = mean
        one2[0, pl.ds(2 + image, 1)] = spread

    first = start_exchange(one2, x_send.at[2], x_recv.at[2], first_peers())
    copy = relay(1)
    adapter(1, order[0])
    second = middle(first, one2, two2, 3)
    copy.wait()
    adapter(1, order[1])
    finish(second, two2, 1, 0)

    def final(image, window, at, rows_of):
        last = dots(window, tail.at[image], pl.ds(0, 128))
        small = last.astype(BF16)
        body = dots(window, kernels.at[1], MAIN)
        span = pixels(at, len(rows_of))
        total[image, span, MAIN] = body + jnp.dot(small, expand[image, :, MAIN], preferred_element_type=F32)
        total[image, span, REST] = last + jnp.dot(small, expand[image, :, REST], preferred_element_type=F32)
        for i, r in enumerate(rows_of):
            value = total[image, pixels(at + i), pl.ds(0, chans)]
            out[image, r] = (value + own[image, r].astype(F32)).astype(BF16)

    for copies in borders:
        wait_borders(copies[4:])
    for image in order:
        widen_image(hidden, top2, bot2, col2, norm.at[1], image, wide, rem, True)

        def chunk(c, carry, image=image):
            at = 1 + c * inner
            final(image, windows(wide, image, at, inner), at, [at + i for i in range(inner)])
            return carry

        lax.fori_loop(0, 2, chunk, 0)
    for copies in borders:
        wait_borders(copies[:4])
    for image in order:
        widen_image(hidden, top2, bot2, col2, norm.at[1], image, wide, rem, False)
        final(image, edge_windows(wide, image), 0, ends)


VM = pl.BlockSpec(memory_space=pltpu.VMEM)
HB = pl.BlockSpec(memory_space=pl.ANY)
SM = pl.BlockSpec(memory_space=pltpu.SMEM)
DMA = pltpu.SemaphoreType.DMA


def local(
    latents, timestep_embedding, embedding_weight, gain, shift, kernel_weight, reduce_library, expand_library,
    image_adapter, adapter_bank_row,
):
    images, rows, columns, chans = latents.shape
    pieces = Y * Z
    deep = UP_AT + 8
    map_of = (images, rows, columns, chans)
    line = pltpu.VMEM((images, columns, chans), BF16)
    edge = pltpu.VMEM((images, rows + 2, EDGE, chans), BF16)
    return pl.pallas_call(
        block_kernel,
        out_shape=jax.ShapeDtypeStruct(map_of, BF16),
        in_specs=[HB, VM, VM, SM, SM, VM, HB, VM, VM, HB],
        out_specs=VM,
        scratch_shapes=[
            pltpu.VMEM((images, rows, chans, columns), BF16),
            pltpu.VMEM((chans, embedding_weight.shape[0]), BF16),
            pltpu.VMEM((chans, chans), BF16),
            pltpu.VMEM(map_of, BF16),
            pltpu.VMEM(map_of, BF16),
            pltpu.VMEM((2, 3, 3 * chans, chans), BF16),
            pltpu.VMEM((images, rows + 2, columns, 3 * chans), BF16),
            pltpu.VMEM((images, rows * columns, 384), F32),
            pltpu.VMEM((2, 3, 3 * chans, 128), BF16),
            pltpu.VMEM((images, 3, 3 * chans, 128), BF16),
            pltpu.VMEM((images, 128, 384), BF16),
            pltpu.VMEM((9 * chans, 128), F32),
            pltpu.VMEM((pieces * 8, 128), F32),
            pltpu.VMEM((128, 128), F32),
            pltpu.VMEM((16, chans), F32),
            pltpu.VMEM((2, deep, 128), F32),
            pltpu.VMEM((8, 2, deep, 128), BF16),
            pltpu.VMEM((2, images, Y, Z, deep, 128), BF16),
            *([line, line, edge] * 2),
            pltpu.VMEM((2, 8, chans), F32),
            pltpu.VMEM((2 * Y, 4, chans), F32),
            pltpu.VMEM((Z, 4, chans), F32),
            pltpu.VMEM((2 * Y, 4, chans), F32),
            pltpu.VMEM((Z, 4, chans), F32),
            DMA((3,)),
            DMA((8,)),
            DMA((8,)),
            DMA((2, Z + Y)),
            DMA((2, Z + Y)),
            DMA((2,)),
            DMA((2,)),
            *([DMA((images, 5))] * 4),
            DMA((4, 8)),
            DMA((4, 8)),
        ],
        compiler_params=pltpu.CompilerParams(
            collective_id=0, has_side_effects=True, vmem_limit_bytes=56 * 2**20
        ),
        name="resnet_block",
    )(
        jnp.swapaxes(latents, 2, 3),
        reduce_library,
        expand_library,
        image_adapter.T,
        adapter_bank_row,
        timestep_embedding,
        embedding_weight.T,
        gain,
        shift,
        kernel_weight.reshape(2, 3, 3 * chans, chans),
    )


def solution(mesh):
    in_specs = (
        P("req", "patch", "owner", None),
        P("req", None),
        P(),
        P(),
        P(),
        P(),
        P(("req", "owner"), None, "patch"),
        P(("req", "owner"), None, "patch"),
        P("req", None),
        P(),
    )
    return jax.shard_map(
        local, mesh=mesh, in_specs=in_specs, out_specs=P("req", "patch", "owner", None), check_vma=False
    )
```

```python
import jax
import jax.numpy as jnp
from jax import lax
from jax.experimental import pallas as pl
from jax.experimental.pallas import tpu as pltpu
from jax.sharding import PartitionSpec as P

MESH = pl.DeviceIdType.MESH
F32, BF16 = jnp.float32, jnp.bfloat16
Y, Z = 4, 8
RANK = 64
EDGE = 16
GROUP = 10


def remote(src, dst, send, recv, device):
    return pltpu.make_async_remote_copy(
        src_ref=src, dst_ref=dst, send_sem=send, recv_sem=recv, device_id=device, device_id_type=MESH
    )


def place():
    patch, req, owner = lax.axis_index("patch"), lax.axis_index("req"), lax.axis_index("owner")
    return patch, req, owner, patch // Z, patch % Z


def greet():
    patch, req, owner, y, z = place()
    sem = pltpu.get_barrier_semaphore()
    count = 0

    def signal(device):
        pl.semaphore_signal(sem, inc=1, device_id=device, device_id_type=MESH)

    for dz in range(1, Z):
        signal((y * Z + (z + dz) % Z, req, owner))
        count += 1
    for dy in range(1, Y):
        signal(((y + dy) % Y * Z + z, req, owner))
        count += 1
    for k in range(1, 2 * Y, 2):
        g = (y * 2 + owner + k) % (2 * Y)
        signal(((g // 2) * Z + z, req, g % 2))
        count += 1
    for step in (1, Y * Z - 1):
        for other in (owner, 1 - owner):
            signal(((patch + step) % (Y * Z), req, other))
            count += 1
    for k in range(1, 8):
        g = (req * 2 + owner + k) % 8
        signal((patch, g // 2, g % 2))
        count += 1
    return lambda: pl.semaphore_wait(sem, count)


def start_borders(src, top, bot, col, image, send, recv):
    patch, req, owner, y, z = place()
    rows = src.shape[1]
    last = Y * Z - 1
    edge = pl.multiple_of((1 - owner) * (src.shape[2] - EDGE), EDGE)
    cols = pl.ds(edge, EDGE)

    def copy(at, block, target, device):
        return remote(block, target, send.at[image, at], recv.at[image, at], device)

    down, up = patch < last, patch > 0
    copies = [
        (down, up, copy(0, src.at[image, rows - 1], top.at[image], (patch + 1, req, owner))),
        (up, down, copy(1, src.at[image, 0], bot.at[image], (patch - 1, req, owner))),
        (down, up, copy(2, src.at[image, rows - 1, cols], col.at[image, 0], (patch + 1, req, 1 - owner))),
        (up, down, copy(3, src.at[image, 0, cols], col.at[image, rows + 1], (patch - 1, req, 1 - owner))),
        (None, None, copy(4, src.at[image, :, cols], col.at[image, pl.ds(1, rows)], (patch, req, 1 - owner))),
    ]
    for sends, _, item in copies:
        if sends is None:
            item.start()
        else:
            pl.when(sends)(item.start)
    return copies


def clear_borders(top, bot, col):
    patch = lax.axis_index("patch")
    end = col.shape[1] - 1

    @pl.when(patch == 0)
    def _():
        top[...] = jnp.zeros_like(top)
        col[:, 0] = jnp.zeros_like(col[:, 0])

    @pl.when(patch == Y * Z - 1)
    def _():
        bot[...] = jnp.zeros_like(bot)
        col[:, end] = jnp.zeros_like(col[:, end])


def wait_borders(copies):
    for sends, receives, copy in copies:
        if sends is None:
            copy.wait()
        else:
            pl.when(sends)(copy.wait_send)
            pl.when(receives)(copy.wait_recv)


def local_stats(rows_of, rows):
    def add(f):
        def step(r, total):
            x = f(rows_of(r).astype(F32))
            return total + jnp.sum(x.reshape(x.shape[0] // 8, 8, x.shape[1]), axis=0)

        return step

    chans = rows_of(0).shape[1]
    count = rows * rows_of(0).shape[0]
    zero = jnp.zeros((8, chans), F32)
    total = lax.fori_loop(0, rows, add(lambda x: x), zero)
    mean = jnp.sum(total, axis=0, keepdims=True) * (1.0 / count)
    spread = lax.fori_loop(0, rows, add(lambda x: (x - mean) * (x - mean)), zero)
    return mean, jnp.sum(spread, axis=0, keepdims=True)


def start_exchange(slots, send, recv, peers):
    copies = [
        remote(slots.at[0], slots.at[k], send.at[k], recv.at[k], peer) for k, peer in enumerate(peers, 1)
    ]
    for copy in copies:
        copy.start()
    return copies


def combine(slots, count):
    values = slots[...]
    half = values.shape[1] // 2
    total = jnp.sum(values, axis=0)
    mean = total * (1.0 / values.shape[0])
    off = values - mean[None]
    between = jnp.sum(off * off, axis=0)
    return mean[0:half], total[half:] + count * between[0:half]


def first_peers():
    patch, req, owner, y, z = place()
    peers = []
    for k in range(1, 2 * Y):
        g = (y * 2 + owner + k) % (2 * Y)
        peers.append(((g // 2) * Z + z, req, g % 2))
    return peers


def second_peers():
    patch, req, owner, y, z = place()
    return [(y * Z + (z + k) % Z, req, owner) for k in range(1, Z)]


def group_matrix(chans):
    row = lax.broadcasted_iota(jnp.int32, (chans, chans), 0)
    column = lax.broadcasted_iota(jnp.int32, (chans, chans), 1)
    return jnp.where((row * 6554) >> 16 == (column * 6554) >> 16, 1.0, 0.0).astype(BF16)


def group_mean(values, groups):
    count = values.shape[0]
    values = jnp.concatenate([values] * (8 // count), axis=0)
    high = values.astype(BF16).astype(F32)
    rest = values - high
    middle = rest.astype(BF16).astype(F32)
    parts = jnp.concatenate([high, middle, rest - middle], axis=0).astype(BF16)
    total = jnp.dot(parts, groups, preferred_element_type=F32)
    return (total[0:count] + total[8 : 8 + count] + total[16 : 16 + count]) * (1.0 / GROUP)


def finish_norm(mean, spread, count, gain, shift, groups):
    center = group_mean(mean, groups)
    off = mean - center
    var = group_mean(spread * (1.0 / count) + off * off, groups)
    scale = gain / jnp.sqrt(var + 1e-05)
    return center, 0.5 * scale, 0.5 * shift


def lay_piece(reduce_row, expand_row, piece):
    down = reduce_row[0].astype(F32)
    up = expand_row[0].astype(F32)
    piece[...] = jnp.zeros_like(piece)
    for i in range(down.shape[1] // 128):
        piece[:, i, :] = down[:, i * 128 : i * 128 + 128]
    for i in range(up.shape[1] // 128):
        piece[:, UP_AT + i, :] = up[:, i * 128 : i * 128 + 128]
    return piece[...].astype(BF16)


def send_along_z(lora, send, recv):
    patch, req, owner, y, z = place()
    block = lora.at[owner, y, z]
    copies = [
        remote(block, block, send.at[k], recv.at[k], (y * Z + (z + k) % Z, req, owner)) for k in range(1, Z)
    ]
    for copy in copies:
        copy.start()
    return copies


def send_along_y(copies, lora, send, recv):
    patch, req, owner, y, z = place()
    for copy in copies:
        copy.wait()
    block = lora.at[owner, y]
    copies = [
        remote(block, block, send.at[Z + k], recv.at[Z + k], ((y + k) % Y * Z + z, req, owner)) for k in (1, Y - 1)
    ]
    for copy in copies:
        copy.start()
    return copies


def forward_along_y(copies, lora, send, recv):
    patch, req, owner, y, z = place()
    for copy in copies:
        copy.wait()
    half = Z // 2
    copies = []
    for at, k, step in ((0, 1, 0), (Z + 2, Y - 1, half)):
        block = lora.at[owner, (y + Y - k) % Y, pl.ds(step, half)]
        copies.append(remote(block, block, send.at[at], recv.at[at], ((y + k) % Y * Z + z, req, owner)))
        copies[-1].start()
    return copies


def lay_adapter(lora, image, base, tail, expand, flat, ups, wide_up):
    pieces = Y * Z
    depth = tail.shape[1] * 3 // pieces
    half = depth // 2

    def lay(p, carry):
        value = lora[image, p // Z, p % Z].astype(F32)
        down = value[0:half]
        flat[pl.ds(p * depth, half, 2)] = pltpu.roll(down, 64, 1)
        flat[pl.ds(p * depth + 1, half, 2)] = down
        ups[pl.ds(pl.multiple_of(p * 8, 8), 8)] = value[UP_AT : UP_AT + 8]
        return carry

    lax.fori_loop(0, pieces, lay, 0, unroll=8)
    lane = lax.broadcasted_iota(jnp.int32, base.shape[1:], 1)
    for d in range(3):
        down = flat[pl.ds(d * base.shape[1], base.shape[1])]
        tail[d] = jnp.where(lane >= 64, down, base[d].astype(F32)).astype(BF16)
    line = [ups[pl.ds(k, pieces, 8)] for k in range(5)]
    turned = [pltpu.roll(v, 64, 1) for v in line]
    low = lax.broadcasted_iota(jnp.int32, line[0].shape, 1) < 64
    even = line[0:3]
    odd = [jnp.where(low, turned[2], turned[3]), jnp.where(low, turned[3], turned[4]), turned[4]]
    for b in range(3):
        wide_up[pl.ds(0, 64)] = jnp.zeros((64, 128), F32)
        wide_up[pl.ds(64, pieces, 2)] = even[b]
        wide_up[pl.ds(65, pieces, 2)] = odd[b]
        expand[:, pl.ds(b * 128, 128)] = wide_up[...].astype(BF16)


def widen_image(source, top, bot, col, norm, image, wide, rem, inner):
    patch, req, owner, y, z = place()
    rows, columns = source.shape[1:3]
    last = Y * Z - 1
    index = lax.broadcasted_iota(jnp.int32, (columns, 1), 0)
    center = norm[pl.ds(image, 1)]
    scale = norm[pl.ds(2 + image, 1)]
    offset = norm[pl.ds(4, 1)]

    def activate(x):
        h = (x.astype(F32) - center) * scale + offset
        return h + h * jnp.tanh(h)

    def border(at):
        return activate(
            jnp.where(owner == 0, col[image, at, 0, :].astype(F32), col[image, at, EDGE - 1, :].astype(F32))
        )

    def lay(r, act, edge):
        left = jnp.where(index == 0, jnp.where(owner == 1, edge, 0.0), pltpu.roll(act, 1, 0))
        right = jnp.where(
            index == columns - 1, jnp.where(owner == 0, edge, 0.0), pltpu.roll(act, columns - 1, 0)
        )
        wide[image, r] = jnp.concatenate([left, act, right], axis=1).astype(BF16)

    if inner:
        rem[pl.ds(0, rows)] = border(slice(1, rows + 1))

        def row(r, carry):
            lay(r + 1, activate(source[image, r]), rem[pl.ds(r, 1)])
            return carry

        lax.fori_loop(0, rows, row, 0, unroll=2)
    else:
        for r, block, inside in ((0, top, patch > 0), (rows + 1, bot, patch < last)):
            edge = jnp.where(inside, border(slice(r, r + 1)), 0.0)
            lay(r, jnp.where(inside, activate(block[image]), 0.0), edge)


def windows(wide, image, at, part):
    columns, depth = wide.shape[2:]
    return [wide[image, pl.ds(at + d, part)].reshape(part * columns, depth) for d in range(3)]


def edge_windows(wide, image):
    last = wide.shape[1] - 3
    return [jnp.concatenate([wide[image, d], wide[image, last + d]], axis=0) for d in range(3)]


def dots(window, matrix, lanes):
    return sum(jnp.dot(window[d], matrix[d, :, lanes], preferred_element_type=F32) for d in range(3))


MAIN, REST = pl.ds(0, 256), pl.ds(256, 128)
UP_AT = 48


def block_kernel(
    raw, reduce_row, expand_row, image_adapter, bank_row, embedding, weight_hbm, gain, shift, kernels_hbm,
    out,
    raw_own, weight, groups, own, hidden, kernels, wide, total, base, tail, expand, flat, ups, wide_up, rem,
    piece, held, lora, top, bot, col, top2, bot2, col2, norm, one, two, one2, two2,
    local_sem, bank_send, bank_recv, lora_send, lora_recv, relay_send, relay_recv,
    edge_send, edge_recv, edge2_send, edge2_recv, x_send, x_recv,
):
    patch, req, owner, y, z = place()
    images, rows, columns, chans = own.shape
    count = rows * columns
    fetch = pltpu.make_async_copy(raw, raw_own, local_sem.at[0])
    fetch.start()
    fetch_kernels = pltpu.make_async_copy(kernels_hbm, kernels, local_sem.at[1])
    fetch_kernels.start()
    fetch_weight = pltpu.make_async_copy(weight_hbm, weight, local_sem.at[2])
    fetch_weight.start()
    arrived = greet()
    me = req * 2 + owner
    held[me] = lay_piece(reduce_row, expand_row, piece)
    clear_borders(top, bot, col)
    clear_borders(top2, bot2, col2)
    groups[...] = group_matrix(chans)
    fetch.wait()

    def turn(t, carry):
        image, r = t // rows, t % rows
        own[image, r] = jnp.transpose(raw_own[image, r].astype(F32)).astype(BF16)
        return carry

    lax.fori_loop(0, images * rows, turn, 0, unroll=4)

    for image in range(images):
        mean, spread = local_stats(lambda r, image=image: own[image, r], rows)
        one[0, pl.ds(image, 1)] = mean
        one[0, pl.ds(2 + image, 1)] = spread
    arrived()

    first = start_exchange(one, x_send.at[0], x_recv.at[0], first_peers())
    bank = []
    for k in range(1, 8):
        g = (me + k) % 8
        copy = remote(held.at[me], held.at[me], bank_send.at[k], bank_recv.at[k], (patch, g // 2, g % 2))
        copy.start()
        bank.append(copy)

    fetch_weight.wait()
    u = embedding[...].astype(F32)
    temb = (u / (1.0 + jnp.exp(-u))).astype(BF16)
    proj = lax.dot_general(temb, weight[...], (((1,), (1,)), ((), ())), preferred_element_type=F32)
    norm[0, pl.ds(5, 2)] = proj
    fetch_kernels.wait()

    def middle(first, one, two, at):
        for copy in first:
            copy.wait()
        mean, spread = combine(one, float(count))
        half = mean.shape[0]
        two[0, pl.ds(0, half)] = mean
        two[0, pl.ds(half, half)] = spread
        return start_exchange(two, x_send.at[at], x_recv.at[at], second_peers())

    def finish(second, two, which, image):
        for copy in second:
            copy.wait()
        mean, spread = combine(two, float(count * 2 * Y))
        half = mean.shape[0]
        center, scale, offset = finish_norm(
            mean, spread, float(count * 2 * Y * Z), gain[pl.ds(which, 1)], shift[pl.ds(which, 1)], groups[...]
        )
        norm[which, pl.ds(image, half)] = center
        norm[which, pl.ds(2 + image, half)] = scale
        norm[which, pl.ds(4, 1)] = offset

    second = middle(first, one, two, 1)
    for copy in bank:
        copy.wait()
    chosen = held[bank_row[image_adapter[0, owner]]]
    lora[0, owner, y, z] = chosen[0]
    lora[1, owner, y, z] = chosen[1]
    pieces = [send_along_z(lora.at[0], lora_send.at[0], lora_recv.at[0])]
    borders = [start_borders(own, top, bot, col, i, edge_send, edge_recv) for i in range(images)]
    for which in range(2):
        for d in range(3):
            last = kernels[which, d, :, pl.ds(256, chans - 256)].astype(F32)
            base[which, d] = jnp.concatenate([last, jnp.zeros_like(last)], axis=1).astype(BF16)
    finish(second, two, 0, 0)
    pieces[0] = send_along_y(pieces[0], lora.at[0], lora_send.at[0], lora_recv.at[0])

    order = (owner, 1 - owner)
    inner = (rows - 2) // 2
    ends = (0, rows - 1)

    def pixels(r, count=1):
        return pl.ds(pl.multiple_of(r * columns, columns), count * columns)

    def main_inner(image):
        def chunk(c, carry):
            at = 1 + c * inner
            total[image, pixels(at, inner), MAIN] = dots(windows(wide, image, at, inner), kernels.at[0], MAIN)
            return carry

        lax.fori_loop(0, 2, chunk, 0)

    def main_edges(image):
        value = dots(edge_windows(wide, image), kernels.at[0], MAIN)
        for i, r in enumerate(ends):
            total[image, pixels(r), MAIN] = value[i * columns : (i + 1) * columns]

    def relay(which):
        for copy in pieces[which]:
            copy.wait()
        block = lora.at[which, owner]
        copy = remote(block, block, relay_send.at[which], relay_recv.at[which], (patch, req, 1 - owner))
        copy.start()
        return copy

    def adapter(which, image):
        lay_adapter(
            lora.at[which], image, base.at[which], tail.at[image], expand.at[image], flat, ups, wide_up
        )

    def tail_dots(image):
        part = rows // 2

        def chunk(c, carry):
            at = c * part
            last = dots(windows(wide, image, at, part), tail.at[image], pl.ds(0, 128))
            small = last.astype(BF16)
            span = pixels(at, part)
            total[image, span, REST] = last + jnp.dot(small, expand[image, :, REST], preferred_element_type=F32)
            total[image, span, MAIN] += jnp.dot(small, expand[image, :, MAIN], preferred_element_type=F32)
            bias = norm[0, pl.ds(5 + image, 1)]
            for r in range(part):
                hidden[image, at + r] = (total[image, pixels(at + r), pl.ds(0, chans)] + bias).astype(BF16)
            return carry

        lax.fori_loop(0, 2, chunk, 0)

    for copies in borders:
        wait_borders(copies[4:])
    for step, image in enumerate(order):
        widen_image(own, top, bot, col, norm.at[0], image, wide, rem, True)
        main_inner(image)
        if step == 0:
            pieces[0] = forward_along_y(pieces[0], lora.at[0], lora_send.at[0], lora_recv.at[0])
            pieces.append(send_along_z(lora.at[1], lora_send.at[1], lora_recv.at[1]))
    for copies in borders:
        wait_borders(copies[:4])
    for image in order:
        widen_image(own, top, bot, col, norm.at[0], image, wide, rem, False)
        main_edges(image)
    pieces[1] = send_along_y(pieces[1], lora.at[1], lora_send.at[1], lora_recv.at[1])

    copy = relay(0)
    borders = []
    for step, image in enumerate(order):
        if step == 1:
            copy.wait()
        adapter(0, image)
        tail_dots(image)
        if step == 0:
            pieces[1] = forward_along_y(pieces[1], lora.at[1], lora_send.at[1], lora_recv.at[1])
        borders.append(start_borders(hidden, top2, bot2, col2, image, edge2_send, edge2_recv))
        mean, spread = local_stats(lambda r, image=image: hidden[image, r], rows)
        one2[0, pl.ds(image, 1)] = mean
        one2[0, pl.ds(2 + image, 1)] = spread

    first = start_exchange(one2, x_send.at[2], x_recv.at[2], first_peers())
    copy = relay(1)
    adapter(1, order[0])
    second = middle(first, one2, two2, 3)
    copy.wait()
    adapter(1, order[1])
    finish(second, two2, 1, 0)

    def final(image, window, at, rows_of):
        last = dots(window, tail.at[image], pl.ds(0, 128))
        small = last.astype(BF16)
        body = dots(window, kernels.at[1], MAIN)
        span = pixels(at, len(rows_of))
        total[image, span, MAIN] = body + jnp.dot(small, expand[image, :, MAIN], preferred_element_type=F32)
        total[image, span, REST] = last + jnp.dot(small, expand[image, :, REST], preferred_element_type=F32)
        for i, r in enumerate(rows_of):
            value = total[image, pixels(at + i), pl.ds(0, chans)]
            out[image, r] = (value + own[image, r].astype(F32)).astype(BF16)

    for copies in borders:
        wait_borders(copies[4:])
    for image in order:
        widen_image(hidden, top2, bot2, col2, norm.at[1], image, wide, rem, True)

        def chunk(c, carry, image=image):
            at = 1 + c * inner
            final(image, windows(wide, image, at, inner), at, [at + i for i in range(inner)])
            return carry

        lax.fori_loop(0, 2, chunk, 0)
    for copies in borders:
        wait_borders(copies[:4])
    for image in order:
        widen_image(hidden, top2, bot2, col2, norm.at[1], image, wide, rem, False)
        final(image, edge_windows(wide, image), 0, ends)


VM = pl.BlockSpec(memory_space=pltpu.VMEM)
HB = pl.BlockSpec(memory_space=pl.ANY)
SM = pl.BlockSpec(memory_space=pltpu.SMEM)
DMA = pltpu.SemaphoreType.DMA


def local(
    latents, timestep_embedding, embedding_weight, gain, shift, kernel_weight, reduce_library, expand_library,
    image_adapter, adapter_bank_row,
):
    images, rows, columns, chans = latents.shape
    pieces = Y * Z
    deep = UP_AT + 8
    map_of = (images, rows, columns, chans)
    line = pltpu.VMEM((images, columns, chans), BF16)
    edge = pltpu.VMEM((images, rows + 2, EDGE, chans), BF16)
    return pl.pallas_call(
        block_kernel,
        out_shape=jax.ShapeDtypeStruct(map_of, BF16),
        in_specs=[HB, VM, VM, SM, SM, VM, HB, VM, VM, HB],
        out_specs=VM,
        scratch_shapes=[
            pltpu.VMEM((images, rows, chans, columns), BF16),
            pltpu.VMEM((chans, embedding_weight.shape[0]), BF16),
            pltpu.VMEM((chans, chans), BF16),
            pltpu.VMEM(map_of, BF16),
            pltpu.VMEM(map_of, BF16),
            pltpu.VMEM((2, 3, 3 * chans, chans), BF16),
            pltpu.VMEM((images, rows + 2, columns, 3 * chans), BF16),
            pltpu.VMEM((images, rows * columns, 384), F32),
            pltpu.VMEM((2, 3, 3 * chans, 128), BF16),
            pltpu.VMEM((images, 3, 3 * chans, 128), BF16),
            pltpu.VMEM((images, 128, 384), BF16),
            pltpu.VMEM((9 * chans, 128), F32),
            pltpu.VMEM((pieces * 8, 128), F32),
            pltpu.VMEM((128, 128), F32),
            pltpu.VMEM((16, chans), F32),
            pltpu.VMEM((2, deep, 128), F32),
            pltpu.VMEM((8, 2, deep, 128), BF16),
            pltpu.VMEM((2, images, Y, Z, deep, 128), BF16),
            *([line, line, edge] * 2),
            pltpu.VMEM((2, 8, chans), F32),
            pltpu.VMEM((2 * Y, 4, chans), F32),
            pltpu.VMEM((Z, 4, chans), F32),
            pltpu.VMEM((2 * Y, 4, chans), F32),
            pltpu.VMEM((Z, 4, chans), F32),
            DMA((3,)),
            DMA((8,)),
            DMA((8,)),
            DMA((2, Z + Y)),
            DMA((2, Z + Y)),
            DMA((2,)),
            DMA((2,)),
            *([DMA((images, 5))] * 4),
            DMA((4, 8)),
            DMA((4, 8)),
        ],
        compiler_params=pltpu.CompilerParams(
            collective_id=0, has_side_effects=True, vmem_limit_bytes=56 * 2**20
        ),
        name="resnet_block",
    )(
        jnp.swapaxes(latents, 2, 3),
        reduce_library,
        expand_library,
        image_adapter.T,
        adapter_bank_row,
        timestep_embedding,
        embedding_weight.T,
        gain,
        shift,
        kernel_weight.reshape(2, 3, 3 * chans, chans),
    )


def solution(mesh):
    in_specs = (
        P("req", "patch", "owner", None),
        P("req", None),
        P(),
        P(),
        P(),
        P(),
        P(("req", "owner"), None, "patch"),
        P(("req", "owner"), None, "patch"),
        P("req", None),
        P(),
    )
    return jax.shard_map(
        local, mesh=mesh, in_specs=in_specs, out_specs=P("req", "patch", "owner", None), check_vma=False
    )
```

```python
import jax
import jax.numpy as jnp
from jax import lax
from jax.experimental import pallas as pl
from jax.experimental.pallas import tpu as pltpu
from jax.sharding import PartitionSpec as P

MESH = pl.DeviceIdType.MESH
F32, BF16 = jnp.float32, jnp.bfloat16
Y, Z = 4, 8
RANK = 64
EDGE = 16
GROUP = 10


def remote(src, dst, send, recv, device):
    return pltpu.make_async_remote_copy(
        src_ref=src, dst_ref=dst, send_sem=send, recv_sem=recv, device_id=device, device_id_type=MESH
    )


def place():
    patch, req, owner = lax.axis_index("patch"), lax.axis_index("req"), lax.axis_index("owner")
    return patch, req, owner, patch // Z, patch % Z


def greet():
    patch, req, owner, y, z = place()
    sem = pltpu.get_barrier_semaphore()
    count = 0

    def signal(device):
        pl.semaphore_signal(sem, inc=1, device_id=device, device_id_type=MESH)

    for dz in range(1, Z):
        signal((y * Z + (z + dz) % Z, req, owner))
        count += 1
    for dy in range(1, Y):
        signal(((y + dy) % Y * Z + z, req, owner))
        count += 1
    for k in range(1, 2 * Y, 2):
        g = (y * 2 + owner + k) % (2 * Y)
        signal(((g // 2) * Z + z, req, g % 2))
        count += 1
    for step in (1, Y * Z - 1):
        for other in (owner, 1 - owner):
            signal(((patch + step) % (Y * Z), req, other))
            count += 1
    for k in range(1, 8):
        g = (req * 2 + owner + k) % 8
        signal((patch, g // 2, g % 2))
        count += 1
    return lambda: pl.semaphore_wait(sem, count)


def start_borders(src, top, bot, col, image, send, recv):
    patch, req, owner, y, z = place()
    rows = src.shape[1]
    last = Y * Z - 1
    edge = pl.multiple_of((1 - owner) * (src.shape[2] - EDGE), EDGE)
    cols = pl.ds(edge, EDGE)

    def copy(at, block, target, device):
        return remote(block, target, send.at[image, at], recv.at[image, at], device)

    down, up = patch < last, patch > 0
    copies = [
        (down, up, copy(0, src.at[image, rows - 1], top.at[image], (patch + 1, req, owner))),
        (up, down, copy(1, src.at[image, 0], bot.at[image], (patch - 1, req, owner))),
        (down, up, copy(2, src.at[image, rows - 1, cols], col.at[image, 0], (patch + 1, req, 1 - owner))),
        (up, down, copy(3, src.at[image, 0, cols], col.at[image, rows + 1], (patch - 1, req, 1 - owner))),
        (None, None, copy(4, src.at[image, :, cols], col.at[image, pl.ds(1, rows)], (patch, req, 1 - owner))),
    ]
    for sends, _, item in copies:
        if sends is None:
            item.start()
        else:
            pl.when(sends)(item.start)
    return copies


def clear_borders(top, bot, col):
    patch = lax.axis_index("patch")
    end = col.shape[1] - 1

    @pl.when(patch == 0)
    def _():
        top[...] = jnp.zeros_like(top)
        col[:, 0] = jnp.zeros_like(col[:, 0])

    @pl.when(patch == Y * Z - 1)
    def _():
        bot[...] = jnp.zeros_like(bot)
        col[:, end] = jnp.zeros_like(col[:, end])


def wait_borders(copies):
    for sends, receives, copy in copies:
        if sends is None:
            copy.wait()
        else:
            pl.when(sends)(copy.wait_send)
            pl.when(receives)(copy.wait_recv)


def local_stats(rows_of, rows):
    def add(f):
        def step(r, total):
            x = f(rows_of(r).astype(F32))
            return total + jnp.sum(x.reshape(x.shape[0] // 8, 8, x.shape[1]), axis=0)

        return step

    chans = rows_of(0).shape[1]
    count = rows * rows_of(0).shape[0]
    zero = jnp.zeros((8, chans), F32)
    total = lax.fori_loop(0, rows, add(lambda x: x), zero)
    mean = jnp.sum(total, axis=0, keepdims=True) * (1.0 / count)
    spread = lax.fori_loop(0, rows, add(lambda x: (x - mean) * (x - mean)), zero)
    return mean, jnp.sum(spread, axis=0, keepdims=True)


def start_exchange(slots, send, recv, peers):
    copies = [
        remote(slots.at[0], slots.at[k], send.at[k], recv.at[k], peer) for k, peer in enumerate(peers, 1)
    ]
    for copy in copies:
        copy.start()
    return copies


def combine(slots, count):
    values = slots[...]
    half = values.shape[1] // 2
    total = jnp.sum(values, axis=0)
    mean = total * (1.0 / values.shape[0])
    off = values - mean[None]
    between = jnp.sum(off * off, axis=0)
    return mean[0:half], total[half:] + count * between[0:half]


def first_peers():
    patch, req, owner, y, z = place()
    peers = []
    for k in range(1, 2 * Y):
        g = (y * 2 + owner + k) % (2 * Y)
        peers.append(((g // 2) * Z + z, req, g % 2))
    return peers


def second_peers():
    patch, req, owner, y, z = place()
    return [(y * Z + (z + k) % Z, req, owner) for k in range(1, Z)]


def group_matrix(chans):
    row = lax.broadcasted_iota(jnp.int32, (chans, chans), 0)
    column = lax.broadcasted_iota(jnp.int32, (chans, chans), 1)
    return jnp.where((row * 6554) >> 16 == (column * 6554) >> 16, 1.0, 0.0).astype(BF16)


def group_mean(values, groups):
    count = values.shape[0]
    values = jnp.concatenate([values] * (8 // count), axis=0)
    high = values.astype(BF16).astype(F32)
    rest = values - high
    middle = rest.astype(BF16).astype(F32)
    parts = jnp.concatenate([high, middle, rest - middle], axis=0).astype(BF16)
    total = jnp.dot(parts, groups, preferred_element_type=F32)
    return (total[0:count] + total[8 : 8 + count] + total[16 : 16 + count]) * (1.0 / GROUP)


def finish_norm(mean, spread, count, gain, shift, groups):
    center = group_mean(mean, groups)
    off = mean - center
    var = group_mean(spread * (1.0 / count) + off * off, groups)
    scale = gain / jnp.sqrt(var + 1e-05)
    return center, 0.5 * scale, 0.5 * shift


def lay_piece(reduce_row, expand_row, piece):
    down = reduce_row[0].astype(F32)
    up = expand_row[0].astype(F32)
    piece[...] = jnp.zeros_like(piece)
    for i in range(down.shape[1] // 128):
        piece[:, i, :] = down[:, i * 128 : i * 128 + 128]
    for i in range(up.shape[1] // 128):
        piece[:, UP_AT + i, :] = up[:, i * 128 : i * 128 + 128]
    return piece[...].astype(BF16)


def send_along_z(lora, send, recv):
    patch, req, owner, y, z = place()
    block = lora.at[owner, y, z]
    copies = [
        remote(block, block, send.at[k], recv.at[k], (y * Z + (z + k) % Z, req, owner)) for k in range(1, Z)
    ]
    for copy in copies:
        copy.start()
    return copies


def send_along_y(copies, lora, send, recv):
    patch, req, owner, y, z = place()
    for copy in copies:
        copy.wait()
    block = lora.at[owner, y]
    copies = [
        remote(block, block, send.at[Z + k], recv.at[Z + k], ((y + k) % Y * Z + z, req, owner)) for k in (1, Y - 1)
    ]
    for copy in copies:
        copy.start()
    return copies


def forward_along_y(copies, lora, send, recv):
    patch, req, owner, y, z = place()
    for copy in copies:
        copy.wait()
    half = Z // 2
    copies = []
    for at, k, step in ((0, 1, 0), (Z + 2, Y - 1, half)):
        block = lora.at[owner, (y + Y - k) % Y, pl.ds(step, half)]
        copies.append(remote(block, block, send.at[at], recv.at[at], ((y + k) % Y * Z + z, req, owner)))
        copies[-1].start()
    return copies


def lay_adapter(lora, image, base, tail, expand, flat, ups, wide_up):
    pieces = Y * Z
    depth = tail.shape[1] * 3 // pieces
    half = depth // 2

    def lay(p, carry):
        value = lora[image, p // Z, p % Z].astype(F32)
        down = value[0:half]
        flat[pl.ds(p * depth, half, 2)] = pltpu.roll(down, 64, 1)
        flat[pl.ds(p * depth + 1, half, 2)] = down
        ups[pl.ds(pl.multiple_of(p * 8, 8), 8)] = value[UP_AT : UP_AT + 8]
        return carry

    lax.fori_loop(0, pieces, lay, 0, unroll=8)
    lane = lax.broadcasted_iota(jnp.int32, base.shape[1:], 1)
    for d in range(3):
        down = flat[pl.ds(d * base.shape[1], base.shape[1])]
        tail[d] = jnp.where(lane >= 64, down, base[d].astype(F32)).astype(BF16)
    line = [ups[pl.ds(k, pieces, 8)] for k in range(5)]
    turned = [pltpu.roll(v, 64, 1) for v in line]
    low = lax.broadcasted_iota(jnp.int32, line[0].shape, 1) < 64
    even = line[0:3]
    odd = [jnp.where(low, turned[2], turned[3]), jnp.where(low, turned[3], turned[4]), turned[4]]
    for b in range(3):
        wide_up[pl.ds(0, 64)] = jnp.zeros((64, 128), F32)
        wide_up[pl.ds(64, pieces, 2)] = even[b]
        wide_up[pl.ds(65, pieces, 2)] = odd[b]
        expand[:, pl.ds(b * 128, 128)] = wide_up[...].astype(BF16)


def widen_image(source, top, bot, col, norm, image, wide, rem, inner):
    patch, req, owner, y, z = place()
    rows, columns = source.shape[1:3]
    last = Y * Z - 1
    index = lax.broadcasted_iota(jnp.int32, (columns, 1), 0)
    center = norm[pl.ds(image, 1)]
    scale = norm[pl.ds(2 + image, 1)]
    offset = norm[pl.ds(4, 1)]

    def activate(x):
        h = (x.astype(F32) - center) * scale + offset
        return h + h * jnp.tanh(h)

    def border(at):
        return activate(
            jnp.where(owner == 0, col[image, at, 0, :].astype(F32), col[image, at, EDGE - 1, :].astype(F32))
        )

    def lay(r, act, edge):
        left = jnp.where(index == 0, jnp.where(owner == 1, edge, 0.0), pltpu.roll(act, 1, 0))
        right = jnp.where(
            index == columns - 1, jnp.where(owner == 0, edge, 0.0), pltpu.roll(act, columns - 1, 0)
        )
        wide[image, r] = jnp.concatenate([left, act, right], axis=1).astype(BF16)

    if inner:
        rem[pl.ds(0, rows)] = border(slice(1, rows + 1))

        def row(r, carry):
            lay(r + 1, activate(source[image, r]), rem[pl.ds(r, 1)])
            return carry

        lax.fori_loop(0, rows, row, 0, unroll=2)
    else:
        for r, block, inside in ((0, top, patch > 0), (rows + 1, bot, patch < last)):
            edge = jnp.where(inside, border(slice(r, r + 1)), 0.0)
            lay(r, jnp.where(inside, activate(block[image]), 0.0), edge)


def windows(wide, image, at, part):
    columns, depth = wide.shape[2:]
    return [wide[image, pl.ds(at + d, part)].reshape(part * columns, depth) for d in range(3)]


def edge_windows(wide, image):
    last = wide.shape[1] - 3
    return [jnp.concatenate([wide[image, d], wide[image, last + d]], axis=0) for d in range(3)]


def dots(window, matrix, lanes):
    return sum(jnp.dot(window[d], matrix[d, :, lanes], preferred_element_type=F32) for d in range(3))


MAIN, REST = pl.ds(0, 256), pl.ds(256, 128)
UP_AT = 48


def block_kernel(
    raw, reduce_row, expand_row, image_adapter, bank_row, embedding, weight_hbm, gain, shift, kernels_hbm,
    out,
    raw_own, result, weight, groups, own, hidden, kernels, wide, total, base, tail, expand, flat, ups, wide_up, rem,
    piece, held, lora, top, bot, col, top2, bot2, col2, norm, one, two, one2, two2,
    local_sem, out_sem, bank_send, bank_recv, lora_send, lora_recv, relay_send, relay_recv,
    edge_send, edge_recv, edge2_send, edge2_recv, x_send, x_recv,
):
    patch, req, owner, y, z = place()
    images, rows, columns, chans = own.shape
    count = rows * columns
    fetch = pltpu.make_async_copy(raw, raw_own, local_sem.at[0])
    fetch.start()
    fetch_kernels = pltpu.make_async_copy(kernels_hbm, kernels, local_sem.at[1])
    fetch_kernels.start()
    fetch_weight = pltpu.make_async_copy(weight_hbm, weight, local_sem.at[2])
    fetch_weight.start()
    arrived = greet()
    me = req * 2 + owner
    held[me] = lay_piece(reduce_row, expand_row, piece)
    clear_borders(top, bot, col)
    clear_borders(top2, bot2, col2)
    groups[...] = group_matrix(chans)
    fetch.wait()

    def turn(t, carry):
        image, r = t // rows, t % rows
        own[image, r] = jnp.transpose(raw_own[image, r].astype(F32)).astype(BF16)
        return carry

    lax.fori_loop(0, images * rows, turn, 0, unroll=4)

    for image in range(images):
        mean, spread = local_stats(lambda r, image=image: own[image, r], rows)
        one[0, pl.ds(image, 1)] = mean
        one[0, pl.ds(2 + image, 1)] = spread
    arrived()

    first = start_exchange(one, x_send.at[0], x_recv.at[0], first_peers())
    bank = []
    for k in range(1, 8):
        g = (me + k) % 8
        copy = remote(held.at[me], held.at[me], bank_send.at[k], bank_recv.at[k], (patch, g // 2, g % 2))
        copy.start()
        bank.append(copy)

    fetch_weight.wait()
    u = embedding[...].astype(F32)
    temb = (u / (1.0 + jnp.exp(-u))).astype(BF16)
    proj = lax.dot_general(temb, weight[...], (((1,), (1,)), ((), ())), preferred_element_type=F32)
    norm[0, pl.ds(5, 2)] = proj
    fetch_kernels.wait()

    def middle(first, one, two, at):
        for copy in first:
            copy.wait()
        mean, spread = combine(one, float(count))
        half = mean.shape[0]
        two[0, pl.ds(0, half)] = mean
        two[0, pl.ds(half, half)] = spread
        return start_exchange(two, x_send.at[at], x_recv.at[at], second_peers())

    def finish(second, two, which, image):
        for copy in second:
            copy.wait()
        mean, spread = combine(two, float(count * 2 * Y))
        half = mean.shape[0]
        center, scale, offset = finish_norm(
            mean, spread, float(count * 2 * Y * Z), gain[pl.ds(which, 1)], shift[pl.ds(which, 1)], groups[...]
        )
        norm[which, pl.ds(image, half)] = center
        norm[which, pl.ds(2 + image, half)] = scale
        norm[which, pl.ds(4, 1)] = offset

    second = middle(first, one, two, 1)
    for copy in bank:
        copy.wait()
    chosen = held[bank_row[image_adapter[0, owner]]]
    lora[0, owner, y, z] = chosen[0]
    lora[1, owner, y, z] = chosen[1]
    pieces = [send_along_z(lora.at[0], lora_send.at[0], lora_recv.at[0])]
    borders = [start_borders(own, top, bot, col, i, edge_send, edge_recv) for i in range(images)]
    for which in range(2):
        for d in range(3):
            last = kernels[which, d, :, pl.ds(256, chans - 256)].astype(F32)
            base[which, d] = jnp.concatenate([last, jnp.zeros_like(last)], axis=1).astype(BF16)
    finish(second, two, 0, 0)
    pieces[0] = send_along_y(pieces[0], lora.at[0], lora_send.at[0], lora_recv.at[0])

    order = (owner, 1 - owner)
    inner = (rows - 2) // 2
    ends = (0, rows - 1)

    def pixels(r, count=1):
        return pl.ds(pl.multiple_of(r * columns, columns), count * columns)

    def main_inner(image):
        def chunk(c, carry):
            at = 1 + c * inner
            total[image, pixels(at, inner), MAIN] = dots(windows(wide, image, at, inner), kernels.at[0], MAIN)
            return carry

        lax.fori_loop(0, 2, chunk, 0)

    def main_edges(image):
        value = dots(edge_windows(wide, image), kernels.at[0], MAIN)
        for i, r in enumerate(ends):
            total[image, pixels(r), MAIN] = value[i * columns : (i + 1) * columns]

    def relay(which):
        for copy in pieces[which]:
            copy.wait()
        block = lora.at[which, owner]
        copy = remote(block, block, relay_send.at[which], relay_recv.at[which], (patch, req, 1 - owner))
        copy.start()
        return copy

    def adapter(which, image):
        lay_adapter(
            lora.at[which], image, base.at[which], tail.at[image], expand.at[image], flat, ups, wide_up
        )

    def tail_dots(image):
        part = rows // 2

        def chunk(c, carry):
            at = c * part
            last = dots(windows(wide, image, at, part), tail.at[image], pl.ds(0, 128))
            small = last.astype(BF16)
            span = pixels(at, part)
            total[image, span, REST] = last + jnp.dot(small, expand[image, :, REST], preferred_element_type=F32)
            total[image, span, MAIN] += jnp.dot(small, expand[image, :, MAIN], preferred_element_type=F32)
            bias = norm[0, pl.ds(5 + image, 1)]
            for r in range(part):
                hidden[image, at + r] = (total[image, pixels(at + r), pl.ds(0, chans)] + bias).astype(BF16)
            return carry

        lax.fori_loop(0, 2, chunk, 0)

    for copies in borders:
        wait_borders(copies[4:])
    for step, image in enumerate(order):
        widen_image(own, top, bot, col, norm.at[0], image, wide, rem, True)
        main_inner(image)
        if step == 0:
            pieces[0] = forward_along_y(pieces[0], lora.at[0], lora_send.at[0], lora_recv.at[0])
            pieces.append(send_along_z(lora.at[1], lora_send.at[1], lora_recv.at[1]))
    for copies in borders:
        wait_borders(copies[:4])
    for image in order:
        widen_image(own, top, bot, col, norm.at[0], image, wide, rem, False)
        main_edges(image)

    copy = relay(0)
    borders = []
    for step, image in enumerate(order):
        if step == 1:
            copy.wait()
        adapter(0, image)
        tail_dots(image)
        if step == 0:
            pieces[1] = send_along_y(pieces[1], lora.at[1], lora_send.at[1], lora_recv.at[1])
        borders.append(start_borders(hidden, top2, bot2, col2, image, edge2_send, edge2_recv))
        mean, spread = local_stats(lambda r, image=image: hidden[image, r], rows)
        one2[0, pl.ds(image, 1)] = mean
        one2[0, pl.ds(2 + image, 1)] = spread

    first = start_exchange(one2, x_send.at[2], x_recv.at[2], first_peers())
    pieces[1] = forward_along_y(pieces[1], lora.at[1], lora_send.at[1], lora_recv.at[1])
    second = middle(first, one2, two2, 3)
    copy = relay(1)
    adapter(1, order[0])
    finish(second, two2, 1, 0)

    def final(image, window, at, rows_of):
        last = dots(window, tail.at[image], pl.ds(0, 128))
        small = last.astype(BF16)
        body = dots(window, kernels.at[1], MAIN)
        span = pixels(at, len(rows_of))
        total[image, span, MAIN] = body + jnp.dot(small, expand[image, :, MAIN], preferred_element_type=F32)
        total[image, span, REST] = last + jnp.dot(small, expand[image, :, REST], preferred_element_type=F32)
        for i, r in enumerate(rows_of):
            value = total[image, pixels(at + i), pl.ds(0, chans)]
            result[image, r] = (jnp.transpose(value) + raw_own[image, r].astype(F32)).astype(BF16)

    for copies in borders:
        wait_borders(copies[4:])
    leaving = []

    def leave(image, at, count, sem):
        part = (image, pl.ds(at, count))
        copy = pltpu.make_async_copy(result.at[part], out.at[part], out_sem.at[sem])
        copy.start()
        leaving.append(copy)

    for step, image in enumerate(order):
        if step == 1:
            copy.wait()
            adapter(1, image)
        widen_image(hidden, top2, bot2, col2, norm.at[1], image, wide, rem, True)

        def chunk(c, carry, image=image):
            at = 1 + c * inner
            final(image, windows(wide, image, at, inner), at, [at + i for i in range(inner)])
            return carry

        lax.fori_loop(0, 2, chunk, 0)
        leave(image, 1, rows - 2, step)
    for copies in borders:
        wait_borders(copies[:4])
    for image in order:
        widen_image(hidden, top2, bot2, col2, norm.at[1], image, wide, rem, False)
        final(image, edge_windows(wide, image), 0, ends)
        for r in ends:
            leave(image, r, 1, len(leaving))
    for copy in leaving:
        copy.wait()


VM = pl.BlockSpec(memory_space=pltpu.VMEM)
HB = pl.BlockSpec(memory_space=pl.ANY)
SM = pl.BlockSpec(memory_space=pltpu.SMEM)
DMA = pltpu.SemaphoreType.DMA


def local(
    latents, timestep_embedding, embedding_weight, gain, shift, kernel_weight, reduce_library, expand_library,
    image_adapter, adapter_bank_row,
):
    images, rows, columns, chans = latents.shape
    pieces = Y * Z
    deep = UP_AT + 8
    map_of = (images, rows, columns, chans)
    line = pltpu.VMEM((images, columns, chans), BF16)
    edge = pltpu.VMEM((images, rows + 2, EDGE, chans), BF16)
    result = pl.pallas_call(
        block_kernel,
        out_shape=jax.ShapeDtypeStruct((images, rows, chans, columns), BF16),
        in_specs=[HB, VM, VM, SM, SM, VM, HB, VM, VM, HB],
        out_specs=HB,
        scratch_shapes=[
            pltpu.VMEM((images, rows, chans, columns), BF16),
            pltpu.VMEM((images, rows, chans, columns), BF16),
            pltpu.VMEM((chans, embedding_weight.shape[0]), BF16),
            pltpu.VMEM((chans, chans), BF16),
            pltpu.VMEM(map_of, BF16),
            pltpu.VMEM(map_of, BF16),
            pltpu.VMEM((2, 3, 3 * chans, chans), BF16),
            pltpu.VMEM((images, rows + 2, columns, 3 * chans), BF16),
            pltpu.VMEM((images, rows * columns, 384), F32),
            pltpu.VMEM((2, 3, 3 * chans, 128), BF16),
            pltpu.VMEM((images, 3, 3 * chans, 128), BF16),
            pltpu.VMEM((images, 128, 384), BF16),
            pltpu.VMEM((9 * chans, 128), F32),
            pltpu.VMEM((pieces * 8, 128), F32),
            pltpu.VMEM((128, 128), F32),
            pltpu.VMEM((16, chans), F32),
            pltpu.VMEM((2, deep, 128), F32),
            pltpu.VMEM((8, 2, deep, 128), BF16),
            pltpu.VMEM((2, images, Y, Z, deep, 128), BF16),
            *([line, line, edge] * 2),
            pltpu.VMEM((2, 8, chans), F32),
            pltpu.VMEM((2 * Y, 4, chans), F32),
            pltpu.VMEM((Z, 4, chans), F32),
            pltpu.VMEM((2 * Y, 4, chans), F32),
            pltpu.VMEM((Z, 4, chans), F32),
            DMA((3,)),
            DMA((6,)),
            DMA((8,)),
            DMA((8,)),
            DMA((2, Z + Y)),
            DMA((2, Z + Y)),
            DMA((2,)),
            DMA((2,)),
            *([DMA((images, 5))] * 4),
            DMA((4, 8)),
            DMA((4, 8)),
        ],
        compiler_params=pltpu.CompilerParams(
            collective_id=0, has_side_effects=True, vmem_limit_bytes=56 * 2**20
        ),
        name="resnet_block",
    )(
        jnp.swapaxes(latents, 2, 3),
        reduce_library,
        expand_library,
        image_adapter.T,
        adapter_bank_row,
        timestep_embedding,
        embedding_weight.T,
        gain,
        shift,
        kernel_weight.reshape(2, 3, 3 * chans, chans),
    )
    return jnp.swapaxes(result, 2, 3)


def solution(mesh):
    in_specs = (
        P("req", "patch", "owner", None),
        P("req", None),
        P(),
        P(),
        P(),
        P(),
        P(("req", "owner"), None, "patch"),
        P(("req", "owner"), None, "patch"),
        P("req", None),
        P(),
    )
    return jax.shard_map(
        local, mesh=mesh, in_specs=in_specs, out_specs=P("req", "patch", "owner", None), check_vma=False
    )
```

```python
import jax
import jax.numpy as jnp
from jax import lax
from jax.experimental import pallas as pl
from jax.experimental.pallas import tpu as pltpu
from jax.sharding import PartitionSpec as P

MESH = pl.DeviceIdType.MESH
F32, BF16 = jnp.float32, jnp.bfloat16
Y, Z = 4, 8
RANK = 64
EDGE = 16
GROUP = 10


def remote(src, dst, send, recv, device):
    return pltpu.make_async_remote_copy(
        src_ref=src, dst_ref=dst, send_sem=send, recv_sem=recv, device_id=device, device_id_type=MESH
    )


def place():
    patch, req, owner = lax.axis_index("patch"), lax.axis_index("req"), lax.axis_index("owner")
    return patch, req, owner, patch // Z, patch % Z


def greet():
    patch, req, owner, y, z = place()
    sem = pltpu.get_barrier_semaphore()
    count = 0

    def signal(device):
        pl.semaphore_signal(sem, inc=1, device_id=device, device_id_type=MESH)

    for dz in range(1, Z):
        signal((y * Z + (z + dz) % Z, req, owner))
        count += 1
    for dy in range(1, Y):
        signal(((y + dy) % Y * Z + z, req, owner))
        count += 1
    for k in range(1, 2 * Y, 2):
        g = (y * 2 + owner + k) % (2 * Y)
        signal(((g // 2) * Z + z, req, g % 2))
        count += 1
    for step in (1, Y * Z - 1):
        for other in (owner, 1 - owner):
            signal(((patch + step) % (Y * Z), req, other))
            count += 1
    for k in range(1, 8):
        g = (req * 2 + owner + k) % 8
        signal((patch, g // 2, g % 2))
        count += 1
    return lambda: pl.semaphore_wait(sem, count)


def start_borders(src, top, bot, col, image, send, recv):
    patch, req, owner, y, z = place()
    rows = src.shape[1]
    last = Y * Z - 1
    edge = pl.multiple_of((1 - owner) * (src.shape[2] - EDGE), EDGE)
    cols = pl.ds(edge, EDGE)

    def copy(at, block, target, device):
        return remote(block, target, send.at[image, at], recv.at[image, at], device)

    down, up = patch < last, patch > 0
    copies = [
        (down, up, copy(0, src.at[image, rows - 1], top.at[image], (patch + 1, req, owner))),
        (up, down, copy(1, src.at[image, 0], bot.at[image], (patch - 1, req, owner))),
        (down, up, copy(2, src.at[image, rows - 1, cols], col.at[image, 0], (patch + 1, req, 1 - owner))),
        (up, down, copy(3, src.at[image, 0, cols], col.at[image, rows + 1], (patch - 1, req, 1 - owner))),
        (None, None, copy(4, src.at[image, :, cols], col.at[image, pl.ds(1, rows)], (patch, req, 1 - owner))),
    ]
    for sends, _, item in copies:
        if sends is None:
            item.start()
        else:
            pl.when(sends)(item.start)
    return copies


def clear_borders(top, bot, col):
    patch = lax.axis_index("patch")
    end = col.shape[1] - 1

    @pl.when(patch == 0)
    def _():
        top[...] = jnp.zeros_like(top)
        col[:, 0] = jnp.zeros_like(col[:, 0])

    @pl.when(patch == Y * Z - 1)
    def _():
        bot[...] = jnp.zeros_like(bot)
        col[:, end] = jnp.zeros_like(col[:, end])


def wait_borders(copies):
    for sends, receives, copy in copies:
        if sends is None:
            copy.wait()
        else:
            pl.when(sends)(copy.wait_send)
            pl.when(receives)(copy.wait_recv)


def local_stats(rows_of, rows):
    def add(f):
        def step(r, total):
            x = f(rows_of(r).astype(F32))
            return total + jnp.sum(x.reshape(x.shape[0] // 8, 8, x.shape[1]), axis=0)

        return step

    chans = rows_of(0).shape[1]
    count = rows * rows_of(0).shape[0]
    zero = jnp.zeros((8, chans), F32)
    total = lax.fori_loop(0, rows, add(lambda x: x), zero)
    mean = jnp.sum(total, axis=0, keepdims=True) * (1.0 / count)
    spread = lax.fori_loop(0, rows, add(lambda x: (x - mean) * (x - mean)), zero)
    return mean, jnp.sum(spread, axis=0, keepdims=True)


def start_exchange(slots, send, recv, peers):
    copies = [
        remote(slots.at[0], slots.at[k], send.at[k], recv.at[k], peer) for k, peer in enumerate(peers, 1)
    ]
    for copy in copies:
        copy.start()
    return copies


def combine(slots, count):
    values = slots[...]
    half = values.shape[1] // 2
    total = jnp.sum(values, axis=0)
    mean = total * (1.0 / values.shape[0])
    off = values - mean[None]
    between = jnp.sum(off * off, axis=0)
    return mean[0:half], total[half:] + count * between[0:half]


def first_peers():
    patch, req, owner, y, z = place()
    peers = []
    for k in range(1, 2 * Y):
        g = (y * 2 + owner + k) % (2 * Y)
        peers.append(((g // 2) * Z + z, req, g % 2))
    return peers


def second_peers():
    patch, req, owner, y, z = place()
    return [(y * Z + (z + k) % Z, req, owner) for k in range(1, Z)]


def group_matrix(chans):
    row = lax.broadcasted_iota(jnp.int32, (chans, chans), 0)
    column = lax.broadcasted_iota(jnp.int32, (chans, chans), 1)
    return jnp.where((row * 6554) >> 16 == (column * 6554) >> 16, 1.0, 0.0).astype(BF16)


def group_mean(values, groups):
    count = values.shape[0]
    values = jnp.concatenate([values] * (8 // count), axis=0)
    high = values.astype(BF16).astype(F32)
    rest = values - high
    middle = rest.astype(BF16).astype(F32)
    parts = jnp.concatenate([high, middle, rest - middle], axis=0).astype(BF16)
    total = jnp.dot(parts, groups, preferred_element_type=F32)
    return (total[0:count] + total[8 : 8 + count] + total[16 : 16 + count]) * (1.0 / GROUP)


def finish_norm(mean, spread, count, gain, shift, groups):
    center = group_mean(mean, groups)
    off = mean - center
    var = group_mean(spread * (1.0 / count) + off * off, groups)
    scale = gain / jnp.sqrt(var + 1e-05)
    return center, 0.5 * scale, 0.5 * shift


def lay_piece(reduce_row, expand_row, piece):
    down = reduce_row[0].astype(F32)
    up = expand_row[0].astype(F32)
    piece[...] = jnp.zeros_like(piece)
    for i in range(down.shape[1] // 128):
        piece[:, i, :] = down[:, i * 128 : i * 128 + 128]
    for i in range(up.shape[1] // 128):
        piece[:, UP_AT + i, :] = up[:, i * 128 : i * 128 + 128]
    return piece[...].astype(BF16)


def send_along_z(lora, send, recv):
    patch, req, owner, y, z = place()
    block = lora.at[owner, y, z]
    copies = [
        remote(block, block, send.at[k], recv.at[k], (y * Z + (z + k) % Z, req, owner)) for k in range(1, Z)
    ]
    for copy in copies:
        copy.start()
    return copies


def send_along_y(copies, lora, send, recv):
    patch, req, owner, y, z = place()
    for copy in copies:
        copy.wait()
    block = lora.at[owner, y]
    copies = [
        remote(block, block, send.at[Z + k], recv.at[Z + k], ((y + k) % Y * Z + z, req, owner)) for k in (1, Y - 1)
    ]
    for copy in copies:
        copy.start()
    return copies


def forward_along_y(copies, lora, send, recv):
    patch, req, owner, y, z = place()
    for copy in copies:
        copy.wait()
    half = Z // 2
    copies = []
    for at, k, step in ((0, 1, 0), (Z + 2, Y - 1, half)):
        block = lora.at[owner, (y + Y - k) % Y, pl.ds(step, half)]
        copies.append(remote(block, block, send.at[at], recv.at[at], ((y + k) % Y * Z + z, req, owner)))
        copies[-1].start()
    return copies


def lay_adapter(lora, image, base, tail, expand, flat, ups, wide_up):
    pieces = Y * Z
    depth = tail.shape[1] * 3 // pieces
    half = depth // 2

    def lay(p, carry):
        value = lora[image, p // Z, p % Z].astype(F32)
        down = value[0:half]
        flat[pl.ds(p * depth, half, 2)] = pltpu.roll(down, 64, 1)
        flat[pl.ds(p * depth + 1, half, 2)] = down
        ups[pl.ds(pl.multiple_of(p * 8, 8), 8)] = value[UP_AT : UP_AT + 8]
        return carry

    lax.fori_loop(0, pieces, lay, 0, unroll=8)
    lane = lax.broadcasted_iota(jnp.int32, base.shape[1:], 1)
    for d in range(3):
        down = flat[pl.ds(d * base.shape[1], base.shape[1])]
        tail[d] = jnp.where(lane >= 64, down, base[d].astype(F32)).astype(BF16)
    line = [ups[pl.ds(k, pieces, 8)] for k in range(5)]
    turned = [pltpu.roll(v, 64, 1) for v in line]
    low = lax.broadcasted_iota(jnp.int32, line[0].shape, 1) < 64
    even = line[0:3]
    odd = [jnp.where(low, turned[2], turned[3]), jnp.where(low, turned[3], turned[4]), turned[4]]
    for b in range(3):
        wide_up[pl.ds(0, 64)] = jnp.zeros((64, 128), F32)
        wide_up[pl.ds(64, pieces, 2)] = even[b]
        wide_up[pl.ds(65, pieces, 2)] = odd[b]
        expand[:, pl.ds(b * 128, 128)] = wide_up[...].astype(BF16)


def widen_image(source, top, bot, col, norm, image, wide, rem, inner):
    patch, req, owner, y, z = place()
    rows, columns = source.shape[1:3]
    last = Y * Z - 1
    index = lax.broadcasted_iota(jnp.int32, (columns, 1), 0)
    center = norm[pl.ds(image, 1)]
    scale = norm[pl.ds(2 + image, 1)]
    offset = norm[pl.ds(4, 1)]

    def activate(x):
        h = (x.astype(F32) - center) * scale + offset
        return h + h * jnp.tanh(h)

    def border(at):
        return activate(
            jnp.where(owner == 0, col[image, at, 0, :].astype(F32), col[image, at, EDGE - 1, :].astype(F32))
        )

    def lay(r, act, edge):
        left = jnp.where(index == 0, jnp.where(owner == 1, edge, 0.0), pltpu.roll(act, 1, 0))
        right = jnp.where(
            index == columns - 1, jnp.where(owner == 0, edge, 0.0), pltpu.roll(act, columns - 1, 0)
        )
        wide[image, r] = jnp.concatenate([left, act, right], axis=1).astype(BF16)

    if inner:
        rem[pl.ds(0, rows)] = border(slice(1, rows + 1))

        def row(r, carry):
            lay(r + 1, activate(source[image, r]), rem[pl.ds(r, 1)])
            return carry

        lax.fori_loop(0, rows, row, 0, unroll=2)
    else:
        for r, block, inside in ((0, top, patch > 0), (rows + 1, bot, patch < last)):
            edge = jnp.where(inside, border(slice(r, r + 1)), 0.0)
            lay(r, jnp.where(inside, activate(block[image]), 0.0), edge)


def windows(wide, image, at, part):
    columns, depth = wide.shape[2:]
    return [wide[image, pl.ds(at + d, part)].reshape(part * columns, depth) for d in range(3)]


def edge_windows(wide, image):
    last = wide.shape[1] - 3
    return [jnp.concatenate([wide[image, d], wide[image, last + d]], axis=0) for d in range(3)]


def dots(window, matrix, lanes):
    return sum(jnp.dot(window[d], matrix[d, :, lanes], preferred_element_type=F32) for d in range(3))


MAIN, REST = pl.ds(0, 256), pl.ds(256, 128)
UP_AT = 48


def block_kernel(
    raw, reduce_row, expand_row, image_adapter, bank_row, embedding, weight_hbm, gain, shift, kernels_hbm,
    out,
    raw_own, result, weight, groups, own, hidden, kernels, wide, total, base, tail, expand, flat, ups, wide_up, rem,
    piece, held, lora, top, bot, col, top2, bot2, col2, norm, one, two, one2, two2,
    local_sem, out_sem, bank_send, bank_recv, lora_send, lora_recv, relay_send, relay_recv,
    edge_send, edge_recv, edge2_send, edge2_recv, x_send, x_recv,
):
    patch, req, owner, y, z = place()
    images, rows, columns, chans = own.shape
    count = rows * columns
    fetch = pltpu.make_async_copy(raw, raw_own, local_sem.at[0])
    fetch.start()
    fetch_kernels = pltpu.make_async_copy(kernels_hbm, kernels, local_sem.at[1])
    fetch_kernels.start()
    fetch_weight = pltpu.make_async_copy(weight_hbm, weight, local_sem.at[2])
    fetch_weight.start()
    arrived = greet()
    me = req * 2 + owner
    held[me] = lay_piece(reduce_row, expand_row, piece)
    clear_borders(top, bot, col)
    clear_borders(top2, bot2, col2)
    groups[...] = group_matrix(chans)
    fetch.wait()

    def turn(t, carry):
        image, r = t // rows, t % rows
        own[image, r] = jnp.transpose(raw_own[image, r].astype(F32)).astype(BF16)
        return carry

    lax.fori_loop(0, images * rows, turn, 0, unroll=4)

    for image in range(images):
        mean, spread = local_stats(lambda r, image=image: own[image, r], rows)
        one[0, pl.ds(image, 1)] = mean
        one[0, pl.ds(2 + image, 1)] = spread
    arrived()

    first = start_exchange(one, x_send.at[0], x_recv.at[0], first_peers())
    bank = []
    for k in range(1, 8):
        g = (me + k) % 8
        copy = remote(held.at[me], held.at[me], bank_send.at[k], bank_recv.at[k], (patch, g // 2, g % 2))
        copy.start()
        bank.append(copy)

    fetch_weight.wait()
    u = embedding[...].astype(F32)
    temb = (u / (1.0 + jnp.exp(-u))).astype(BF16)
    proj = lax.dot_general(temb, weight[...], (((1,), (1,)), ((), ())), preferred_element_type=F32)
    norm[0, pl.ds(5, 2)] = proj
    fetch_kernels.wait()

    def middle(first, one, two, at):
        for copy in first:
            copy.wait()
        mean, spread = combine(one, float(count))
        half = mean.shape[0]
        two[0, pl.ds(0, half)] = mean
        two[0, pl.ds(half, half)] = spread
        return start_exchange(two, x_send.at[at], x_recv.at[at], second_peers())

    def finish(second, two, which, image):
        for copy in second:
            copy.wait()
        mean, spread = combine(two, float(count * 2 * Y))
        half = mean.shape[0]
        center, scale, offset = finish_norm(
            mean, spread, float(count * 2 * Y * Z), gain[pl.ds(which, 1)], shift[pl.ds(which, 1)], groups[...]
        )
        norm[which, pl.ds(image, half)] = center
        norm[which, pl.ds(2 + image, half)] = scale
        norm[which, pl.ds(4, 1)] = offset

    second = middle(first, one, two, 1)
    for copy in bank:
        copy.wait()
    chosen = held[bank_row[image_adapter[0, owner]]]
    lora[0, owner, y, z] = chosen[0]
    lora[1, owner, y, z] = chosen[1]
    pieces = [send_along_z(lora.at[0], lora_send.at[0], lora_recv.at[0])]
    borders = [start_borders(own, top, bot, col, i, edge_send, edge_recv) for i in range(images)]
    for which in range(2):
        for d in range(3):
            last = kernels[which, d, :, pl.ds(256, chans - 256)].astype(F32)
            base[which, d] = jnp.concatenate([last, jnp.zeros_like(last)], axis=1).astype(BF16)
    finish(second, two, 0, 0)
    pieces[0] = send_along_y(pieces[0], lora.at[0], lora_send.at[0], lora_recv.at[0])

    order = (owner, 1 - owner)
    inner = (rows - 2) // 2
    ends = (0, rows - 1)

    def pixels(r, count=1):
        return pl.ds(pl.multiple_of(r * columns, columns), count * columns)

    def main_inner(image):
        def chunk(c, carry):
            at = 1 + c * inner
            total[image, pixels(at, inner), MAIN] = dots(windows(wide, image, at, inner), kernels.at[0], MAIN)
            return carry

        lax.fori_loop(0, 2, chunk, 0)

    def main_edges(image):
        value = dots(edge_windows(wide, image), kernels.at[0], MAIN)
        for i, r in enumerate(ends):
            total[image, pixels(r), MAIN] = value[i * columns : (i + 1) * columns]

    def relay(which):
        for copy in pieces[which]:
            copy.wait()
        block = lora.at[which, owner]
        copy = remote(block, block, relay_send.at[which], relay_recv.at[which], (patch, req, 1 - owner))
        copy.start()
        return copy

    def adapter(which, image):
        lay_adapter(
            lora.at[which], image, base.at[which], tail.at[image], expand.at[image], flat, ups, wide_up
        )

    def tail_dots(image):
        part = rows // 2

        def chunk(c, carry):
            at = c * part
            last = dots(windows(wide, image, at, part), tail.at[image], pl.ds(0, 128))
            small = last.astype(BF16)
            span = pixels(at, part)
            total[image, span, REST] = last + jnp.dot(small, expand[image, :, REST], preferred_element_type=F32)
            total[image, span, MAIN] += jnp.dot(small, expand[image, :, MAIN], preferred_element_type=F32)
            bias = norm[0, pl.ds(5 + image, 1)]
            for r in range(part):
                hidden[image, at + r] = (total[image, pixels(at + r), pl.ds(0, chans)] + bias).astype(BF16)
            return carry

        lax.fori_loop(0, 2, chunk, 0)

    for copies in borders:
        wait_borders(copies[4:])
    for step, image in enumerate(order):
        widen_image(own, top, bot, col, norm.at[0], image, wide, rem, True)
        main_inner(image)
        if step == 0:
            pieces[0] = forward_along_y(pieces[0], lora.at[0], lora_send.at[0], lora_recv.at[0])
            pieces.append(send_along_z(lora.at[1], lora_send.at[1], lora_recv.at[1]))
    for copies in borders:
        wait_borders(copies[:4])
    for image in order:
        widen_image(own, top, bot, col, norm.at[0], image, wide, rem, False)
        main_edges(image)

    copy = relay(0)
    borders = []
    for step, image in enumerate(order):
        if step == 1:
            copy.wait()
        adapter(0, image)
        tail_dots(image)
        if step == 0:
            pieces[1] = send_along_y(pieces[1], lora.at[1], lora_send.at[1], lora_recv.at[1])
        if step == 0:
            borders.append(start_borders(hidden, top2, bot2, col2, image, edge2_send, edge2_recv))
        mean, spread = local_stats(lambda r, image=image: hidden[image, r], rows)
        one2[0, pl.ds(image, 1)] = mean
        one2[0, pl.ds(2 + image, 1)] = spread

    first = start_exchange(one2, x_send.at[2], x_recv.at[2], first_peers())
    pieces[1] = forward_along_y(pieces[1], lora.at[1], lora_send.at[1], lora_recv.at[1])
    second = middle(first, one2, two2, 3)
    borders.append(start_borders(hidden, top2, bot2, col2, order[1], edge2_send, edge2_recv))
    copy = relay(1)
    adapter(1, order[0])
    finish(second, two2, 1, 0)

    def final(image, window, at, rows_of):
        last = dots(window, tail.at[image], pl.ds(0, 128))
        small = last.astype(BF16)
        body = dots(window, kernels.at[1], MAIN)
        span = pixels(at, len(rows_of))
        total[image, span, MAIN] = body + jnp.dot(small, expand[image, :, MAIN], preferred_element_type=F32)
        total[image, span, REST] = last + jnp.dot(small, expand[image, :, REST], preferred_element_type=F32)
        for i, r in enumerate(rows_of):
            value = total[image, pixels(at + i), pl.ds(0, chans)]
            result[image, r] = (jnp.transpose(value) + raw_own[image, r].astype(F32)).astype(BF16)

    for copies in borders:
        wait_borders(copies[4:])
    leaving = []

    def leave(image, at, count, sem):
        part = (image, pl.ds(at, count))
        copy = pltpu.make_async_copy(result.at[part], out.at[part], out_sem.at[sem])
        copy.start()
        leaving.append(copy)

    for step, image in enumerate(order):
        if step == 1:
            copy.wait()
            adapter(1, image)
        widen_image(hidden, top2, bot2, col2, norm.at[1], image, wide, rem, True)

        def chunk(c, carry, image=image):
            at = 1 + c * inner
            final(image, windows(wide, image, at, inner), at, [at + i for i in range(inner)])
            return carry

        lax.fori_loop(0, 2, chunk, 0)
        leave(image, 1, rows - 2, step)
    for copies in borders:
        wait_borders(copies[:4])
    for image in order:
        widen_image(hidden, top2, bot2, col2, norm.at[1], image, wide, rem, False)
        final(image, edge_windows(wide, image), 0, ends)
        for r in ends:
            leave(image, r, 1, len(leaving))
    for copy in leaving:
        copy.wait()


def copy_out(source, target, sem):
    images, rows = source.shape[:2]
    copies = [
        pltpu.make_async_copy(source.at[i, pl.ds(r, 2)], target.at[i, pl.ds(r, 2)], sem.at[i, r // 2])
        for i in range(images)
        for r in range(0, rows, 2)
    ]
    for copy in copies:
        copy.start()
    for copy in copies:
        copy.wait()


VM = pl.BlockSpec(memory_space=pltpu.VMEM)
HB = pl.BlockSpec(memory_space=pl.ANY)
SM = pl.BlockSpec(memory_space=pltpu.SMEM)
DMA = pltpu.SemaphoreType.DMA


def local(
    latents, timestep_embedding, embedding_weight, gain, shift, kernel_weight, reduce_library, expand_library,
    image_adapter, adapter_bank_row,
):
    images, rows, columns, chans = latents.shape
    pieces = Y * Z
    deep = UP_AT + 8
    map_of = (images, rows, columns, chans)
    line = pltpu.VMEM((images, columns, chans), BF16)
    edge = pltpu.VMEM((images, rows + 2, EDGE, chans), BF16)
    result = pl.pallas_call(
        block_kernel,
        out_shape=jax.ShapeDtypeStruct((images, rows, chans, columns), BF16),
        in_specs=[HB, VM, VM, SM, SM, VM, HB, VM, VM, HB],
        out_specs=HB,
        scratch_shapes=[
            pltpu.VMEM((images, rows, chans, columns), BF16),
            pltpu.VMEM((images, rows, chans, columns), BF16),
            pltpu.VMEM((chans, embedding_weight.shape[0]), BF16),
            pltpu.VMEM((chans, chans), BF16),
            pltpu.VMEM(map_of, BF16),
            pltpu.VMEM(map_of, BF16),
            pltpu.VMEM((2, 3, 3 * chans, chans), BF16),
            pltpu.VMEM((images, rows + 2, columns, 3 * chans), BF16),
            pltpu.VMEM((images, rows * columns, 384), F32),
            pltpu.VMEM((2, 3, 3 * chans, 128), BF16),
            pltpu.VMEM((images, 3, 3 * chans, 128), BF16),
            pltpu.VMEM((images, 128, 384), BF16),
            pltpu.VMEM((9 * chans, 128), F32),
            pltpu.VMEM((pieces * 8, 128), F32),
            pltpu.VMEM((128, 128), F32),
            pltpu.VMEM((16, chans), F32),
            pltpu.VMEM((2, deep, 128), F32),
            pltpu.VMEM((8, 2, deep, 128), BF16),
            pltpu.VMEM((2, images, Y, Z, deep, 128), BF16),
            *([line, line, edge] * 2),
            pltpu.VMEM((2, 8, chans), F32),
            pltpu.VMEM((2 * Y, 4, chans), F32),
            pltpu.VMEM((Z, 4, chans), F32),
            pltpu.VMEM((2 * Y, 4, chans), F32),
            pltpu.VMEM((Z, 4, chans), F32),
            DMA((3,)),
            DMA((6,)),
            DMA((8,)),
            DMA((8,)),
            DMA((2, Z + Y)),
            DMA((2, Z + Y)),
            DMA((2,)),
            DMA((2,)),
            *([DMA((images, 5))] * 4),
            DMA((4, 8)),
            DMA((4, 8)),
        ],
        compiler_params=pltpu.CompilerParams(
            collective_id=0, has_side_effects=True, vmem_limit_bytes=56 * 2**20
        ),
        name="resnet_block",
    )(
        jnp.swapaxes(latents, 2, 3),
        reduce_library,
        expand_library,
        image_adapter.T,
        adapter_bank_row,
        timestep_embedding,
        embedding_weight.T,
        gain,
        shift,
        kernel_weight.reshape(2, 3, 3 * chans, chans),
    )
    result = pl.pallas_call(
        copy_out,
        out_shape=jax.ShapeDtypeStruct(result.shape, BF16),
        in_specs=[HB],
        out_specs=HB,
        scratch_shapes=[DMA((images, rows // 2))],
        name="copy_out",
    )(result)
    return jnp.swapaxes(result, 2, 3)


def solution(mesh):
    in_specs = (
        P("req", "patch", "owner", None),
        P("req", None),
        P(),
        P(),
        P(),
        P(),
        P(("req", "owner"), None, "patch"),
        P(("req", "owner"), None, "patch"),
        P("req", None),
        P(),
    )
    return jax.shard_map(
        local, mesh=mesh, in_specs=in_specs, out_specs=P("req", "patch", "owner", None), check_vma=False
    )
```

```python
import jax
import jax.numpy as jnp
from jax import lax
from jax.experimental import pallas as pl
from jax.experimental.pallas import tpu as pltpu
from jax.sharding import PartitionSpec as P

MESH = pl.DeviceIdType.MESH
F32, BF16 = jnp.float32, jnp.bfloat16
Y, Z = 4, 8
RANK = 64
EDGE = 16
GROUP = 10


def remote(src, dst, send, recv, device):
    return pltpu.make_async_remote_copy(
        src_ref=src, dst_ref=dst, send_sem=send, recv_sem=recv, device_id=device, device_id_type=MESH
    )


def place():
    patch, req, owner = lax.axis_index("patch"), lax.axis_index("req"), lax.axis_index("owner")
    return patch, req, owner, patch // Z, patch % Z


def greet():
    patch, req, owner, y, z = place()
    sem = pltpu.get_barrier_semaphore()
    count = 0

    def signal(device):
        pl.semaphore_signal(sem, inc=1, device_id=device, device_id_type=MESH)

    for dz in range(1, Z):
        signal((y * Z + (z + dz) % Z, req, owner))
        count += 1
    for dy in range(1, Y):
        signal(((y + dy) % Y * Z + z, req, owner))
        count += 1
    for k in range(1, 2 * Y, 2):
        g = (y * 2 + owner + k) % (2 * Y)
        signal(((g // 2) * Z + z, req, g % 2))
        count += 1
    for step in (1, Y * Z - 1):
        for other in (owner, 1 - owner):
            signal(((patch + step) % (Y * Z), req, other))
            count += 1
    for k in range(1, 8):
        g = (req * 2 + owner + k) % 8
        signal((patch, g // 2, g % 2))
        count += 1
    return lambda: pl.semaphore_wait(sem, count)


def start_borders(src, top, bot, col, image, send, recv):
    patch, req, owner, y, z = place()
    rows = src.shape[1]
    last = Y * Z - 1
    edge = pl.multiple_of((1 - owner) * (src.shape[2] - EDGE), EDGE)
    cols = pl.ds(edge, EDGE)

    def copy(at, block, target, device):
        return remote(block, target, send.at[image, at], recv.at[image, at], device)

    down, up = patch < last, patch > 0
    copies = [
        (down, up, copy(0, src.at[image, rows - 1], top.at[image], (patch + 1, req, owner))),
        (up, down, copy(1, src.at[image, 0], bot.at[image], (patch - 1, req, owner))),
        (down, up, copy(2, src.at[image, rows - 1, cols], col.at[image, 0], (patch + 1, req, 1 - owner))),
        (up, down, copy(3, src.at[image, 0, cols], col.at[image, rows + 1], (patch - 1, req, 1 - owner))),
        (None, None, copy(4, src.at[image, :, cols], col.at[image, pl.ds(1, rows)], (patch, req, 1 - owner))),
    ]
    for sends, _, item in copies:
        if sends is None:
            item.start()
        else:
            pl.when(sends)(item.start)
    return copies


def clear_borders(top, bot, col):
    patch = lax.axis_index("patch")
    end = col.shape[1] - 1

    @pl.when(patch == 0)
    def _():
        top[...] = jnp.zeros_like(top)
        col[:, 0] = jnp.zeros_like(col[:, 0])

    @pl.when(patch == Y * Z - 1)
    def _():
        bot[...] = jnp.zeros_like(bot)
        col[:, end] = jnp.zeros_like(col[:, end])


def wait_borders(copies):
    for sends, receives, copy in copies:
        if sends is None:
            copy.wait()
        else:
            pl.when(sends)(copy.wait_send)
            pl.when(receives)(copy.wait_recv)


def local_stats(rows_of, rows):
    def add(f):
        def step(r, total):
            x = f(rows_of(r).astype(F32))
            return total + jnp.sum(x.reshape(x.shape[0] // 8, 8, x.shape[1]), axis=0)

        return step

    chans = rows_of(0).shape[1]
    count = rows * rows_of(0).shape[0]
    zero = jnp.zeros((8, chans), F32)
    total = lax.fori_loop(0, rows, add(lambda x: x), zero)
    mean = jnp.sum(total, axis=0, keepdims=True) * (1.0 / count)
    spread = lax.fori_loop(0, rows, add(lambda x: (x - mean) * (x - mean)), zero)
    return mean, jnp.sum(spread, axis=0, keepdims=True)


def start_exchange(slots, send, recv, peers):
    copies = [
        remote(slots.at[0], slots.at[k], send.at[k], recv.at[k], peer) for k, peer in enumerate(peers, 1)
    ]
    for copy in copies:
        copy.start()
    return copies


def combine(slots, count):
    values = slots[...]
    half = values.shape[1] // 2
    total = jnp.sum(values, axis=0)
    mean = total * (1.0 / values.shape[0])
    off = values - mean[None]
    between = jnp.sum(off * off, axis=0)
    return mean[0:half], total[half:] + count * between[0:half]


def first_peers():
    patch, req, owner, y, z = place()
    peers = []
    for k in range(1, 2 * Y):
        g = (y * 2 + owner + k) % (2 * Y)
        peers.append(((g // 2) * Z + z, req, g % 2))
    return peers


def second_peers():
    patch, req, owner, y, z = place()
    return [(y * Z + (z + k) % Z, req, owner) for k in range(1, Z)]


def group_matrix(chans):
    row = lax.broadcasted_iota(jnp.int32, (chans, chans), 0)
    column = lax.broadcasted_iota(jnp.int32, (chans, chans), 1)
    return jnp.where((row * 6554) >> 16 == (column * 6554) >> 16, 1.0, 0.0).astype(BF16)


def group_mean(values, groups):
    count = values.shape[0]
    values = jnp.concatenate([values] * (8 // count), axis=0)
    high = values.astype(BF16).astype(F32)
    rest = values - high
    middle = rest.astype(BF16).astype(F32)
    parts = jnp.concatenate([high, middle, rest - middle], axis=0).astype(BF16)
    total = jnp.dot(parts, groups, preferred_element_type=F32)
    return (total[0:count] + total[8 : 8 + count] + total[16 : 16 + count]) * (1.0 / GROUP)


def finish_norm(mean, spread, count, gain, shift, groups):
    center = group_mean(mean, groups)
    off = mean - center
    var = group_mean(spread * (1.0 / count) + off * off, groups)
    scale = gain / jnp.sqrt(var + 1e-05)
    return center, 0.5 * scale, 0.5 * shift


def lay_piece(reduce_row, expand_row, piece):
    down = reduce_row[0].astype(F32)
    up = expand_row[0].astype(F32)
    piece[...] = jnp.zeros_like(piece)
    for i in range(down.shape[1] // 128):
        piece[:, i, :] = down[:, i * 128 : i * 128 + 128]
    for i in range(up.shape[1] // 128):
        piece[:, UP_AT + i, :] = up[:, i * 128 : i * 128 + 128]
    return piece[...].astype(BF16)


def send_along_z(lora, send, recv):
    patch, req, owner, y, z = place()
    block = lora.at[owner, y, z]
    copies = [
        remote(block, block, send.at[k], recv.at[k], (y * Z + (z + k) % Z, req, owner)) for k in range(1, Z)
    ]
    for copy in copies:
        copy.start()
    return copies


def send_along_y(copies, lora, send, recv):
    patch, req, owner, y, z = place()
    for copy in copies:
        copy.wait()
    block = lora.at[owner, y]
    copies = [
        remote(block, block, send.at[Z + k], recv.at[Z + k], ((y + k) % Y * Z + z, req, owner)) for k in (1, Y - 1)
    ]
    for copy in copies:
        copy.start()
    return copies


def forward_along_y(copies, lora, send, recv):
    patch, req, owner, y, z = place()
    for copy in copies:
        copy.wait()
    half = Z // 2
    copies = []
    for at, k, step in ((0, 1, 0), (Z + 2, Y - 1, half)):
        block = lora.at[owner, (y + Y - k) % Y, pl.ds(step, half)]
        copies.append(remote(block, block, send.at[at], recv.at[at], ((y + k) % Y * Z + z, req, owner)))
        copies[-1].start()
    return copies


def lay_adapter(lora, image, base, tail, expand, flat, ups, wide_up):
    pieces = Y * Z
    depth = tail.shape[1] * 3 // pieces
    half = depth // 2

    def lay(p, carry):
        value = lora[image, p // Z, p % Z].astype(F32)
        down = value[0:half]
        flat[pl.ds(p * depth, half, 2)] = pltpu.roll(down, 64, 1)
        flat[pl.ds(p * depth + 1, half, 2)] = down
        ups[pl.ds(pl.multiple_of(p * 8, 8), 8)] = value[UP_AT : UP_AT + 8]
        return carry

    lax.fori_loop(0, pieces, lay, 0, unroll=8)
    lane = lax.broadcasted_iota(jnp.int32, base.shape[1:], 1)
    for d in range(3):
        down = flat[pl.ds(d * base.shape[1], base.shape[1])]
        tail[d] = jnp.where(lane >= 64, down, base[d].astype(F32)).astype(BF16)
    line = [ups[pl.ds(k, pieces, 8)] for k in range(5)]
    turned = [pltpu.roll(v, 64, 1) for v in line]
    low = lax.broadcasted_iota(jnp.int32, line[0].shape, 1) < 64
    even = line[0:3]
    odd = [jnp.where(low, turned[2], turned[3]), jnp.where(low, turned[3], turned[4]), turned[4]]
    for b in range(3):
        wide_up[pl.ds(0, 64)] = jnp.zeros((64, 128), F32)
        wide_up[pl.ds(64, pieces, 2)] = even[b]
        wide_up[pl.ds(65, pieces, 2)] = odd[b]
        expand[:, pl.ds(b * 128, 128)] = wide_up[...].astype(BF16)


def widen_image(source, top, bot, col, norm, image, wide, rem, inner):
    patch, req, owner, y, z = place()
    rows, columns = source.shape[1:3]
    last = Y * Z - 1
    index = lax.broadcasted_iota(jnp.int32, (columns, 1), 0)
    center = norm[pl.ds(image, 1)]
    scale = norm[pl.ds(2 + image, 1)]
    offset = norm[pl.ds(4, 1)]

    def activate(x):
        h = (x.astype(F32) - center) * scale + offset
        return h + h * jnp.tanh(h)

    def border(at):
        return activate(
            jnp.where(owner == 0, col[image, at, 0, :].astype(F32), col[image, at, EDGE - 1, :].astype(F32))
        )

    def lay(r, act, edge):
        left = jnp.where(index == 0, jnp.where(owner == 1, edge, 0.0), pltpu.roll(act, 1, 0))
        right = jnp.where(
            index == columns - 1, jnp.where(owner == 0, edge, 0.0), pltpu.roll(act, columns - 1, 0)
        )
        wide[image, r] = jnp.concatenate([left, act, right], axis=1).astype(BF16)

    if inner:
        rem[pl.ds(0, rows)] = border(slice(1, rows + 1))

        def row(r, carry):
            lay(r + 1, activate(source[image, r]), rem[pl.ds(r, 1)])
            return carry

        lax.fori_loop(0, rows, row, 0, unroll=2)
    else:
        for r, block, inside in ((0, top, patch > 0), (rows + 1, bot, patch < last)):
            edge = jnp.where(inside, border(slice(r, r + 1)), 0.0)
            lay(r, jnp.where(inside, activate(block[image]), 0.0), edge)


def windows(wide, image, at, part):
    columns, depth = wide.shape[2:]
    return [wide[image, pl.ds(at + d, part)].reshape(part * columns, depth) for d in range(3)]


def edge_windows(wide, image):
    last = wide.shape[1] - 3
    return [jnp.concatenate([wide[image, d], wide[image, last + d]], axis=0) for d in range(3)]


def dots(window, matrix, lanes):
    return sum(jnp.dot(window[d], matrix[d, :, lanes], preferred_element_type=F32) for d in range(3))


MAIN, REST = pl.ds(0, 256), pl.ds(256, 128)
UP_AT = 48


def block_kernel(
    raw, reduce_row, expand_row, image_adapter, bank_row, embedding, weight_hbm, gain, shift, kernels_hbm,
    out,
    raw_own, result, weight, groups, own, hidden, kernels, wide, total, base, tail, expand, flat, ups, wide_up, rem,
    piece, held, lora, top, bot, col, top2, bot2, col2, norm, one, two, one2, two2,
    local_sem, out_sem, bank_send, bank_recv, lora_send, lora_recv, relay_send, relay_recv,
    edge_send, edge_recv, edge2_send, edge2_recv, x_send, x_recv,
):
    patch, req, owner, y, z = place()
    images, rows, columns, chans = own.shape
    count = rows * columns
    fetch = pltpu.make_async_copy(raw, raw_own, local_sem.at[0])
    fetch.start()
    fetch_kernels = pltpu.make_async_copy(kernels_hbm, kernels, local_sem.at[1])
    fetch_kernels.start()
    fetch_weight = pltpu.make_async_copy(weight_hbm, weight, local_sem.at[2])
    fetch_weight.start()
    arrived = greet()
    me = req * 2 + owner
    held[me] = lay_piece(reduce_row, expand_row, piece)
    clear_borders(top, bot, col)
    clear_borders(top2, bot2, col2)
    groups[...] = group_matrix(chans)
    fetch.wait()

    def turn(t, carry):
        image, r = t // rows, t % rows
        own[image, r] = jnp.transpose(raw_own[image, r].astype(F32)).astype(BF16)
        return carry

    lax.fori_loop(0, images * rows, turn, 0, unroll=4)

    for image in range(images):
        mean, spread = local_stats(lambda r, image=image: own[image, r], rows)
        one[0, pl.ds(image, 1)] = mean
        one[0, pl.ds(2 + image, 1)] = spread
    arrived()

    first = start_exchange(one, x_send.at[0], x_recv.at[0], first_peers())
    bank = []
    for k in range(1, 8):
        g = (me + k) % 8
        copy = remote(held.at[me], held.at[me], bank_send.at[k], bank_recv.at[k], (patch, g // 2, g % 2))
        copy.start()
        bank.append(copy)

    fetch_weight.wait()
    u = embedding[...].astype(F32)
    temb = (u / (1.0 + jnp.exp(-u))).astype(BF16)
    proj = lax.dot_general(temb, weight[...], (((1,), (1,)), ((), ())), preferred_element_type=F32)
    norm[0, pl.ds(5, 2)] = proj
    fetch_kernels.wait()

    def middle(first, one, two, at):
        for copy in first:
            copy.wait()
        mean, spread = combine(one, float(count))
        half = mean.shape[0]
        two[0, pl.ds(0, half)] = mean
        two[0, pl.ds(half, half)] = spread
        return start_exchange(two, x_send.at[at], x_recv.at[at], second_peers())

    def finish(second, two, which, image):
        for copy in second:
            copy.wait()
        mean, spread = combine(two, float(count * 2 * Y))
        half = mean.shape[0]
        center, scale, offset = finish_norm(
            mean, spread, float(count * 2 * Y * Z), gain[pl.ds(which, 1)], shift[pl.ds(which, 1)], groups[...]
        )
        norm[which, pl.ds(image, half)] = center
        norm[which, pl.ds(2 + image, half)] = scale
        norm[which, pl.ds(4, 1)] = offset

    second = middle(first, one, two, 1)
    for copy in bank:
        copy.wait()
    chosen = held[bank_row[image_adapter[0, owner]]]
    lora[0, owner, y, z] = chosen[0]
    lora[1, owner, y, z] = chosen[1]
    pieces = [send_along_z(lora.at[0], lora_send.at[0], lora_recv.at[0])]
    borders = [start_borders(own, top, bot, col, i, edge_send, edge_recv) for i in range(images)]
    for which in range(2):
        for d in range(3):
            last = kernels[which, d, :, pl.ds(256, chans - 256)].astype(F32)
            base[which, d] = jnp.concatenate([last, jnp.zeros_like(last)], axis=1).astype(BF16)
    finish(second, two, 0, 0)
    pieces[0] = send_along_y(pieces[0], lora.at[0], lora_send.at[0], lora_recv.at[0])

    order = (owner, 1 - owner)
    inner = (rows - 2) // 2
    ends = (0, rows - 1)

    def pixels(r, count=1):
        return pl.ds(pl.multiple_of(r * columns, columns), count * columns)

    def main_inner(image):
        def chunk(c, carry):
            at = 1 + c * inner
            total[image, pixels(at, inner), MAIN] = dots(windows(wide, image, at, inner), kernels.at[0], MAIN)
            return carry

        lax.fori_loop(0, 2, chunk, 0)

    def main_edges(image):
        value = dots(edge_windows(wide, image), kernels.at[0], MAIN)
        for i, r in enumerate(ends):
            total[image, pixels(r), MAIN] = value[i * columns : (i + 1) * columns]

    def relay(which):
        for copy in pieces[which]:
            copy.wait()
        block = lora.at[which, owner]
        copy = remote(block, block, relay_send.at[which], relay_recv.at[which], (patch, req, 1 - owner))
        copy.start()
        return copy

    def adapter(which, image):
        lay_adapter(
            lora.at[which], image, base.at[which], tail.at[image], expand.at[image], flat, ups, wide_up
        )

    def tail_dots(image):
        part = rows // 2

        def chunk(c, carry):
            at = c * part
            last = dots(windows(wide, image, at, part), tail.at[image], pl.ds(0, 128))
            small = last.astype(BF16)
            span = pixels(at, part)
            total[image, span, REST] = last + jnp.dot(small, expand[image, :, REST], preferred_element_type=F32)
            total[image, span, MAIN] += jnp.dot(small, expand[image, :, MAIN], preferred_element_type=F32)
            bias = norm[0, pl.ds(5 + image, 1)]
            for r in range(part):
                hidden[image, at + r] = (total[image, pixels(at + r), pl.ds(0, chans)] + bias).astype(BF16)
            return carry

        lax.fori_loop(0, 2, chunk, 0)

    for copies in borders:
        wait_borders(copies[4:])
    for step, image in enumerate(order):
        widen_image(own, top, bot, col, norm.at[0], image, wide, rem, True)
        main_inner(image)
        if step == 0:
            pieces[0] = forward_along_y(pieces[0], lora.at[0], lora_send.at[0], lora_recv.at[0])
            pieces.append(send_along_z(lora.at[1], lora_send.at[1], lora_recv.at[1]))
    for copies in borders:
        wait_borders(copies[:4])
    for image in order:
        widen_image(own, top, bot, col, norm.at[0], image, wide, rem, False)
        main_edges(image)

    copy = relay(0)
    borders = []
    for step, image in enumerate(order):
        if step == 1:
            copy.wait()
        adapter(0, image)
        tail_dots(image)
        if step == 0:
            pieces[1] = send_along_y(pieces[1], lora.at[1], lora_send.at[1], lora_recv.at[1])
        if step == 0:
            borders.append(start_borders(hidden, top2, bot2, col2, image, edge2_send, edge2_recv))
        mean, spread = local_stats(lambda r, image=image: hidden[image, r], rows)
        one2[0, pl.ds(image, 1)] = mean
        one2[0, pl.ds(2 + image, 1)] = spread

    first = start_exchange(one2, x_send.at[2], x_recv.at[2], first_peers())
    pieces[1] = forward_along_y(pieces[1], lora.at[1], lora_send.at[1], lora_recv.at[1])
    second = middle(first, one2, two2, 3)
    borders.append(start_borders(hidden, top2, bot2, col2, order[1], edge2_send, edge2_recv))
    copy = relay(1)
    adapter(1, order[0])
    finish(second, two2, 1, 0)

    def final(image, window, at, rows_of):
        last = dots(window, tail.at[image], pl.ds(0, 128))
        small = last.astype(BF16)
        body = dots(window, kernels.at[1], MAIN)
        span = pixels(at, len(rows_of))
        total[image, span, MAIN] = body + jnp.dot(small, expand[image, :, MAIN], preferred_element_type=F32)
        total[image, span, REST] = last + jnp.dot(small, expand[image, :, REST], preferred_element_type=F32)
        for i, r in enumerate(rows_of):
            value = total[image, pixels(at + i), pl.ds(0, chans)]
            result[image, r] = (jnp.transpose(value) + raw_own[image, r].astype(F32)).astype(BF16)

    for copies in borders:
        wait_borders(copies[4:])
    leaving = []

    def leave(image, at, count, sem):
        part = (image, pl.ds(at, count))
        copy = pltpu.make_async_copy(result.at[part], out.at[part], out_sem.at[sem])
        copy.start()
        leaving.append(copy)

    for step, image in enumerate(order):
        if step == 1:
            copy.wait()
            adapter(1, image)
        widen_image(hidden, top2, bot2, col2, norm.at[1], image, wide, rem, True)

        def chunk(c, carry, image=image):
            at = 1 + c * inner
            final(image, windows(wide, image, at, inner), at, [at + i for i in range(inner)])
            return carry

        lax.fori_loop(0, 2, chunk, 0)
        leave(image, 1, rows - 2, step)
    for copies in borders:
        wait_borders(copies[:4])
    for image in order:
        widen_image(hidden, top2, bot2, col2, norm.at[1], image, wide, rem, False)
        final(image, edge_windows(wide, image), 0, ends)
        for r in ends:
            leave(image, r, 1, len(leaving))
    for copy in leaving:
        copy.wait()


VM = pl.BlockSpec(memory_space=pltpu.VMEM)
HB = pl.BlockSpec(memory_space=pl.ANY)
SM = pl.BlockSpec(memory_space=pltpu.SMEM)
DMA = pltpu.SemaphoreType.DMA


def local(
    latents, timestep_embedding, embedding_weight, gain, shift, kernel_weight, reduce_library, expand_library,
    image_adapter, adapter_bank_row,
):
    images, rows, columns, chans = latents.shape
    pieces = Y * Z
    deep = UP_AT + 8
    map_of = (images, rows, columns, chans)
    line = pltpu.VMEM((images, columns, chans), BF16)
    edge = pltpu.VMEM((images, rows + 2, EDGE, chans), BF16)
    result = pl.pallas_call(
        block_kernel,
        out_shape=jax.ShapeDtypeStruct((images, rows, chans, columns), BF16),
        in_specs=[HB, VM, VM, SM, SM, VM, HB, VM, VM, HB],
        out_specs=HB,
        scratch_shapes=[
            pltpu.VMEM((images, rows, chans, columns), BF16),
            pltpu.VMEM((images, rows, chans, columns), BF16),
            pltpu.VMEM((chans, embedding_weight.shape[0]), BF16),
            pltpu.VMEM((chans, chans), BF16),
            pltpu.VMEM(map_of, BF16),
            pltpu.VMEM(map_of, BF16),
            pltpu.VMEM((2, 3, 3 * chans, chans), BF16),
            pltpu.VMEM((images, rows + 2, columns, 3 * chans), BF16),
            pltpu.VMEM((images, rows * columns, 384), F32),
            pltpu.VMEM((2, 3, 3 * chans, 128), BF16),
            pltpu.VMEM((images, 3, 3 * chans, 128), BF16),
            pltpu.VMEM((images, 128, 384), BF16),
            pltpu.VMEM((9 * chans, 128), F32),
            pltpu.VMEM((pieces * 8, 128), F32),
            pltpu.VMEM((128, 128), F32),
            pltpu.VMEM((16, chans), F32),
            pltpu.VMEM((2, deep, 128), F32),
            pltpu.VMEM((8, 2, deep, 128), BF16),
            pltpu.VMEM((2, images, Y, Z, deep, 128), BF16),
            *([line, line, edge] * 2),
            pltpu.VMEM((2, 8, chans), F32),
            pltpu.VMEM((2 * Y, 4, chans), F32),
            pltpu.VMEM((Z, 4, chans), F32),
            pltpu.VMEM((2 * Y, 4, chans), F32),
            pltpu.VMEM((Z, 4, chans), F32),
            DMA((3,)),
            DMA((6,)),
            DMA((8,)),
            DMA((8,)),
            DMA((2, Z + Y)),
            DMA((2, Z + Y)),
            DMA((2,)),
            DMA((2,)),
            *([DMA((images, 5))] * 4),
            DMA((4, 8)),
            DMA((4, 8)),
        ],
        compiler_params=pltpu.CompilerParams(
            collective_id=0, has_side_effects=True, vmem_limit_bytes=56 * 2**20
        ),
        name="resnet_block",
    )(
        jnp.swapaxes(latents, 2, 3),
        reduce_library,
        expand_library,
        image_adapter.T,
        adapter_bank_row,
        timestep_embedding,
        embedding_weight.T,
        gain,
        shift,
        kernel_weight.reshape(2, 3, 3 * chans, chans),
    )
    return jnp.swapaxes(result, 2, 3)


def solution(mesh):
    in_specs = (
        P("req", "patch", "owner", None),
        P("req", None),
        P(),
        P(),
        P(),
        P(),
        P(("req", "owner"), None, "patch"),
        P(("req", "owner"), None, "patch"),
        P("req", None),
        P(),
    )
    return jax.shard_map(
        local, mesh=mesh, in_specs=in_specs, out_specs=P("req", "patch", "owner", None), check_vma=False
    )
```

```python
import jax
import jax.numpy as jnp
from jax import lax
from jax.experimental import pallas as pl
from jax.experimental.pallas import tpu as pltpu
from jax.sharding import PartitionSpec as P

MESH = pl.DeviceIdType.MESH
F32, BF16 = jnp.float32, jnp.bfloat16
Y, Z = 4, 8
RANK = 64
EDGE = 16
GROUP = 10


def remote(src, dst, send, recv, device):
    return pltpu.make_async_remote_copy(
        src_ref=src, dst_ref=dst, send_sem=send, recv_sem=recv, device_id=device, device_id_type=MESH
    )


def place():
    patch, req, owner = lax.axis_index("patch"), lax.axis_index("req"), lax.axis_index("owner")
    return patch, req, owner, patch // Z, patch % Z


def greet():
    patch, req, owner, y, z = place()
    sem = pltpu.get_barrier_semaphore()
    count = 0

    def signal(device):
        pl.semaphore_signal(sem, inc=1, device_id=device, device_id_type=MESH)

    for dz in range(1, Z):
        signal((y * Z + (z + dz) % Z, req, owner))
        count += 1
    for dy in range(1, Y):
        signal(((y + dy) % Y * Z + z, req, owner))
        count += 1
    for k in range(1, 2 * Y, 2):
        g = (y * 2 + owner + k) % (2 * Y)
        signal(((g // 2) * Z + z, req, g % 2))
        count += 1
    for step in (1, Y * Z - 1):
        for other in (owner, 1 - owner):
            signal(((patch + step) % (Y * Z), req, other))
            count += 1
    for k in range(1, 8):
        g = (req * 2 + owner + k) % 8
        signal((patch, g // 2, g % 2))
        count += 1
    return lambda: pl.semaphore_wait(sem, count)


def start_borders(src, top, bot, col, image, send, recv):
    patch, req, owner, y, z = place()
    rows = src.shape[1]
    last = Y * Z - 1
    edge = pl.multiple_of((1 - owner) * (src.shape[2] - EDGE), EDGE)
    cols = pl.ds(edge, EDGE)

    def copy(at, block, target, device):
        return remote(block, target, send.at[image, at], recv.at[image, at], device)

    down, up = patch < last, patch > 0
    copies = [
        (down, up, copy(0, src.at[image, rows - 1], top.at[image], (patch + 1, req, owner))),
        (up, down, copy(1, src.at[image, 0], bot.at[image], (patch - 1, req, owner))),
        (down, up, copy(2, src.at[image, rows - 1, cols], col.at[image, 0], (patch + 1, req, 1 - owner))),
        (up, down, copy(3, src.at[image, 0, cols], col.at[image, rows + 1], (patch - 1, req, 1 - owner))),
        (None, None, copy(4, src.at[image, :, cols], col.at[image, pl.ds(1, rows)], (patch, req, 1 - owner))),
    ]
    for sends, _, item in copies:
        if sends is None:
            item.start()
        else:
            pl.when(sends)(item.start)
    return copies


def clear_borders(top, bot, col):
    patch = lax.axis_index("patch")
    end = col.shape[1] - 1

    @pl.when(patch == 0)
    def _():
        top[...] = jnp.zeros_like(top)
        col[:, 0] = jnp.zeros_like(col[:, 0])

    @pl.when(patch == Y * Z - 1)
    def _():
        bot[...] = jnp.zeros_like(bot)
        col[:, end] = jnp.zeros_like(col[:, end])


def wait_borders(copies):
    for sends, receives, copy in copies:
        if sends is None:
            copy.wait()
        else:
            pl.when(sends)(copy.wait_send)
            pl.when(receives)(copy.wait_recv)


def local_stats(rows_of, rows):
    def add(f):
        def step(r, total):
            x = f(rows_of(r).astype(F32))
            return total + jnp.sum(x.reshape(x.shape[0] // 8, 8, x.shape[1]), axis=0)

        return step

    chans = rows_of(0).shape[1]
    count = rows * rows_of(0).shape[0]
    zero = jnp.zeros((8, chans), F32)
    total = lax.fori_loop(0, rows, add(lambda x: x), zero)
    mean = jnp.sum(total, axis=0, keepdims=True) * (1.0 / count)
    spread = lax.fori_loop(0, rows, add(lambda x: (x - mean) * (x - mean)), zero)
    return mean, jnp.sum(spread, axis=0, keepdims=True)


def start_exchange(slots, send, recv, peers):
    copies = [
        remote(slots.at[0], slots.at[k], send.at[k], recv.at[k], peer) for k, peer in enumerate(peers, 1)
    ]
    for copy in copies:
        copy.start()
    return copies


def combine(slots, count):
    values = slots[...]
    half = values.shape[1] // 2
    total = jnp.sum(values, axis=0)
    mean = total * (1.0 / values.shape[0])
    off = values - mean[None]
    between = jnp.sum(off * off, axis=0)
    return mean[0:half], total[half:] + count * between[0:half]


def first_peers():
    patch, req, owner, y, z = place()
    peers = []
    for k in range(1, 2 * Y):
        g = (y * 2 + owner + k) % (2 * Y)
        peers.append(((g // 2) * Z + z, req, g % 2))
    return peers


def second_peers():
    patch, req, owner, y, z = place()
    return [(y * Z + (z + k) % Z, req, owner) for k in range(1, Z)]


def group_matrix(chans):
    row = lax.broadcasted_iota(jnp.int32, (chans, chans), 0)
    column = lax.broadcasted_iota(jnp.int32, (chans, chans), 1)
    return jnp.where((row * 6554) >> 16 == (column * 6554) >> 16, 1.0, 0.0).astype(BF16)


def group_mean(values, groups):
    count = values.shape[0]
    values = jnp.concatenate([values] * (8 // count), axis=0)
    high = values.astype(BF16).astype(F32)
    rest = values - high
    middle = rest.astype(BF16).astype(F32)
    parts = jnp.concatenate([high, middle, rest - middle], axis=0).astype(BF16)
    total = jnp.dot(parts, groups, preferred_element_type=F32)
    return (total[0:count] + total[8 : 8 + count] + total[16 : 16 + count]) * (1.0 / GROUP)


def finish_norm(mean, spread, count, gain, shift, groups):
    center = group_mean(mean, groups)
    off = mean - center
    var = group_mean(spread * (1.0 / count) + off * off, groups)
    scale = gain / jnp.sqrt(var + 1e-05)
    return center, 0.5 * scale, 0.5 * shift


def lay_piece(reduce_row, expand_row, piece):
    down = reduce_row[0].astype(F32)
    up = expand_row[0].astype(F32)
    piece[...] = jnp.zeros_like(piece)
    for i in range(down.shape[1] // 128):
        piece[:, i, :] = down[:, i * 128 : i * 128 + 128]
    for i in range(up.shape[1] // 128):
        piece[:, UP_AT + i, :] = up[:, i * 128 : i * 128 + 128]
    return piece[...].astype(BF16)


def send_along_z(lora, send, recv):
    patch, req, owner, y, z = place()
    block = lora.at[owner, y, z]
    copies = [
        remote(block, block, send.at[k], recv.at[k], (y * Z + (z + k) % Z, req, owner)) for k in range(1, Z)
    ]
    for copy in copies:
        copy.start()
    return copies


def send_along_y(copies, lora, send, recv):
    patch, req, owner, y, z = place()
    for copy in copies:
        copy.wait()
    block = lora.at[owner, y]
    copies = [
        remote(block, block, send.at[Z + k], recv.at[Z + k], ((y + k) % Y * Z + z, req, owner)) for k in (1, Y - 1)
    ]
    for copy in copies:
        copy.start()
    return copies


def forward_along_y(copies, lora, send, recv):
    patch, req, owner, y, z = place()
    for copy in copies:
        copy.wait()
    half = Z // 2
    copies = []
    for at, k, step in ((0, 1, 0), (Z + 2, Y - 1, half)):
        block = lora.at[owner, (y + Y - k) % Y, pl.ds(step, half)]
        copies.append(remote(block, block, send.at[at], recv.at[at], ((y + k) % Y * Z + z, req, owner)))
        copies[-1].start()
    return copies


def lay_adapter(lora, image, base, tail, expand, flat, ups, wide_up):
    pieces = Y * Z
    depth = tail.shape[1] * 3 // pieces
    half = depth // 2

    def lay(p, carry):
        value = lora[image, p // Z, p % Z].astype(F32)
        down = value[0:half]
        flat[pl.ds(p * depth, half, 2)] = pltpu.roll(down, 64, 1)
        flat[pl.ds(p * depth + 1, half, 2)] = down
        ups[pl.ds(pl.multiple_of(p * 8, 8), 8)] = value[UP_AT : UP_AT + 8]
        return carry

    lax.fori_loop(0, pieces, lay, 0, unroll=8)
    lane = lax.broadcasted_iota(jnp.int32, base.shape[1:], 1)
    for d in range(3):
        down = flat[pl.ds(d * base.shape[1], base.shape[1])]
        tail[d] = jnp.where(lane >= 64, down, base[d].astype(F32)).astype(BF16)
    line = [ups[pl.ds(k, pieces, 8)] for k in range(5)]
    turned = [pltpu.roll(v, 64, 1) for v in line]
    low = lax.broadcasted_iota(jnp.int32, line[0].shape, 1) < 64
    even = line[0:3]
    odd = [jnp.where(low, turned[2], turned[3]), jnp.where(low, turned[3], turned[4]), turned[4]]
    for b in range(3):
        wide_up[pl.ds(0, 64)] = jnp.zeros((64, 128), F32)
        wide_up[pl.ds(64, pieces, 2)] = even[b]
        wide_up[pl.ds(65, pieces, 2)] = odd[b]
        expand[:, pl.ds(b * 128, 128)] = wide_up[...].astype(BF16)


def widen_image(source, top, bot, col, norm, image, wide, rem, inner):
    patch, req, owner, y, z = place()
    rows, columns = source.shape[1:3]
    last = Y * Z - 1
    index = lax.broadcasted_iota(jnp.int32, (columns, 1), 0)
    center = norm[pl.ds(image, 1)]
    scale = norm[pl.ds(2 + image, 1)]
    offset = norm[pl.ds(4, 1)]

    def activate(x):
        h = (x.astype(F32) - center) * scale + offset
        return h + h * jnp.tanh(h)

    def border(at):
        return activate(
            jnp.where(owner == 0, col[image, at, 0, :].astype(F32), col[image, at, EDGE - 1, :].astype(F32))
        )

    def lay(r, act, edge):
        left = jnp.where(index == 0, jnp.where(owner == 1, edge, 0.0), pltpu.roll(act, 1, 0))
        right = jnp.where(
            index == columns - 1, jnp.where(owner == 0, edge, 0.0), pltpu.roll(act, columns - 1, 0)
        )
        wide[image, r] = jnp.concatenate([left, act, right], axis=1).astype(BF16)

    if inner:
        rem[pl.ds(0, rows)] = border(slice(1, rows + 1))

        def row(r, carry):
            lay(r + 1, activate(source[image, r]), rem[pl.ds(r, 1)])
            return carry

        lax.fori_loop(0, rows, row, 0, unroll=2)
    else:
        for r, block, inside in ((0, top, patch > 0), (rows + 1, bot, patch < last)):
            edge = jnp.where(inside, border(slice(r, r + 1)), 0.0)
            lay(r, jnp.where(inside, activate(block[image]), 0.0), edge)


def windows(wide, image, at, part):
    columns, depth = wide.shape[2:]
    return [wide[image, pl.ds(at + d, part)].reshape(part * columns, depth) for d in range(3)]


def edge_windows(wide, image):
    last = wide.shape[1] - 3
    return [jnp.concatenate([wide[image, d], wide[image, last + d]], axis=0) for d in range(3)]


def dots(window, matrix, lanes):
    return sum(jnp.dot(window[d], matrix[d, :, lanes], preferred_element_type=F32) for d in range(3))


MAIN, REST = pl.ds(0, 256), pl.ds(256, 128)
UP_AT = 48


def block_kernel(
    raw, reduce_row, expand_row, image_adapter, bank_row, embedding, weight_hbm, gain, shift, kernels_hbm,
    out,
    raw_own, result, weight, groups, own, hidden, kernels, wide, total, base, tail, expand, flat, ups, wide_up, rem,
    piece, held, lora, top, bot, col, top2, bot2, col2, norm, one, two, one2, two2,
    local_sem, out_sem, bank_send, bank_recv, lora_send, lora_recv, relay_send, relay_recv,
    edge_send, edge_recv, edge2_send, edge2_recv, x_send, x_recv,
):
    patch, req, owner, y, z = place()
    images, rows, columns, chans = own.shape
    count = rows * columns
    fetch = pltpu.make_async_copy(raw, raw_own, local_sem.at[0])
    fetch.start()
    fetch_kernels = pltpu.make_async_copy(kernels_hbm, kernels, local_sem.at[1])
    fetch_kernels.start()
    fetch_weight = pltpu.make_async_copy(weight_hbm, weight, local_sem.at[2])
    fetch_weight.start()
    arrived = greet()
    me = req * 2 + owner
    held[me] = lay_piece(reduce_row, expand_row, piece)
    clear_borders(top, bot, col)
    clear_borders(top2, bot2, col2)
    groups[...] = group_matrix(chans)
    fetch.wait()

    def turn(t, carry):
        image, r = t // rows, t % rows
        own[image, r] = jnp.transpose(raw_own[image, r].astype(F32)).astype(BF16)
        return carry

    lax.fori_loop(0, images * rows, turn, 0, unroll=4)

    for image in range(images):
        mean, spread = local_stats(lambda r, image=image: own[image, r], rows)
        one[0, pl.ds(image, 1)] = mean
        one[0, pl.ds(2 + image, 1)] = spread
    arrived()

    first = start_exchange(one, x_send.at[0], x_recv.at[0], first_peers())
    bank = []
    for k in range(1, 8):
        g = (me + k) % 8
        copy = remote(held.at[me], held.at[me], bank_send.at[k], bank_recv.at[k], (patch, g // 2, g % 2))
        copy.start()
        bank.append(copy)

    fetch_weight.wait()
    u = embedding[...].astype(F32)
    temb = (u / (1.0 + jnp.exp(-u))).astype(BF16)
    proj = lax.dot_general(temb, weight[...], (((1,), (1,)), ((), ())), preferred_element_type=F32)
    norm[0, pl.ds(5, 2)] = proj
    fetch_kernels.wait()

    def middle(first, one, two, at):
        for copy in first:
            copy.wait()
        mean, spread = combine(one, float(count))
        half = mean.shape[0]
        two[0, pl.ds(0, half)] = mean
        two[0, pl.ds(half, half)] = spread
        return start_exchange(two, x_send.at[at], x_recv.at[at], second_peers())

    def finish(second, two, which, image):
        for copy in second:
            copy.wait()
        mean, spread = combine(two, float(count * 2 * Y))
        half = mean.shape[0]
        center, scale, offset = finish_norm(
            mean, spread, float(count * 2 * Y * Z), gain[pl.ds(which, 1)], shift[pl.ds(which, 1)], groups[...]
        )
        norm[which, pl.ds(image, half)] = center
        norm[which, pl.ds(2 + image, half)] = scale
        norm[which, pl.ds(4, 1)] = offset

    second = middle(first, one, two, 1)
    for copy in bank:
        copy.wait()
    chosen = held[bank_row[image_adapter[0, owner]]]
    lora[0, owner, y, z] = chosen[0]
    lora[1, owner, y, z] = chosen[1]
    pieces = [send_along_z(lora.at[0], lora_send.at[0], lora_recv.at[0])]
    borders = [start_borders(own, top, bot, col, i, edge_send, edge_recv) for i in range(images)]
    for which in range(2):
        for d in range(3):
            last = kernels[which, d, :, pl.ds(256, chans - 256)].astype(F32)
            base[which, d] = jnp.concatenate([last, jnp.zeros_like(last)], axis=1).astype(BF16)
    finish(second, two, 0, 0)
    pieces[0] = send_along_y(pieces[0], lora.at[0], lora_send.at[0], lora_recv.at[0])

    order = (owner, 1 - owner)
    inner = (rows - 2) // 2
    ends = (0, rows - 1)

    def pixels(r, count=1):
        return pl.ds(pl.multiple_of(r * columns, columns), count * columns)

    def main_inner(image):
        def chunk(c, carry):
            at = 1 + c * inner
            total[image, pixels(at, inner), MAIN] = dots(windows(wide, image, at, inner), kernels.at[0], MAIN)
            return carry

        lax.fori_loop(0, 2, chunk, 0)

    def main_edges(image):
        value = dots(edge_windows(wide, image), kernels.at[0], MAIN)
        for i, r in enumerate(ends):
            total[image, pixels(r), MAIN] = value[i * columns : (i + 1) * columns]

    def relay(which):
        for copy in pieces[which]:
            copy.wait()
        block = lora.at[which, owner]
        copy = remote(block, block, relay_send.at[which], relay_recv.at[which], (patch, req, 1 - owner))
        copy.start()
        return copy

    def adapter(which, image):
        lay_adapter(
            lora.at[which], image, base.at[which], tail.at[image], expand.at[image], flat, ups, wide_up
        )

    def tail_dots(image):
        part = rows // 2

        def chunk(c, carry):
            at = c * part
            last = dots(windows(wide, image, at, part), tail.at[image], pl.ds(0, 128))
            small = last.astype(BF16)
            span = pixels(at, part)
            total[image, span, REST] = last + jnp.dot(small, expand[image, :, REST], preferred_element_type=F32)
            total[image, span, MAIN] += jnp.dot(small, expand[image, :, MAIN], preferred_element_type=F32)
            bias = norm[0, pl.ds(5 + image, 1)]
            for r in range(part):
                hidden[image, at + r] = (total[image, pixels(at + r), pl.ds(0, chans)] + bias).astype(BF16)
            return carry

        lax.fori_loop(0, 2, chunk, 0)

    for copies in borders:
        wait_borders(copies[4:])
    for step, image in enumerate(order):
        widen_image(own, top, bot, col, norm.at[0], image, wide, rem, True)
        main_inner(image)
        if step == 0:
            pieces[0] = forward_along_y(pieces[0], lora.at[0], lora_send.at[0], lora_recv.at[0])
            pieces.append(send_along_z(lora.at[1], lora_send.at[1], lora_recv.at[1]))
    for copies in borders:
        wait_borders(copies[:4])
    for image in order:
        widen_image(own, top, bot, col, norm.at[0], image, wide, rem, False)
        main_edges(image)

    copy = relay(0)
    borders = []
    for step, image in enumerate(order):
        if step == 1:
            copy.wait()
        adapter(0, image)
        tail_dots(image)
        if step == 0:
            pieces[1] = send_along_y(pieces[1], lora.at[1], lora_send.at[1], lora_recv.at[1])
        if step == 0:
            borders.append(start_borders(hidden, top2, bot2, col2, image, edge2_send, edge2_recv))
        mean, spread = local_stats(lambda r, image=image: hidden[image, r], rows)
        one2[0, pl.ds(image, 1)] = mean
        one2[0, pl.ds(2 + image, 1)] = spread

    first = start_exchange(one2, x_send.at[2], x_recv.at[2], first_peers())
    second = middle(first, one2, two2, 3)
    pieces[1] = forward_along_y(pieces[1], lora.at[1], lora_send.at[1], lora_recv.at[1])
    borders.append(start_borders(hidden, top2, bot2, col2, order[1], edge2_send, edge2_recv))
    copy = relay(1)
    adapter(1, order[0])
    finish(second, two2, 1, 0)

    def final(image, window, at, rows_of):
        last = dots(window, tail.at[image], pl.ds(0, 128))
        small = last.astype(BF16)
        body = dots(window, kernels.at[1], MAIN)
        span = pixels(at, len(rows_of))
        total[image, span, MAIN] = body + jnp.dot(small, expand[image, :, MAIN], preferred_element_type=F32)
        total[image, span, REST] = last + jnp.dot(small, expand[image, :, REST], preferred_element_type=F32)
        for i, r in enumerate(rows_of):
            value = total[image, pixels(at + i), pl.ds(0, chans)]
            result[image, r] = (jnp.transpose(value) + raw_own[image, r].astype(F32)).astype(BF16)

    for copies in borders:
        wait_borders(copies[4:])
    leaving = []

    def leave(image, at, count, sem):
        part = (image, pl.ds(at, count))
        copy = pltpu.make_async_copy(result.at[part], out.at[part], out_sem.at[sem])
        copy.start()
        leaving.append(copy)

    for step, image in enumerate(order):
        if step == 1:
            copy.wait()
            adapter(1, image)
        widen_image(hidden, top2, bot2, col2, norm.at[1], image, wide, rem, True)

        def chunk(c, carry, image=image):
            at = 1 + c * inner
            final(image, windows(wide, image, at, inner), at, [at + i for i in range(inner)])
            return carry

        lax.fori_loop(0, 2, chunk, 0)
        leave(image, 1, rows - 2, step)
    for copies in borders:
        wait_borders(copies[:4])
    for image in order:
        widen_image(hidden, top2, bot2, col2, norm.at[1], image, wide, rem, False)
        final(image, edge_windows(wide, image), 0, ends)
        for r in ends:
            leave(image, r, 1, len(leaving))
    for copy in leaving:
        copy.wait()


VM = pl.BlockSpec(memory_space=pltpu.VMEM)
HB = pl.BlockSpec(memory_space=pl.ANY)
SM = pl.BlockSpec(memory_space=pltpu.SMEM)
DMA = pltpu.SemaphoreType.DMA


def local(
    latents, timestep_embedding, embedding_weight, gain, shift, kernel_weight, reduce_library, expand_library,
    image_adapter, adapter_bank_row,
):
    images, rows, columns, chans = latents.shape
    pieces = Y * Z
    deep = UP_AT + 8
    map_of = (images, rows, columns, chans)
    line = pltpu.VMEM((images, columns, chans), BF16)
    edge = pltpu.VMEM((images, rows + 2, EDGE, chans), BF16)
    result = pl.pallas_call(
        block_kernel,
        out_shape=jax.ShapeDtypeStruct((images, rows, chans, columns), BF16),
        in_specs=[HB, VM, VM, SM, SM, VM, HB, VM, VM, HB],
        out_specs=HB,
        scratch_shapes=[
            pltpu.VMEM((images, rows, chans, columns), BF16),
            pltpu.VMEM((images, rows, chans, columns), BF16),
            pltpu.VMEM((chans, embedding_weight.shape[0]), BF16),
            pltpu.VMEM((chans, chans), BF16),
            pltpu.VMEM(map_of, BF16),
            pltpu.VMEM(map_of, BF16),
            pltpu.VMEM((2, 3, 3 * chans, chans), BF16),
            pltpu.VMEM((images, rows + 2, columns, 3 * chans), BF16),
            pltpu.VMEM((images, rows * columns, 384), F32),
            pltpu.VMEM((2, 3, 3 * chans, 128), BF16),
            pltpu.VMEM((images, 3, 3 * chans, 128), BF16),
            pltpu.VMEM((images, 128, 384), BF16),
            pltpu.VMEM((9 * chans, 128), F32),
            pltpu.VMEM((pieces * 8, 128), F32),
            pltpu.VMEM((128, 128), F32),
            pltpu.VMEM((16, chans), F32),
            pltpu.VMEM((2, deep, 128), F32),
            pltpu.VMEM((8, 2, deep, 128), BF16),
            pltpu.VMEM((2, images, Y, Z, deep, 128), BF16),
            *([line, line, edge] * 2),
            pltpu.VMEM((2, 8, chans), F32),
            pltpu.VMEM((2 * Y, 4, chans), F32),
            pltpu.VMEM((Z, 4, chans), F32),
            pltpu.VMEM((2 * Y, 4, chans), F32),
            pltpu.VMEM((Z, 4, chans), F32),
            DMA((3,)),
            DMA((6,)),
            DMA((8,)),
            DMA((8,)),
            DMA((2, Z + Y)),
            DMA((2, Z + Y)),
            DMA((2,)),
            DMA((2,)),
            *([DMA((images, 5))] * 4),
            DMA((4, 8)),
            DMA((4, 8)),
        ],
        compiler_params=pltpu.CompilerParams(
            collective_id=0, has_side_effects=True, vmem_limit_bytes=56 * 2**20
        ),
        name="resnet_block",
    )(
        jnp.swapaxes(latents, 2, 3),
        reduce_library,
        expand_library,
        image_adapter.T,
        adapter_bank_row,
        timestep_embedding,
        embedding_weight.T,
        gain,
        shift,
        kernel_weight.reshape(2, 3, 3 * chans, chans),
    )
    return jnp.swapaxes(result, 2, 3)


def solution(mesh):
    in_specs = (
        P("req", "patch", "owner", None),
        P("req", None),
        P(),
        P(),
        P(),
        P(),
        P(("req", "owner"), None, "patch"),
        P(("req", "owner"), None, "patch"),
        P("req", None),
        P(),
    )
    return jax.shard_map(
        local, mesh=mesh, in_specs=in_specs, out_specs=P("req", "patch", "owner", None), check_vma=False
    )
```
